32 devices in a mesh: dp: 8 (over z, x), mp: 4 (over y, core).
Axes of the slice: x: 2, y: 2, z: 4, core: 2. Of those that a mesh axis runs over, the one named last changes fastest.
Arguments:
- tokens: bfloat16 [18432, 1024], P('dp'), may hold values from -6 to 6
- cotangent: bfloat16 [18432, 1024], P('dp'), may hold values from -6 to 6
- seq_lengths: int32 [16, 4], P('dp'), may hold values from 1 to 1024, 1152 in all within a row
- deal: int32 [64], replicated, may hold values from 0 to 63, as said below
- w_query: bfloat16 [1024, 1024], P(None, 'mp'), may hold values from -0.1875 to 0.1875
- w_keyval: bfloat16 [1024, 2, 512], P(None, None, 'mp'), may hold values from -0.1875 to 0.1875
- w_output: bfloat16 [1024, 1024], P('mp'), may hold values from -3 to 3
- w_gateup: bfloat16 [1024, 2, 4608], P(None, None, 'mp'), may hold values from -0.1875 to 0.1875
- w_down: bfloat16 [4608, 1024], P('mp'), may hold values from -0.09375 to 0.09375
- norm_gains: float32 [2, 1024], replicated, may hold values from 0.5 to 1.5
- head_gains: float32 [2, 64], replicated, may hold values from 0.5 to 1.5
- master_query: float32 [1024, 1024], P('dp', 'mp'), may hold values from -0.1875 to 0.1875
- master_keyval: float32 [1024, 2, 512], P('dp', None, 'mp'), may hold values from -0.1875 to 0.1875
- master_output: float32 [1024, 1024], P('mp', 'dp'), may hold values from -0.1875 to 0.1875
- master_gateup: float32 [1024, 2, 4608], P('dp', None, 'mp'), may hold values from -0.1875 to 0.1875
- master_down: float32 [4608, 1024], P('mp', 'dp'), may hold values from -0.09375 to 0.09375
- start_query: float32 [1024, 1024], P('dp', 'mp'), may hold values from -6 to 6
- start_keyval: float32 [1024, 2, 512], P('dp', None, 'mp'), may hold values from -6 to 6
- start_output: float32 [1024, 1024], P('mp', 'dp'), may hold values from -6 to 6
- start_gateup: float32 [1024, 2, 4608], P('dp', None, 'mp'), may hold values from -6 to 6
- start_down: float32 [4608, 1024], P('mp', 'dp'), may hold values from -6 to 6
- start_norms: float32 [2, 1024], replicated, may hold values from -6 to 6
- start_heads: float32 [2, 64], replicated, may hold values from -6 to 6
- step_size: float32 [1], replicated, may hold values from 0.03 to 0.2
Outputs:
- output: bfloat16 [18432, 1024], P('dp')
- input_grad: bfloat16 [18432, 1024], P('dp')
- clip_norm: float32 [1], replicated
- moment_query: float32 [1024, 1024], P('dp', 'mp')
- moment_keyval: float32 [1024, 2, 512], P('dp', None, 'mp')
- moment_output: float32 [1024, 1024], P('mp', 'dp')
- moment_gateup: float32 [1024, 2, 4608], P('dp', None, 'mp')
- moment_down: float32 [4608, 1024], P('mp', 'dp')
- moment_norms: float32 [2, 1024], replicated
- moment_heads: float32 [2, 64], replicated
- next_query: float32 [1024, 1024], P('dp', 'mp')
- next_keyval: float32 [1024, 2, 512], P('dp', None, 'mp')
- next_output: float32 [1024, 1024], P('mp', 'dp')
- next_gateup: float32 [1024, 2, 4608], P('dp', None, 'mp')
- next_down: float32 [4608, 1024], P('mp', 'dp')
- next_norms: float32 [2, 1024], replicated
- next_heads: float32 [2, 64], replicated
- weight_query: bfloat16 [1024, 1024], P(None, 'mp')
- weight_keyval: bfloat16 [1024, 2, 512], P(None, None, 'mp')
- weight_output: bfloat16 [1024, 1024], P('mp')
- weight_gateup: bfloat16 [1024, 2, 4608], P(None, None, 'mp')
- weight_down: bfloat16 [4608, 1024], P('mp')
The draws below stay inside these ranges and needn't reach their ends.
Inputs may be any that keep to these rules, and one draw needn't show every extreme that they name: A permutation: given piece g (piece g % 8 of device g // 8) goes to dealt place deal[g], held by device deal[g] // 8; every device sends exactly 1 pieces to every device. `seq_lengths`: row s lists the sequence lengths of slot s in order; each row sums to 1152 and its largest is 1024.
All inputs are finite; a program needn't handle non-finite values.
Results may differ from the reference program's by a relative error of at most 0.02.
Values may be sent and summed in bfloat16 or wider, within the bound.
No kernel may reach another device: no remote copies, remote signals or barrier semaphores. Data moves between devices by JAX's collectives and lax.ppermute only.
A program may use at most 256 MiB of HBM per device.

```python
import math
import jax
import jax.numpy as jnp
import numpy as np
from jax import lax

D = 1024
H = 16
KV = 8
HD = 64
FF = 4608
SLOT = 1152
NSEQ = 4
PER_PEER = 1
SEQ_MAX = 1024
SLOTS = 16
TOKENS = 18432
PIECES_DEV = 8
PIECE = 288
PIECES = 64
N_MP = 4


def draw_deal(key, part):
    devices = PIECES // PIECES_DEV
    key_dest = jax.random.fold_in(key, 11)
    key_source = jax.random.fold_in(key, 23)
    base_row = jnp.arange(PIECES_DEV, dtype=jnp.int32) // PER_PEER

    def dest_row(index_dev):
        return jax.random.permutation(jax.random.fold_in(key_dest, index_dev), base_row)
    source_of = jax.vmap(dest_row)(jnp.arange(devices, dtype=jnp.int32)).reshape(-1)
    places = jnp.arange(PIECES, dtype=jnp.int32)
    grouped = jnp.argsort(source_of * PIECES + places).astype(jnp.int32)

    def local_row(index_dev):
        return jax.random.permutation(jax.random.fold_in(key_source, index_dev), PIECES_DEV).astype(jnp.int32)
    local_order = jax.vmap(local_row)(jnp.arange(devices, dtype=jnp.int32))
    given_index = (jnp.arange(devices, dtype=jnp.int32)[:, None] * PIECES_DEV + local_order).reshape(-1)
    return jnp.zeros((PIECES,), jnp.int32).at[given_index].set(grouped)


def block_scale(key, shape, cuts, smallest, top_value):
    gain, own = 1.0, jax.random.fold_in(key, 6)
    for dim, parts in cuts:
        heights = jnp.exp(jax.random.uniform(jax.random.fold_in(own, dim), (parts,), jnp.float32, smallest / len(cuts), top_value / len(cuts)))
        gain = gain * jnp.repeat(heights, shape[dim] // parts).reshape([-1 if axis == dim else 1 for axis in range(len(shape))])
    return gain


def split_up(number_of, total, most, skew):
    portions = [(1 << 20) // math.isqrt(standing ** skew) + 1 for standing in range(2, number_of + 1)]
    spare, counts = total - most - (number_of - 1), [1] * (number_of - 1)
    while spare > 0:
        movable = [i for i in range(number_of - 1) if counts[i] < most]
        mass, remaining = sum([portions[i] for i in movable]), spare
        for i in movable:
            more = min(most - counts[i], max(1, remaining * portions[i] // mass), spare)
            counts[i] = counts[i] + more
            spare = spare - more
    return np.array([most] + counts)


def uneven(rng, count, total, most, slope):
    if count == 2:
        one = jax.random.randint(rng, (), max(1, total - most), min(most, total - 1) + 1)
        return jnp.stack([one, total - one])
    sizes = jnp.asarray(split_up(count, total, most, slope), jnp.int32)
    couples = (count - 1) // 2
    donor, receiver = sizes[1:1 + 2 * couples:2], sizes[2:2 + 2 * couples:2]
    margin = jnp.minimum(donor - 1, most - receiver)
    moved = jax.random.randint(jax.random.fold_in(rng, 1), (couples,), 0, 1 << 20) % (margin + 1)
    sizes = sizes.at[1:1 + 2 * couples:2].set(donor - moved).at[2:2 + 2 * couples:2].set(receiver + moved)
    return sizes[jax.random.permutation(jax.random.fold_in(rng, 2), count)]


def noise(stream_key, shape, width, most, cuts=(), kind=jnp.bfloat16):
    loudness = block_scale(stream_key, shape, cuts, -0.22, 0.18) if cuts else 1.0
    array = jax.random.normal(stream_key, shape, jnp.float32) * width * loudness
    return jnp.minimum(jnp.maximum(array, -most), most).astype(kind)


def setup_inputs(seed: int = 0) -> dict:
    seeds = jax.random.split(jax.random.key(seed), 25)
    tokens = noise(seeds[0], (TOKENS, D), 1.0, 6.0, ((0, 8),))
    cotangent = noise(seeds[1], (TOKENS, D), 1.0, 6.0, ((0, 8),))
    seq_lengths = jax.vmap(lambda own: uneven(own, NSEQ, SLOT, SEQ_MAX, 2))(jax.random.split(seeds[2], SLOTS)).reshape((SLOTS, NSEQ)).astype(jnp.int32)
    deal = draw_deal(jax.random.fold_in(seeds[24], 71), 0)
    w_query = noise(seeds[4], (D, H * HD), D ** -0.5, 0.1875, ((1, 4),))
    w_keyval = noise(seeds[5], (D, 2, KV * HD), D ** -0.5, 0.1875, ((2, 4),))
    w_output = noise(seeds[6], (H * HD, D), (max(4, H * HD // 256)) ** -0.5, 3.0, ((0, 4),))
    w_gateup = noise(seeds[7], (D, 2, FF), D ** -0.5, 0.1875, ((2, 4),))
    w_down = noise(seeds[8], (FF, D), FF ** -0.5, 0.09375, ((0, 4),))
    norm_gains = jnp.clip(1.0 + 0.1 * jax.random.normal(seeds[9], (2, D), jnp.float32), 0.5, 1.5)
    head_gains = jnp.clip(1.0 + 0.1 * jax.random.normal(seeds[10], (2, HD), jnp.float32), 0.5, 1.5)
    master_query = noise(seeds[11], (D, H * HD), D ** -0.5, 0.1875, ((0, 8), (1, 4)), jnp.float32)
    master_keyval = noise(seeds[12], (D, 2, KV * HD), D ** -0.5, 0.1875, ((0, 8), (2, 4)), jnp.float32)
    master_output = noise(seeds[13], (H * HD, D), (H * HD) ** -0.5, 0.1875, ((0, 4), (1, 8)), jnp.float32)
    master_gateup = noise(seeds[14], (D, 2, FF), D ** -0.5, 0.1875, ((0, 8), (2, 4)), jnp.float32)
    master_down = noise(seeds[15], (FF, D), FF ** -0.5, 0.09375, ((0, 4), (1, 8)), jnp.float32)
    start_query = noise(seeds[16], (D, H * HD), 1.0, 6.0, ((0, 8), (1, 4)), jnp.float32)
    start_keyval = noise(seeds[17], (D, 2, KV * HD), 1.0, 6.0, ((0, 8), (2, 4)), jnp.float32)
    start_output = noise(seeds[18], (H * HD, D), 1.0, 6.0, ((0, 4), (1, 8)), jnp.float32)
    start_gateup = noise(seeds[19], (D, 2, FF), 1.0, 6.0, ((0, 8), (2, 4)), jnp.float32)
    start_down = noise(seeds[20], (FF, D), 1.0, 6.0, ((0, 4), (1, 8)), jnp.float32)
    start_norms = noise(seeds[21], (2, D), 1.0, 6.0, (), jnp.float32)
    start_heads = noise(seeds[22], (2, HD), 1.0, 6.0, (), jnp.float32)
    step_size = jnp.clip(jnp.exp(jax.random.uniform(seeds[23], (1,), jnp.float32, math.log(0.03), math.log(0.2))), 0.03, 0.2)
    return {"tokens": tokens, "cotangent": cotangent, "seq_lengths": seq_lengths, "deal": deal, "w_query": w_query, "w_keyval": w_keyval, "w_output": w_output, "w_gateup": w_gateup, "w_down": w_down, "norm_gains": norm_gains, "head_gains": head_gains, "master_query": master_query, "master_keyval": master_keyval, "master_output": master_output, "master_gateup": master_gateup, "master_down": master_down, "start_query": start_query, "start_keyval": start_keyval, "start_output": start_output, "start_gateup": start_gateup, "start_down": start_down, "start_norms": start_norms, "start_heads": start_heads, "step_size": step_size}


@jax.custom_vjp
def low(v):
    return lax.optimization_barrier(v.astype(jnp.bfloat16)).astype(jnp.float32)

@jax.custom_vjp
def low_back(v):
    return v

def low_keep(v):
    return (low(v), None)

def low_pass(kept, grad):
    return (grad,)

def back_keep(v):
    return (v, None)

def back_low(kept, grad):
    return (low(grad),)
low.defvjp(low_keep, low_pass)
low_back.defvjp(back_keep, back_low)
EPSILON = 1e-05
ROPE_BASE = 1000000.0
HIGHEST = lax.Precision.HIGHEST

def layout(lengths_row, count):
    ends = jnp.cumsum(lengths_row)
    index_row = jnp.arange(count, dtype=jnp.int32)
    passed = (index_row[:, None] >= ends[None, :]).astype(jnp.int32)
    segment = lax.optimization_barrier(jnp.sum(passed, axis=1))
    position = index_row - lax.optimization_barrier(jnp.sum(passed * lengths_row[None, :], axis=1))
    return (segment, position)

def rotation(position, head_dim):
    half = head_dim // 2
    freqs = ROPE_BASE ** (-jnp.arange(half, dtype=jnp.float32) * (2.0 / head_dim))
    angles = position.astype(jnp.float32)[:, None] * freqs[None, :]
    return (jnp.cos(angles)[:, None, :], jnp.sin(angles)[:, None, :])

def rotate(values, cosine, sine):
    half = values.shape[-1] // 2
    first = values[..., :half]
    second = values[..., half:]
    return jnp.concatenate([first * cosine - second * sine, second * cosine + first * sine], axis=-1)

def head_norm(values, gain_row):
    return values * lax.rsqrt(lax.optimization_barrier(jnp.mean(values * values, axis=-1, keepdims=True)) + EPSILON) * gain_row

def attention(query_heads, key_heads, value_heads, segment):
    row_count = query_heads.shape[0]
    scores = jnp.einsum('qkrd,skd->krqs', query_heads, key_heads, precision=HIGHEST) * HD ** (-0.5)
    scores = low_back(scores)
    index_row = jnp.arange(row_count, dtype=jnp.int32)
    allowed = (index_row[None, :] <= index_row[:, None]) & (segment[None, :] == segment[:, None])
    scores = jnp.where(allowed, scores, -1e+30)
    row_max = lax.optimization_barrier(jnp.max(scores, axis=-1, keepdims=True))
    exponent = jnp.exp(scores - row_max)
    attn_probs = low(exponent / lax.optimization_barrier(jnp.sum(exponent, axis=-1, keepdims=True)))
    return jnp.einsum('krqs,skd->qkrd', attn_probs, value_heads, precision=HIGHEST)

def forward(x_value, param_tuple, segment, position):
    w_query, w_keyval, w_output, w_gateup, w_down, norm_gains, head_gains = param_tuple
    row_count = x_value.shape[0]
    groups = N_MP
    query_cols = H * HD // groups
    key_cols = KV * HD // groups
    unit_cols = FF // groups
    inv_one = lax.rsqrt(lax.optimization_barrier(jnp.mean(x_value * x_value, axis=1, keepdims=True)) + EPSILON)
    norm_one = low(x_value * inv_one * norm_gains[0])
    split_one = low_back(jnp.broadcast_to(norm_one, (groups, row_count, D)))
    query_raw = low_back(jnp.einsum('gtd,gdc->gtc', split_one, w_query.reshape(D, groups, query_cols).transpose(1, 0, 2), precision=HIGHEST))
    keyval_raw = jnp.einsum('gtd,gdsc->gtsc', split_one, w_keyval.reshape(D, 2, groups, key_cols).transpose(2, 0, 1, 3), precision=HIGHEST)
    key_raw = low_back(keyval_raw[:, :, 0])
    value_raw = low(low_back(keyval_raw[:, :, 1]))
    query_raw = query_raw.reshape(groups, row_count, H // groups, HD).transpose(1, 0, 2, 3).reshape(row_count, H, HD)
    key_raw = key_raw.reshape(groups, row_count, KV // groups, HD).transpose(1, 0, 2, 3).reshape(row_count, KV, HD)
    value_heads = value_raw.reshape(groups, row_count, KV // groups, HD).transpose(1, 0, 2, 3).reshape(row_count, KV, HD)
    cosine, sine = rotation(position, HD)
    query_heads = low(rotate(head_norm(query_raw, head_gains[0]), cosine, sine))
    key_heads = low(rotate(head_norm(key_raw, head_gains[1]), cosine, sine))
    mixed = jax.checkpoint(attention)(query_heads.reshape(row_count, KV, H // KV, HD), key_heads, value_heads, segment)
    mixed = low(low_back(mixed.reshape(row_count, H * HD)))
    attn_parts = low(low_back(jnp.einsum('gtc,gcd->gtd', mixed.reshape(row_count, groups, query_cols).transpose(1, 0, 2), w_output.reshape(groups, query_cols, D), precision=HIGHEST)))
    hidden_one = x_value + lax.optimization_barrier(jnp.sum(attn_parts, axis=0))
    inv_two = lax.rsqrt(lax.optimization_barrier(jnp.mean(hidden_one * hidden_one, axis=1, keepdims=True)) + EPSILON)
    norm_two = low(hidden_one * inv_two * norm_gains[1])
    split_two = low_back(jnp.broadcast_to(norm_two, (groups, row_count, D)))
    gateup = jnp.einsum('gtd,gdsf->gtsf', split_two, w_gateup.reshape(D, 2, groups, unit_cols).transpose(2, 0, 1, 3), precision=HIGHEST)
    gate = low_back(gateup[:, :, 0])
    up_part = low_back(gateup[:, :, 1])
    inner = low(gate * jax.nn.sigmoid(gate) * up_part)
    ffn_parts = low(low_back(jnp.einsum('gtf,gfd->gtd', inner, w_down.reshape(groups, unit_cols, D), precision=HIGHEST)))
    return hidden_one + lax.optimization_barrier(jnp.sum(ffn_parts, axis=0))

def reference(tokens, cotangent, seq_lengths, deal, w_query, w_keyval, w_output, w_gateup, w_down, norm_gains, head_gains, master_query, master_keyval, master_output, master_gateup, master_down, start_query, start_keyval, start_output, start_gateup, start_down, start_norms, start_heads, step_size):
    piece_count = deal.shape[0]
    inverse = jnp.zeros((piece_count,), jnp.int32).at[deal].set(jnp.arange(piece_count, dtype=jnp.int32))

    def to_slots(given):
        pieces = given.astype(jnp.float32).reshape(piece_count, PIECE, D)
        return pieces[inverse].reshape(SLOTS, SLOT, D)

    def to_given(dealt):
        return dealt.reshape(piece_count, PIECE, D)[deal].reshape(TOKENS, D)
    param_tuple = (w_query.astype(jnp.float32), w_keyval.astype(jnp.float32), w_output.astype(jnp.float32), w_gateup.astype(jnp.float32), w_down.astype(jnp.float32), norm_gains.astype(jnp.float32), head_gains.astype(jnp.float32))
    zero_grads = jax.tree.map(jnp.zeros_like, param_tuple)

    def one_slot(running, item):
        x_slot, back_slot, lengths_row = item
        segment, position = layout(lengths_row, SLOT)

        def slot_forward(x_value, params_now):
            return forward(x_value, params_now, segment, position)
        result, pullback = jax.vjp(slot_forward, x_slot, param_tuple)
        d_input, d_params = pullback(back_slot)
        return (jax.tree.map(jnp.add, running, d_params), (result, d_input))
    grads, (results, d_inputs) = lax.scan(one_slot, zero_grads, (to_slots(tokens), to_slots(cotangent), seq_lengths))
    clip_value = jnp.sqrt(sum([jnp.sum(gradient * gradient) for gradient in grads]))
    limit = math.sqrt(2 * D * H * HD + 2 * D * KV * HD + 3 * D * FF + 2 * D + 2 * HD)
    factor = jnp.minimum(1.0, limit / clip_value)
    starts = (start_query, start_keyval, start_output, start_gateup, start_down, start_norms, start_heads)
    masters = (master_query, master_keyval, master_output, master_gateup, master_down, norm_gains, head_gains)
    moments = [0.5 * begin + factor * gradient for begin, gradient in zip(starts, grads)]
    nexts = [held - step_size[0] * moved for held, moved in zip(masters, moments)]
    return (to_given(results).astype(jnp.bfloat16), to_given(d_inputs).astype(jnp.bfloat16), clip_value.reshape(1), moments[0], moments[1], moments[2], moments[3], moments[4], moments[5], moments[6], nexts[0], nexts[1], nexts[2], nexts[3], nexts[4], nexts[5], nexts[6], nexts[0].astype(jnp.bfloat16), nexts[1].astype(jnp.bfloat16), nexts[2].astype(jnp.bfloat16), nexts[3].astype(jnp.bfloat16), nexts[4].astype(jnp.bfloat16))
```

```python
import functools
import math

import jax
import jax.numpy as jnp
from jax import lax
from jax.experimental import pallas as pl
from jax.experimental.pallas import tpu as pltpu
from jax.sharding import PartitionSpec as P

D = 1024
H = 16
KV = 8
HD = 64
FF = 4608


EPSILON = 1e-05
ROPE_BASE = 1000000.0
LOW = jnp.bfloat16
FULL = jnp.float32
LANES = 128


def dot(left, right, left_dim=1, right_dim=0):
    return lax.dot_general(
        left, right, (((left_dim,), (right_dim,)), ((), ())), preferred_element_type=FULL
    )


def swap(values, axis, bit):
    size = lax.axis_size(axis)
    return lax.ppermute(values, axis, [(place, place ^ bit) for place in range(size)])


def far(values):
    return swap(values, "mp", 2)


def near(values):
    return swap(values, "mp", 1)


def bits_of(count):
    return [1 << place for place in range(count.bit_length() - 1)]


RELATIVE = (0, 2, 1, 3)
VMEM = pl.BlockSpec(memory_space=pltpu.VMEM)
SMEM = pl.BlockSpec(memory_space=pltpu.SMEM)
VMEM_BYTES = 60 * 1024 * 1024


def group_sums(values, ones):
    high = values.astype(LOW)
    rest = (values - high.astype(FULL)).astype(LOW)
    return dot(high, ones) + dot(rest, ones)


def head_ones(head_dim):
    row = lax.broadcasted_iota(jnp.int32, (LANES, LANES), 0) // head_dim
    col = lax.broadcasted_iota(jnp.int32, (LANES, LANES), 1) // head_dim
    return (row == col).astype(FULL).astype(LOW)


def turn_halves(values, half):
    lane = lax.broadcasted_iota(jnp.int32, values.shape, 1)
    ahead = pltpu.roll(values, LANES - half, 1)
    behind = pltpu.roll(values, half, 1)
    return jnp.where(lane % (2 * half) < half, ahead, behind)


def attend_body(last, dims, *refs):
    rows, pieces, part, block, head_dim, heads = dims
    (member, n_own, n_near, w_q, w_kv, cos, sin, start, gain_q, gain_k) = refs[:10]
    refs = refs[10:]
    if last:
        (w_o, w_o_first, mixed_first) = refs[:3]
        refs = refs[3:]
    (mixed, raw, inverse, q_pair, k_lo, k_hi, v_lo, v_hi) = refs[:8]
    refs = refs[8:]
    if last:
        (sum_own, sum_near) = refs[:2]
        refs = refs[2:]
    (by_token, a_token, r_token) = refs
    quarter_rows = pieces * part
    piece = 4 * part
    ones = head_ones(head_dim)

    def place(k, p):
        quarter = member[0] ^ RELATIVE[k]
        return pl.multiple_of(p * piece + quarter * part, 8)

    for k in range(4):
        here = pl.ds(k * quarter_rows, quarter_rows)
        source = n_own if k < 2 else n_near
        n_rows = source[(k % 2) * quarter_rows : (k % 2 + 1) * quarter_rows, :]
        query = dot(n_rows, w_q[...])
        keyval = dot(n_rows, w_kv[...])
        raw[here, : heads * LANES] = query.astype(LOW)
        raw[here, heads * LANES :] = keyval[:, :LANES].astype(LOW)
        parts = [query[:, h * LANES : (h + 1) * LANES] for h in range(heads)]
        parts.append(keyval[:, :LANES])
        turned = []
        for index, values in enumerate(parts):
            gain = gain_k if index == heads else gain_q
            mean = group_sums(values * values, ones) * (1.0 / head_dim)
            normed = values * lax.rsqrt(mean + EPSILON) * gain[...]
            turned.append(
                normed * cos[here, :] + turn_halves(normed, head_dim // 2) * sin[here, :]
            )
        turned.append(keyval[:, LANES:])
        for p in range(pieces):
            there = pl.ds(place(k, p), part)
            for index, values in enumerate(turned):
                by_token[index, there, :] = values[p * part : (p + 1) * part, :]

    scale = head_dim ** (-0.5)

    def prepare(i, carry):
        there = pl.ds(pl.multiple_of(i * block, block), block)
        low = lax.broadcasted_iota(jnp.int32, (block, LANES), 1) < head_dim
        for h in range(heads):
            q_pair[h, there, :] = (by_token[h, there, :] * scale).astype(LOW)
        key = by_token[heads, there, :]
        value = by_token[heads + 1, there, :]
        key_low = jnp.where(low, key, 0.0)
        key_high = jnp.where(low, 0.0, key)
        value_low = jnp.where(low, value, 1.0)
        value_high = jnp.where(low, 1.0, value)
        k_lo[0, there, :] = key_low.astype(LOW)
        k_hi[0, there, :] = pltpu.roll(key_low, head_dim, 1).astype(LOW)
        k_lo[1, there, :] = pltpu.roll(key_high, head_dim, 1).astype(LOW)
        k_hi[1, there, :] = key_high.astype(LOW)
        v_lo[0, there, :] = value_low.astype(LOW)
        v_hi[0, there, :] = pltpu.roll(value_low, head_dim, 1).astype(LOW)
        v_lo[1, there, :] = pltpu.roll(value_high, head_dim, 1).astype(LOW)
        v_hi[1, there, :] = value_high.astype(LOW)
        return carry

    lax.fori_loop(0, rows // block, prepare, 0)

    def one_head(h, carry):
        for i in range(rows // block):
            here = pl.ds(i * block, block)
            end = (i + 1) * block
            query = q_pair[h, here, :]
            key_row = lax.broadcasted_iota(jnp.int32, (block, end), 1)
            query_row = lax.broadcasted_iota(jnp.int32, (block, end), 0) + i * block
            seen = (key_row <= query_row) & (key_row >= start[here, :])
            mixed_parts = []
            for keys, values in ((k_lo, v_lo), (k_hi, v_hi)):
                scores = dot(query, keys[h, :end, :], 1, 1)
                weight = jnp.where(seen, jnp.exp(scores), 0.0).astype(LOW)
                mixed_parts.append(dot(weight, values[h, :end, :]))
            even, odd = mixed_parts
            low = lax.broadcasted_iota(jnp.int32, (block, LANES), 1) < head_dim
            divided = 1.0 / pltpu.roll(jnp.where(low, odd, even), head_dim, 1)
            a_token[h, here, :] = jnp.where(low, even, odd) * divided
            r_token[h, here, :] = divided
        return carry

    lax.fori_loop(0, heads, one_head, 0)

    for k in range(4):
        here = pl.ds(k * quarter_rows, quarter_rows)
        for h in range(heads):
            pieces_a = [a_token[h, pl.ds(place(k, p), part), :] for p in range(pieces)]
            pieces_r = [r_token[h, pl.ds(place(k, p), part), :] for p in range(pieces)]
            mixed[here, h * LANES : (h + 1) * LANES] = jnp.concatenate(pieces_a, axis=0).astype(LOW)
            inverse[h, here, :] = jnp.concatenate(pieces_r, axis=0)
        if last:
            total = dot(mixed[here, :], w_o[...]) + dot(mixed_first[here, :], w_o_first[...])
            target = sum_own if k < 2 else sum_near
            target[(k % 2) * quarter_rows : (k % 2 + 1) * quarter_rows, :] = total.astype(LOW)


def attend_back_body(last, dims, *refs):
    rows, pieces, part, block, head_dim, heads = dims
    (member, d_own, d_near, w_o, mixed, inverse, raw, cos, sin, start, gain_q, gain_k) = refs[:12]
    (q_pair, k_lo, k_hi, v_lo, v_hi) = refs[12:17]
    refs = refs[17:]
    if last:
        (w_q, w_kv, w_q_first, w_kv_first, d_raw_first) = refs[:5]
        refs = refs[5:]
    (d_raw, gains) = refs[:2]
    refs = refs[2:]
    if last:
        (sum_own, sum_near) = refs[:2]
        refs = refs[2:]
    (grad_token, grad_even, grad_odd, dq_token, dk_token, dv_token) = refs
    quarter_rows = pieces * part
    piece = 4 * part
    ones = head_ones(head_dim)
    scale = head_dim ** (-0.5)

    def place(k, p):
        quarter = member[0] ^ RELATIVE[k]
        return pl.multiple_of(p * piece + quarter * part, 8)

    for k in range(4):
        here = pl.ds(k * quarter_rows, quarter_rows)
        source = d_own if k < 2 else d_near
        d_rows = source[(k % 2) * quarter_rows : (k % 2 + 1) * quarter_rows, :]
        d_mixed = dot(d_rows, w_o[...], 1, 1)
        lane = lax.broadcasted_iota(jnp.int32, (quarter_rows, LANES), 1)
        low = lane < head_dim
        for h in range(heads):
            cols = slice(h * LANES, (h + 1) * LANES)
            grad = d_mixed[:, cols] * inverse[h, here, :]
            delta = group_sums(grad * mixed[here, cols].astype(FULL), ones)
            other = -pltpu.roll(delta, head_dim, 1)
            high = other.astype(LOW).astype(FULL)
            extra = jnp.where(lane % head_dim == 0, high, 0.0)
            extra = jnp.where(lane % head_dim == 1, other - high, extra)
            even = jnp.where(low, grad, extra)
            odd = jnp.where(low, extra, grad)
            for p in range(pieces):
                there = pl.ds(place(k, p), part)
                grad_token[2 * h, there, :] = even[p * part : (p + 1) * part, :]
                grad_token[2 * h + 1, there, :] = odd[p * part : (p + 1) * part, :]

    def prepare(i, carry):
        there = pl.ds(pl.multiple_of(i * block, block), block)
        for h in range(heads):
            grad_even[h, there, :] = grad_token[2 * h, there, :].astype(LOW)
            grad_odd[h, there, :] = grad_token[2 * h + 1, there, :].astype(LOW)
            dq_token[h, there, :] = jnp.zeros((block, LANES), FULL)
        return carry

    lax.fori_loop(0, rows // block, prepare, 0)

    def one_head(h, carry):
        for i in range(rows // block):
            first = i * block
            count = rows - first
            here = pl.ds(first, block)
            after = pl.ds(first, count)
            query = q_pair[h, after, :]
            key_row = lax.broadcasted_iota(jnp.int32, (block, count), 0)
            query_row = lax.broadcasted_iota(jnp.int32, (block, count), 1)
            seen = (key_row <= query_row) & (key_row + first >= start[:, after])
            d_keys = []
            d_values = []
            d_query = None
            for keys, values, grads in ((k_lo, v_lo, grad_even), (k_hi, v_hi, grad_odd)):
                key = keys[h, here, :]
                grad = grads[h, after, :]
                weight = jnp.where(seen, jnp.exp(dot(key, query, 1, 1)), 0.0)
                d_scores = (weight * dot(values[h, here, :], grad, 1, 1)).astype(LOW)
                d_values.append(dot(weight.astype(LOW), grad))
                d_keys.append(dot(d_scores, query))
                moved = dot(d_scores, key, 0, 0)
                d_query = moved if d_query is None else d_query + moved
            dq_token[h, after, :] += d_query
            low = lax.broadcasted_iota(jnp.int32, (block, LANES), 1) < head_dim
            for (even, odd), kept in ((d_keys, dk_token), (d_values, dv_token)):
                kept[h, here, :] = even + pltpu.roll(odd, head_dim, 1)
        return carry

    lax.fori_loop(0, heads, one_head, 0)

    gain_sums = [jnp.zeros((8, LANES), FULL), jnp.zeros((8, LANES), FULL)]
    for k in range(4):
        here = pl.ds(k * quarter_rows, quarter_rows)
        low = lax.broadcasted_iota(jnp.int32, (quarter_rows, LANES), 1) < head_dim

        def rows_of(token, h):
            return jnp.concatenate(
                [token[h, pl.ds(place(k, p), part), :] for p in range(pieces)], axis=0
            )

        def pair_of(token):
            return jnp.where(
                low, rows_of(token, 0), pltpu.roll(rows_of(token, 1), head_dim, 1)
            )

        turned = [rows_of(dq_token, h) * scale for h in range(heads)] + [pair_of(dk_token)]
        for index, values in enumerate(turned):
            is_key = index == heads
            gain = gain_k if is_key else gain_q
            cols = slice(index * LANES, (index + 1) * LANES)
            held = raw[here, cols].astype(FULL)
            root = lax.rsqrt(group_sums(held * held, ones) * (1.0 / head_dim) + EPSILON)
            normed = held * root
            back = values * cos[here, :] - turn_halves(values, head_dim // 2) * sin[here, :]
            scaled = back * gain[...]
            mean = group_sums(scaled * normed, ones) * (1.0 / head_dim)
            d_raw[here, cols] = (root * (scaled - normed * mean)).astype(LOW)
            products = (back * normed).reshape(quarter_rows // 8, 8, LANES)
            gain_sums[int(is_key)] = gain_sums[int(is_key)] + jnp.sum(products, axis=0)
        d_raw[here, (heads + 1) * LANES :] = pair_of(dv_token).astype(LOW)
        if last:
            wide = heads * LANES
            total = dot(d_raw[here, :wide], w_q[...], 1, 1)
            total = total + dot(d_raw[here, wide:], w_kv[...], 1, 1)
            total = total + dot(d_raw_first[here, :wide], w_q_first[...], 1, 1)
            total = total + dot(d_raw_first[here, wide:], w_kv_first[...], 1, 1)
            target = sum_own if k < 2 else sum_near
            target[(k % 2) * quarter_rows : (k % 2 + 1) * quarter_rows, :] = total.astype(LOW)
    gains[:8, :] = gain_sums[0]
    gains[8:, :] = gain_sums[1]


def feed_body(chunk, n_own, n_near, c_own, c_near, w_gate, w_up, w_down, *refs):
    refs = refs[-7:]
    (inner, d_gate, d_up, n_all, c_all, d_norm, partial) = refs
    step = pl.program_id(0)

    def run(n_ref, c_ref):
        n_rows = n_ref[...]
        c_rows = c_ref[...]
        n_all[...] = n_rows
        c_all[...] = c_rows
        hidden = w_gate.shape[1]
        total_n = None
        total_y = None
        for begin in range(0, hidden, chunk):
            cols = slice(begin, begin + chunk)
            gate = dot(n_rows, w_gate[:, cols])
            up_part = dot(n_rows, w_up[:, cols])
            d_inner = dot(c_rows, w_down[cols, :], 1, 1)
            sigma = 1.0 / (1.0 + jnp.exp(-gate))
            held = gate * sigma
            inner_low = (held * up_part).astype(LOW)
            d_gate_low = (d_inner * up_part * sigma * (1.0 + gate * (1.0 - sigma))).astype(LOW)
            d_up_low = (d_inner * held).astype(LOW)
            inner[:, cols] = inner_low
            d_gate[:, cols] = d_gate_low
            d_up[:, cols] = d_up_low
            more_n = dot(d_gate_low, w_gate[:, cols], 1, 1) + dot(d_up_low, w_up[:, cols], 1, 1)
            more_y = dot(inner_low, w_down[cols, :])
            total_n = more_n if total_n is None else total_n + more_n
            total_y = more_y if total_y is None else total_y + more_y
        d_norm[...] = total_n.astype(LOW)
        partial[...] = total_y.astype(LOW)

    @pl.when(step == 0)
    def _():
        run(n_own, c_own)

    @pl.when(step == 1)
    def _():
        run(n_near, c_near)


def feed(half, kept, n_own, n_near, c_own, c_near, w_gate, w_up, w_down):
    rows, width = n_own.shape
    hidden = w_gate.shape[1]
    whole = lambda shape: pl.BlockSpec(shape, lambda i: (0, 0))
    part = lambda cols: pl.BlockSpec((rows, cols), lambda i: (i + 2 * half, 0))
    in_specs = [whole(v.shape) for v in (n_own, n_near, c_own, c_near, w_gate, w_up, w_down)]
    all_rows = [
        jax.ShapeDtypeStruct((4 * rows, cols), LOW) for cols in (hidden, hidden, hidden, width, width)
    ]
    outs = all_rows + [jax.ShapeDtypeStruct((2 * rows, width), LOW)] * 2
    out_specs = [part(hidden)] * 3 + [part(width)] * 2
    out_specs += [pl.BlockSpec((rows, width), lambda i: (i, 0))] * 2
    aliases = {}
    if half:
        in_specs += [pl.BlockSpec(memory_space=pl.ANY)] * 5
        aliases = {7 + index: index for index in range(5)}
    work = 2 * rows * width * hidden * 2 * 6
    return pl.pallas_call(
        functools.partial(feed_body, hidden // 3),
        grid=(2,),
        in_specs=in_specs,
        out_specs=out_specs,
        out_shape=outs,
        input_output_aliases=aliases,
        compiler_params=pltpu.CompilerParams(
            vmem_limit_bytes=VMEM_BYTES, dimension_semantics=("arbitrary",)
        ),
        cost_estimate=pl.CostEstimate(
            flops=work, bytes_accessed=12 * rows * width * 4, transcendentals=0
        ),
    )(n_own, n_near, c_own, c_near, w_gate, w_up, w_down, *(kept if half else ()))


def each(count, act):
    if count <= 8:
        for index in range(count):
            act(index)
    else:
        lax.fori_loop(0, count, lambda index, carry: (act(index), carry)[1], 0)


def fetch(copies):
    for count, copy_of in copies:
        each(count, lambda index: copy_of(index).start())
    for count, copy_of in copies:
        each(count, lambda index: copy_of(index).wait())


HELD = pl.BlockSpec(memory_space=pl.ANY)


def pick_body(order, source, target, arrived):
    def copy_of(index):
        return pltpu.make_async_copy(
            source.at[order[index]], target.at[index], arrived.at[index]
        )

    fetch([(order.shape[0], copy_of)])


def pick(values, order):
    count = order.shape[0]
    return pl.pallas_call(
        pick_body,
        in_specs=[SMEM, HELD],
        out_specs=VMEM,
        out_shape=jax.ShapeDtypeStruct((count,) + values.shape[1:], values.dtype),
        scratch_shapes=[pltpu.SemaphoreType.DMA((count,))],
        compiler_params=pltpu.CompilerParams(vmem_limit_bytes=VMEM_BYTES),
    )(order, values)


def across_dp(values):
    return lax.all_to_all(values, "dp", split_axis=0, concat_axis=0, tiled=True)


def join_body(first_order, second_order, first, second, target, arrived):
    count = first_order.shape[0]

    def first_copy(index):
        return pltpu.make_async_copy(
            first.at[first_order[index]], target.at[index], arrived.at[index]
        )

    def second_copy(index):
        return pltpu.make_async_copy(
            second.at[second_order[index]], target.at[count + index], arrived.at[count + index]
        )

    fetch([(count, first_copy), (count, second_copy)])


def join(first, first_order, second, second_order):
    count = first_order.shape[0]
    return pl.pallas_call(
        join_body,
        in_specs=[SMEM, SMEM, HELD, HELD],
        out_specs=VMEM,
        out_shape=jax.ShapeDtypeStruct((2 * count,) + first.shape[1:], first.dtype),
        scratch_shapes=[pltpu.SemaphoreType.DMA((2 * count,))],
        compiler_params=pltpu.CompilerParams(vmem_limit_bytes=VMEM_BYTES),
    )(first_order, second_order, first, second)


def place_body(order, member, *refs):
    sources = refs[:4]
    target, arrived = refs[4:]
    copies = []
    for k, source in enumerate(sources):

        def copy_of(index, k=k, source=source):
            return pltpu.make_async_copy(
                source.at[order[index]],
                target.at[index, member[0] ^ RELATIVE[k]],
                arrived.at[k, index],
            )

        copies.append((order.shape[0], copy_of))
    fetch(copies)


def place_pieces(parts, order, member):
    count, part_rows, width = parts[0].shape
    pieces = pl.pallas_call(
        place_body,
        in_specs=[SMEM, SMEM] + [HELD] * 4,
        out_specs=VMEM,
        out_shape=jax.ShapeDtypeStruct((count, 4, part_rows, width), parts[0].dtype),
        scratch_shapes=[pltpu.SemaphoreType.DMA((4, count))],
        compiler_params=pltpu.CompilerParams(vmem_limit_bytes=VMEM_BYTES),
    )(order, member, *parts)
    return pieces.reshape(count * 4 * part_rows, width)


def fence(*values):
    return lax.optimization_barrier(values)


def reduce_step(total, step, device):
    bit = (device // step) & 1
    split = total.reshape((total.shape[0] // 2, 2) + total.shape[1:])
    sent = lax.dynamic_index_in_dim(split, 1 - bit, 1, keepdims=False).astype(LOW)
    kept = lax.dynamic_index_in_dim(split, bit, 1, keepdims=False)
    return (kept, swap(sent, "dp", step))


def add(first, second):
    return first.astype(FULL) + second.astype(FULL)


def reduce_rest(kept, got, steps, device):
    for step in steps:
        kept, got = reduce_step(add(kept, got), step, device)
    return add(kept, got)[0]


def by_device(product, devices):
    return product.reshape((devices, product.shape[0] // devices) + product.shape[1:])


def gather_dp(own, devices):
    held = own[None]
    for step in reversed(bits_of(devices)):
        held = jnp.concatenate([held, swap(held, "dp", step)], axis=0)
    return held


def places_of(devices, device):
    apart = jnp.arange(devices, dtype=jnp.int32) ^ device
    place = jnp.zeros_like(apart)
    for index, step in enumerate(bits_of(devices)):
        place = place + ((apart // step) & 1) * (devices // 2 // step)
    return place


def row_norm(values, gain_row):
    inverse = lax.rsqrt(jnp.mean(values * values, axis=-1, keepdims=True) + EPSILON)
    return (values * inverse * gain_row, inverse)


def row_norm_back(gradient, values, inverse, gain_row):
    scaled = gradient * gain_row
    d_values = inverse * scaled - values * (inverse * inverse * inverse) * jnp.mean(
        scaled * values, axis=-1, keepdims=True
    )
    d_gain = jnp.sum(gradient * values * inverse, axis=0)
    return (d_values, d_gain)


def local(
    tokens,
    cotangent,
    seq_lengths,
    deal,
    w_query,
    w_keyval,
    w_output,
    w_gateup,
    w_down,
    norm_gains,
    head_gains,
    master_query,
    master_keyval,
    master_output,
    master_gateup,
    master_down,
    start_query,
    start_keyval,
    start_output,
    start_gateup,
    start_down,
    start_norms,
    start_heads,
    step_size,
):
    devices = lax.axis_size("dp")
    ways = lax.axis_size("mp")
    device = lax.axis_index("dp")
    member = lax.axis_index("mp")
    row_count, width = tokens.shape
    total_pieces = deal.shape[0]
    pieces_dev = total_pieces // devices
    piece_rows = row_count // pieces_dev
    part_rows = piece_rows // ways
    slot_count = seq_lengths.shape[0]
    slot_rows = row_count // slot_count
    slot_pieces = pieces_dev // slot_count
    quarter_rows = slot_pieces * part_rows
    half_rows = 2 * quarter_rows
    head_dim = head_gains.shape[1]
    query_cols = w_query.shape[1]
    key_cols = w_keyval.shape[2]
    heads = query_cols // LANES
    hidden = w_down.shape[0]
    step = step_size[0]
    slot = member // 2
    member_ref = member.reshape(1).astype(jnp.int32)

    placed = jnp.arange(pieces_dev, dtype=jnp.int32)
    my_places = lax.dynamic_slice_in_dim(deal, device * pieces_dev, pieces_dev)
    target = my_places // pieces_dev
    piece_to = jnp.sum((target[:, None] == placed[None, :]) * placed[:, None], axis=0)
    whole = jnp.arange(total_pieces, dtype=jnp.int32)
    held_here = deal[:, None] == (device * pieces_dev + placed)[None, :]
    source = jnp.sum(held_here * (whole // pieces_dev)[:, None], axis=0)
    place_from = jnp.sum((source[:, None] == placed[None, :]) * placed[:, None], axis=0)
    slot_source = source.reshape(slot_count, slot_pieces)
    own_source = lax.dynamic_index_in_dim(slot_source, slot, 0, keepdims=False)
    other_source = lax.dynamic_index_in_dim(slot_source, 1 - slot, 0, keepdims=False)
    in_order = jnp.arange(slot_pieces, dtype=jnp.int32)

    def deal_in(values):
        quarters = values.reshape(pieces_dev * ways, part_rows, width)
        return across_dp(pick(quarters, piece_to * ways + member))

    def rows_of(pieces):
        return pieces.reshape(-1, width)

    x_got = deal_in(tokens)

    lengths = lax.dynamic_index_in_dim(seq_lengths, slot, 0, keepdims=False)
    ends = jnp.cumsum(lengths)

    def position_of(token):
        passed = (token[:, None] >= ends[None, :]).astype(jnp.int32)
        return token - jnp.sum(passed * lengths[None, :], axis=1)

    token_row = jnp.arange(slot_rows, dtype=jnp.int32)
    start = token_row - position_of(token_row)
    quarters = jnp.asarray(RELATIVE, jnp.int32) ^ member
    relative_token = (
        (in_order * piece_rows)[None, :, None]
        + (quarters * part_rows)[:, None, None]
        + jnp.arange(part_rows, dtype=jnp.int32)[None, None, :]
    ).reshape(-1)
    lane = jnp.arange(LANES, dtype=jnp.int32)
    half = head_dim // 2
    freqs = ROPE_BASE ** (-(lane % half).astype(FULL) * (2.0 / head_dim))
    angles = position_of(relative_token).astype(FULL)[:, None] * freqs[None, :]
    cosine = jnp.cos(angles)
    sine = jnp.sin(angles) * jnp.where(lane % head_dim < half, -1.0, 1.0)[None, :]
    gain_q = jnp.tile(head_gains[0:1], (1, LANES // head_dim))
    gain_k = jnp.tile(head_gains[1:2], (1, LANES // head_dim))

    w_keyval_flat = w_keyval.reshape(width, 2 * key_cols)
    groups = (
        (w_query, w_keyval_flat, w_output),
        (far(w_query), far(w_keyval_flat), far(w_output)),
    )
    w_gate = w_gateup[:, 0]
    w_up = w_gateup[:, 1]

    def ahead(master, begin):
        return (master - 0.5 * step * begin).astype(LOW)

    small = jnp.concatenate(
        [
            ahead(master_query, start_query),
            ahead(master_keyval, start_keyval).reshape(-1, 2 * key_cols),
            ahead(master_output, start_output).T,
        ],
        axis=1,
    )
    part_gateup = ahead(master_gateup, start_gateup)
    part_down = ahead(master_down, start_down)

    early = fence(x_got, small, part_gateup, part_down, cosine, sine, w_gate, w_up, groups)
    x_got, small, part_gateup, part_down, cosine, sine, w_gate, w_up, groups = early
    x_other = far(pick(x_got, other_source))
    cotangent, _ = fence(cotangent, x_got)
    c_got = deal_in(cotangent)
    x_own = rows_of(join(x_got, own_source, x_other, in_order))
    ahead_small = lax.all_gather(small, "dp", axis=0, tiled=True)
    ahead_gateup = lax.all_gather(part_gateup, "dp", axis=0, tiled=True)
    ahead_down = lax.all_gather(part_down, "dp", axis=0, tiled=False)

    x_full = x_own.astype(FULL)
    norm_one_f, inv_one = row_norm(x_full, norm_gains[0])
    norm_own = norm_one_f.astype(LOW)
    norm_near = near(norm_own)

    dims = (slot_rows, slot_pieces, part_rows, slot_rows // 6, head_dim, heads)
    shape = jax.ShapeDtypeStruct

    def attend(last, weights, more):
        token_shape = (heads, slot_rows, LANES)
        outs = [
            shape((slot_rows, query_cols), LOW),
            shape((slot_rows, query_cols + key_cols), LOW),
            shape(token_shape, FULL),
        ] + [shape(token_shape, LOW)] * 5
        if last:
            outs += [shape((half_rows, width), LOW)] * 2
        arguments = (
            member_ref,
            norm_own,
            norm_near,
            weights[0],
            weights[1],
            cosine,
            sine,
            start.reshape(-1, 1),
            gain_q,
            gain_k,
        ) + more
        return pl.pallas_call(
            functools.partial(attend_body, last, dims),
            in_specs=[SMEM] + [VMEM] * (len(arguments) - 1),
            out_specs=[VMEM] * len(outs),
            out_shape=outs,
            scratch_shapes=[
                pltpu.VMEM((heads + 2, slot_rows, LANES), FULL),
                pltpu.VMEM((heads, slot_rows, LANES), FULL),
                pltpu.VMEM((heads, slot_rows, LANES), FULL),
            ],
            compiler_params=pltpu.CompilerParams(vmem_limit_bytes=VMEM_BYTES),
            cost_estimate=pl.CostEstimate(
                flops=12_000_000_000, bytes_accessed=12_000_000, transcendentals=0
            ),
        )(*arguments)

    def attend_back(last, weights, kept, d_own, d_near, more):
        token_shape = (heads, slot_rows, LANES)
        mixed, raw, inverse, *tables = kept
        outs = [shape((slot_rows, query_cols + 2 * key_cols), LOW), shape((16, LANES), FULL)]
        if last:
            outs += [shape((half_rows, width), LOW)] * 2
        arguments = (
            member_ref,
            d_own,
            d_near,
            weights[2],
            mixed,
            inverse,
            raw,
            cosine,
            sine,
            start.reshape(1, -1),
            gain_q,
            gain_k,
            *tables,
        ) + more
        return pl.pallas_call(
            functools.partial(attend_back_body, last, dims),
            in_specs=[SMEM] + [VMEM] * (len(arguments) - 1),
            out_specs=[VMEM] * len(outs),
            out_shape=outs,
            scratch_shapes=[
                pltpu.VMEM((2 * heads, slot_rows, LANES), FULL),
                pltpu.VMEM(token_shape, LOW),
                pltpu.VMEM(token_shape, LOW),
                pltpu.VMEM(token_shape, FULL),
                pltpu.VMEM(token_shape, FULL),
                pltpu.VMEM(token_shape, FULL),
            ],
            compiler_params=pltpu.CompilerParams(vmem_limit_bytes=VMEM_BYTES),
            cost_estimate=pl.CostEstimate(
                flops=20_000_000_000, bytes_accessed=14_000_000, transcendentals=0
            ),
        )(*arguments)

    first_kept = attend(False, groups[0], ())
    c_got, first_kept = fence(c_got, first_kept)
    c_own_far = far(pick(c_got, other_source))
    c_other_far = far(pick(c_got, own_source))
    *second_kept, attn_own, attn_near = attend(
        True, groups[1], (groups[1][2], groups[0][2], first_kept[0])
    )
    c_own = rows_of(join(c_got, own_source, c_own_far, in_order))
    c_near = near(c_own)
    attn_sum = add(attn_own, near(attn_near))
    hidden_one = x_full + attn_sum
    norm_two_f, inv_two = row_norm(hidden_one, norm_gains[1])
    two_own = norm_two_f.astype(LOW)
    two_near = near(two_own)
    two_far = far(two_own)
    two_across = near(two_far)
    c_far = rows_of(join(c_other_far, in_order, c_got, other_source))
    c_across = near(c_far)

    *kept, d_two_own, ffn_own = feed(0, (), two_own, two_near, c_own, c_near, w_gate, w_up, w_down)
    near_own = near(d_two_own[half_rows:])
    *kept, d_two_far, ffn_far = feed(
        1, kept, two_far, two_across, c_far, c_across, w_gate, w_up, w_down
    )
    near_far = near(d_two_far[half_rows:])
    pair_far = add(d_two_far[:half_rows], near_far).astype(LOW)
    pair_far, kept, ffn_far = fence(pair_far, kept, ffn_far)
    inner, d_gate, d_up, two_all, c_all = kept
    pair_got = far(pair_far)
    grad_down = dot(c_all, inner, 0, 0).astype(LOW)
    grad_gate = dot(two_all, d_gate, 0, 0).astype(LOW)
    grad_up = dot(two_all, d_up, 0, 0).astype(LOW)
    ffn_pair_far = add(ffn_far[:half_rows], near(ffn_far[half_rows:])).astype(LOW)
    ffn_pair_own = add(ffn_own[:half_rows], near(ffn_own[half_rows:]))
    stepped = fence(pair_got, grad_down, grad_gate, grad_up, ffn_pair_far)
    pair_got, grad_down, grad_gate, grad_up, ffn_pair_far = stepped
    steps = bits_of(devices)
    down_kept, down_got = reduce_step(by_device(grad_down, devices), steps[0], device)
    gate_kept, gate_got = reduce_step(by_device(grad_gate, devices), steps[0], device)
    up_kept, up_got = reduce_step(by_device(grad_up, devices), steps[0], device)
    ffn_got = far(ffn_pair_far)

    d_norm_two = add(d_two_own[:half_rows], near_own) + pair_got.astype(FULL)
    d_hidden_part, gain_two = row_norm_back(d_norm_two, hidden_one, inv_two, norm_gains[1])
    d_hidden = c_own.astype(FULL) + d_hidden_part
    dh_own = d_hidden.astype(LOW)
    dh_near = near(dh_own)

    def over_rows(own, other, values):
        return dot(own, values[:half_rows], 0, 0) + dot(other, values[half_rows:], 0, 0)

    d_raw_far, gains_far = attend_back(False, groups[1], second_kept, dh_own, dh_near, ())
    stepped = fence(d_raw_far, down_got, gate_got, ffn_got)
    d_raw_far, down_got, gate_got, ffn_got = stepped
    down_kept, down_got = reduce_step(add(down_kept, down_got), steps[1], device)
    gate_kept, gate_got = reduce_step(add(gate_kept, gate_got), steps[1], device)
    out_own = (hidden_one + ffn_pair_own + ffn_got.astype(FULL)).astype(LOW)
    out_other = far(out_own[quarter_rows:])
    grad_output_got = far(over_rows(dh_own, dh_near, second_kept[0]).astype(LOW))
    grad_qkv_got = far(over_rows(norm_own, norm_near, d_raw_far).astype(LOW))
    grad_output_mine = over_rows(dh_own, dh_near, first_kept[0])
    d_raw_own, gains_own, d_one_own, d_one_near = attend_back(
        True,
        groups[0],
        first_kept,
        dh_own,
        dh_near,
        (groups[0][0], groups[0][1], groups[1][0], groups[1][1], d_raw_far),
    )
    stepped = fence(d_raw_own, d_one_near, down_got, gate_got, up_got, out_other, grad_output_got)
    d_raw_own, d_one_near, down_got, gate_got, up_got, out_other, grad_output_got = stepped
    d_norm_one = add(d_one_own, near(d_one_near))
    d_input_part, gain_one = row_norm_back(d_norm_one, x_full, inv_one, norm_gains[0])
    dx_own = (d_hidden + d_input_part).astype(LOW)

    own_down = reduce_rest(down_kept, down_got, steps[2:], device)
    own_gate = reduce_rest(gate_kept, gate_got, steps[2:], device)
    own_up = reduce_rest(up_kept, up_got, steps[1:], device)
    grad_output = add(grad_output_mine, grad_output_got)
    grad_qkv = add(over_rows(norm_own, norm_near, d_raw_own), grad_qkv_got)
    own_output = reduce_rest(
        *reduce_step(by_device(grad_output, devices), steps[0], device), steps[1:], device
    )
    own_qkv = reduce_rest(
        *reduce_step(by_device(grad_qkv, devices), steps[0], device), steps[1:], device
    )

    def deal_out(values, other):
        mine = values[:quarter_rows].reshape(slot_pieces, part_rows, width)
        other = other.reshape(slot_pieces, part_rows, width)
        held = jnp.concatenate([mine, other], axis=0)
        order = (place_from + (slot_count - slot) * slot_pieces) % pieces_dev
        got = across_dp(pick(held, order))
        got_far = far(got)
        return place_pieces((got, got_far, near(got), near(got_far)), target, member_ref)

    output = deal_out(out_own, out_other)
    input_grad = deal_out(dx_own, far(dx_own[quarter_rows:]))

    owned = (own_qkv, own_output, own_gate, own_up, own_down)
    own_square = sum([jnp.sum(part_grad * part_grad) for part_grad in owned])
    gains = jnp.sum((gains_far + gains_own).reshape(2, 8, LANES // head_dim, head_dim), axis=(1, 2))
    packed = jnp.concatenate(
        [gain_one, gain_two, gains.reshape(-1), jnp.broadcast_to(own_square, (LANES,))]
    ).reshape(-1, LANES)
    for axis, size in (("mp", ways), ("dp", devices)):
        for bit in bits_of(size):
            packed = packed + swap(packed, axis, bit)
    flat = packed.reshape(-1)
    norm_sum = flat[: 2 * width].reshape(2, width)
    head_sum = flat[2 * width : 2 * width + 2 * head_dim].reshape(2, head_dim)
    square_sum = flat[2 * width + 2 * head_dim]
    clip_value = jnp.sqrt(square_sum + jnp.sum(norm_sum * norm_sum) + jnp.sum(head_sum * head_sum))
    limit = math.sqrt(2 * D * H * HD + 2 * D * KV * HD + 3 * D * FF + 2 * D + 2 * HD)
    factor = jnp.minimum(1.0, limit / clip_value)

    owned_parts = (
        own_qkv[:, :query_cols],
        own_qkv[:, query_cols:].reshape(-1, 2, key_cols),
        own_output.T,
        jnp.stack([own_gate, own_up], axis=1),
        own_down.T,
    )
    starts = (start_query, start_keyval, start_output, start_gateup, start_down)
    masters = (master_query, master_keyval, master_output, master_gateup, master_down)
    moments = [0.5 * begin + factor * part_grad for begin, part_grad in zip(starts, owned_parts)]
    nexts = [held - step * moved for held, moved in zip(masters, moments)]
    moment_norms = 0.5 * start_norms + factor * norm_sum
    moment_heads = 0.5 * start_heads + factor * head_sum
    next_norms = norm_gains - step * moment_norms
    next_heads = head_gains - step * moment_heads

    order = places_of(devices, device)

    def spread(own):
        return pick(gather_dp(own.astype(LOW), devices), order)

    all_qkv = spread(own_qkv).reshape(width, -1)
    all_output = spread(own_output).reshape(width, -1)
    all_gateup = spread(owned_parts[3]).reshape(width, 2, hidden)
    all_down = spread(owned_parts[4])
    pull = step * factor

    def finish(ahead_part, gradient):
        return (ahead_part.astype(FULL) - pull * gradient.astype(FULL)).astype(LOW)

    done_small = finish(ahead_small, jnp.concatenate([all_qkv, all_output], axis=1))
    weights = (
        done_small[:, :query_cols],
        done_small[:, query_cols : query_cols + 2 * key_cols].reshape(width, 2, key_cols),
        done_small[:, query_cols + 2 * key_cols :].T,
        finish(ahead_gateup, all_gateup),
        finish(ahead_down, all_down).transpose(1, 0, 2).reshape(hidden, width),
    )
    return (
        output,
        input_grad,
        clip_value.reshape(1),
        *moments,
        moment_norms,
        moment_heads,
        *nexts,
        next_norms,
        next_heads,
        *weights,
    )


def solution(mesh):
    in_specs = (
        P("dp", None),
        P("dp", None),
        P("dp", None),
        P(),
        P(None, "mp"),
        P(None, None, "mp"),
        P("mp", None),
        P(None, None, "mp"),
        P("mp", None),
        P(),
        P(),
        P("dp", "mp"),
        P("dp", None, "mp"),
        P("mp", "dp"),
        P("dp", None, "mp"),
        P("mp", "dp"),
        P("dp", "mp"),
        P("dp", None, "mp"),
        P("mp", "dp"),
        P("dp", None, "mp"),
        P("mp", "dp"),
        P(),
        P(),
        P(),
    )
    out_specs = (
        P("dp", None),
        P("dp", None),
        P(),
        P("dp", "mp"),
        P("dp", None, "mp"),
        P("mp", "dp"),
        P("dp", None, "mp"),
        P("mp", "dp"),
        P(),
        P(),
        P("dp", "mp"),
        P("dp", None, "mp"),
        P("mp", "dp"),
        P("dp", None, "mp"),
        P("mp", "dp"),
        P(),
        P(),
        P(None, "mp"),
        P(None, None, "mp"),
        P("mp", None),
        P(None, None, "mp"),
        P("mp", None),
    )
    return jax.shard_map(local, mesh=mesh, in_specs=in_specs, out_specs=out_specs, check_vma=False)
```

```python
import functools
import math

import jax
import jax.numpy as jnp
from jax import lax
from jax.experimental import pallas as pl
from jax.experimental.pallas import tpu as pltpu
from jax.sharding import PartitionSpec as P

D = 1024
H = 16
KV = 8
HD = 64
FF = 4608


EPSILON = 1e-05
ROPE_BASE = 1000000.0
LOW = jnp.bfloat16
FULL = jnp.float32
LANES = 128


def dot(left, right, left_dim=1, right_dim=0):
    return lax.dot_general(
        left, right, (((left_dim,), (right_dim,)), ((), ())), preferred_element_type=FULL
    )


def swap(values, axis, bit):
    size = lax.axis_size(axis)
    return lax.ppermute(values, axis, [(place, place ^ bit) for place in range(size)])


def far(values):
    return swap(values, "mp", 2)


def near(values):
    return swap(values, "mp", 1)


def bits_of(count):
    return [1 << place for place in range(count.bit_length() - 1)]


RELATIVE = (0, 2, 1, 3)
VMEM = pl.BlockSpec(memory_space=pltpu.VMEM)
SMEM = pl.BlockSpec(memory_space=pltpu.SMEM)
VMEM_BYTES = 60 * 1024 * 1024


def group_sums(values, ones):
    high = values.astype(LOW)
    rest = (values - high.astype(FULL)).astype(LOW)
    return dot(high, ones) + dot(rest, ones)


def head_ones(head_dim):
    row = lax.broadcasted_iota(jnp.int32, (LANES, LANES), 0) // head_dim
    col = lax.broadcasted_iota(jnp.int32, (LANES, LANES), 1) // head_dim
    return (row == col).astype(FULL).astype(LOW)


def turn_halves(values, half):
    lane = lax.broadcasted_iota(jnp.int32, values.shape, 1)
    ahead = pltpu.roll(values, LANES - half, 1)
    behind = pltpu.roll(values, half, 1)
    return jnp.where(lane % (2 * half) < half, ahead, behind)


def attend_body(last, dims, *refs):
    rows, pieces, part, block, head_dim, heads = dims
    (member, n_own, n_near, w_q, w_kv, cos, sin, start, gain_q, gain_k) = refs[:10]
    refs = refs[10:]
    if last:
        (w_o, w_o_first, mixed_first) = refs[:3]
        refs = refs[3:]
    (mixed, raw, inverse, q_pair, k_lo, k_hi, v_lo, v_hi) = refs[:8]
    refs = refs[8:]
    if last:
        (sum_own, sum_near) = refs[:2]
        refs = refs[2:]
    (by_token, a_token, r_token) = refs
    quarter_rows = pieces * part
    piece = 4 * part
    ones = head_ones(head_dim)

    def place(k, p):
        quarter = member[0] ^ RELATIVE[k]
        return pl.multiple_of(p * piece + quarter * part, 8)

    for k in range(4):
        here = pl.ds(k * quarter_rows, quarter_rows)
        source = n_own if k < 2 else n_near
        n_rows = source[(k % 2) * quarter_rows : (k % 2 + 1) * quarter_rows, :]
        query = dot(n_rows, w_q[...])
        keyval = dot(n_rows, w_kv[...])
        raw[here, : heads * LANES] = query.astype(LOW)
        raw[here, heads * LANES :] = keyval[:, :LANES].astype(LOW)
        parts = [query[:, h * LANES : (h + 1) * LANES] for h in range(heads)]
        parts.append(keyval[:, :LANES])
        turned = []
        for index, values in enumerate(parts):
            gain = gain_k if index == heads else gain_q
            mean = group_sums(values * values, ones) * (1.0 / head_dim)
            normed = values * lax.rsqrt(mean + EPSILON) * gain[...]
            turned.append(
                normed * cos[here, :] + turn_halves(normed, head_dim // 2) * sin[here, :]
            )
        turned.append(keyval[:, LANES:])
        for p in range(pieces):
            there = pl.ds(place(k, p), part)
            for index, values in enumerate(turned):
                by_token[index, there, :] = values[p * part : (p + 1) * part, :]

    scale = head_dim ** (-0.5)

    def prepare(i, carry):
        there = pl.ds(pl.multiple_of(i * block, block), block)
        low = lax.broadcasted_iota(jnp.int32, (block, LANES), 1) < head_dim
        for h in range(heads):
            q_pair[h, there, :] = (by_token[h, there, :] * scale).astype(LOW)
        key = by_token[heads, there, :]
        value = by_token[heads + 1, there, :]
        key_low = jnp.where(low, key, 0.0)
        key_high = jnp.where(low, 0.0, key)
        value_low = jnp.where(low, value, 1.0)
        value_high = jnp.where(low, 1.0, value)
        k_lo[0, there, :] = key_low.astype(LOW)
        k_hi[0, there, :] = pltpu.roll(key_low, head_dim, 1).astype(LOW)
        k_lo[1, there, :] = pltpu.roll(key_high, head_dim, 1).astype(LOW)
        k_hi[1, there, :] = key_high.astype(LOW)
        v_lo[0, there, :] = value_low.astype(LOW)
        v_hi[0, there, :] = pltpu.roll(value_low, head_dim, 1).astype(LOW)
        v_lo[1, there, :] = pltpu.roll(value_high, head_dim, 1).astype(LOW)
        v_hi[1, there, :] = value_high.astype(LOW)
        return carry

    lax.fori_loop(0, rows // block, prepare, 0)

    def one_head(h, carry):
        for i in range(rows // block):
            here = pl.ds(i * block, block)
            end = (i + 1) * block
            query = q_pair[h, here, :]
            key_row = lax.broadcasted_iota(jnp.int32, (block, end), 1)
            query_row = lax.broadcasted_iota(jnp.int32, (block, end), 0) + i * block
            seen = (key_row <= query_row) & (key_row >= start[here, :])
            mixed_parts = []
            for keys, values in ((k_lo, v_lo), (k_hi, v_hi)):
                scores = dot(query, keys[h, :end, :], 1, 1)
                weight = jnp.where(seen, jnp.exp(scores), 0.0).astype(LOW)
                mixed_parts.append(dot(weight, values[h, :end, :]))
            even, odd = mixed_parts
            low = lax.broadcasted_iota(jnp.int32, (block, LANES), 1) < head_dim
            divided = 1.0 / pltpu.roll(jnp.where(low, odd, even), head_dim, 1)
            a_token[h, here, :] = jnp.where(low, even, odd) * divided
            r_token[h, here, :] = divided
        return carry

    lax.fori_loop(0, heads, one_head, 0)

    for k in range(4):
        here = pl.ds(k * quarter_rows, quarter_rows)
        for h in range(heads):
            pieces_a = [a_token[h, pl.ds(place(k, p), part), :] for p in range(pieces)]
            pieces_r = [r_token[h, pl.ds(place(k, p), part), :] for p in range(pieces)]
            mixed[here, h * LANES : (h + 1) * LANES] = jnp.concatenate(pieces_a, axis=0).astype(LOW)
            inverse[h, here, :] = jnp.concatenate(pieces_r, axis=0)
        if last:
            total = dot(mixed[here, :], w_o[...]) + dot(mixed_first[here, :], w_o_first[...])
            target = sum_own if k < 2 else sum_near
            target[(k % 2) * quarter_rows : (k % 2 + 1) * quarter_rows, :] = total.astype(LOW)


def attend_back_body(last, dims, *refs):
    rows, pieces, part, block, head_dim, heads = dims
    (member, d_own, d_near, w_o, mixed, inverse, raw, cos, sin, start, gain_q, gain_k) = refs[:12]
    (q_pair, k_lo, k_hi, v_lo, v_hi) = refs[12:17]
    refs = refs[17:]
    if last:
        (w_q, w_kv, w_q_first, w_kv_first, d_raw_first) = refs[:5]
        refs = refs[5:]
    (d_raw, gains) = refs[:2]
    refs = refs[2:]
    if last:
        (sum_own, sum_near) = refs[:2]
        refs = refs[2:]
    (grad_token, grad_even, grad_odd, dq_token, dk_token, dv_token) = refs
    quarter_rows = pieces * part
    piece = 4 * part
    ones = head_ones(head_dim)
    scale = head_dim ** (-0.5)

    def place(k, p):
        quarter = member[0] ^ RELATIVE[k]
        return pl.multiple_of(p * piece + quarter * part, 8)

    for k in range(4):
        here = pl.ds(k * quarter_rows, quarter_rows)
        source = d_own if k < 2 else d_near
        d_rows = source[(k % 2) * quarter_rows : (k % 2 + 1) * quarter_rows, :]
        d_mixed = dot(d_rows, w_o[...], 1, 1)
        lane = lax.broadcasted_iota(jnp.int32, (quarter_rows, LANES), 1)
        low = lane < head_dim
        for h in range(heads):
            cols = slice(h * LANES, (h + 1) * LANES)
            grad = d_mixed[:, cols] * inverse[h, here, :]
            delta = group_sums(grad * mixed[here, cols].astype(FULL), ones)
            other = -pltpu.roll(delta, head_dim, 1)
            high = other.astype(LOW).astype(FULL)
            extra = jnp.where(lane % head_dim == 0, high, 0.0)
            extra = jnp.where(lane % head_dim == 1, other - high, extra)
            even = jnp.where(low, grad, extra)
            odd = jnp.where(low, extra, grad)
            for p in range(pieces):
                there = pl.ds(place(k, p), part)
                grad_token[2 * h, there, :] = even[p * part : (p + 1) * part, :]
                grad_token[2 * h + 1, there, :] = odd[p * part : (p + 1) * part, :]

    def prepare(i, carry):
        there = pl.ds(pl.multiple_of(i * block, block), block)
        for h in range(heads):
            grad_even[h, there, :] = grad_token[2 * h, there, :].astype(LOW)
            grad_odd[h, there, :] = grad_token[2 * h + 1, there, :].astype(LOW)
            dq_token[h, there, :] = jnp.zeros((block, LANES), FULL)
        return carry

    lax.fori_loop(0, rows // block, prepare, 0)

    def one_head(h, carry):
        for i in range(rows // block):
            first = i * block
            count = rows - first
            here = pl.ds(first, block)
            after = pl.ds(first, count)
            query = q_pair[h, after, :]
            key_row = lax.broadcasted_iota(jnp.int32, (block, count), 0)
            query_row = lax.broadcasted_iota(jnp.int32, (block, count), 1)
            seen = (key_row <= query_row) & (key_row + first >= start[:, after])
            d_keys = []
            d_values = []
            d_query = None
            for keys, values, grads in ((k_lo, v_lo, grad_even), (k_hi, v_hi, grad_odd)):
                key = keys[h, here, :]
                grad = grads[h, after, :]
                weight = jnp.where(seen, jnp.exp(dot(key, query, 1, 1)), 0.0)
                d_scores = (weight * dot(values[h, here, :], grad, 1, 1)).astype(LOW)
                d_values.append(dot(weight.astype(LOW), grad))
                d_keys.append(dot(d_scores, query))
                moved = dot(d_scores, key, 0, 0)
                d_query = moved if d_query is None else d_query + moved
            dq_token[h, after, :] += d_query
            low = lax.broadcasted_iota(jnp.int32, (block, LANES), 1) < head_dim
            for (even, odd), kept in ((d_keys, dk_token), (d_values, dv_token)):
                kept[h, here, :] = even + pltpu.roll(odd, head_dim, 1)
        return carry

    lax.fori_loop(0, heads, one_head, 0)

    gain_sums = [jnp.zeros((8, LANES), FULL), jnp.zeros((8, LANES), FULL)]
    for k in range(4):
        here = pl.ds(k * quarter_rows, quarter_rows)
        low = lax.broadcasted_iota(jnp.int32, (quarter_rows, LANES), 1) < head_dim

        def rows_of(token, h):
            return jnp.concatenate(
                [token[h, pl.ds(place(k, p), part), :] for p in range(pieces)], axis=0
            )

        def pair_of(token):
            return jnp.where(
                low, rows_of(token, 0), pltpu.roll(rows_of(token, 1), head_dim, 1)
            )

        turned = [rows_of(dq_token, h) * scale for h in range(heads)] + [pair_of(dk_token)]
        for index, values in enumerate(turned):
            is_key = index == heads
            gain = gain_k if is_key else gain_q
            cols = slice(index * LANES, (index + 1) * LANES)
            held = raw[here, cols].astype(FULL)
            root = lax.rsqrt(group_sums(held * held, ones) * (1.0 / head_dim) + EPSILON)
            normed = held * root
            back = values * cos[here, :] - turn_halves(values, head_dim // 2) * sin[here, :]
            scaled = back * gain[...]
            mean = group_sums(scaled * normed, ones) * (1.0 / head_dim)
            d_raw[here, cols] = (root * (scaled - normed * mean)).astype(LOW)
            products = (back * normed).reshape(quarter_rows // 8, 8, LANES)
            gain_sums[int(is_key)] = gain_sums[int(is_key)] + jnp.sum(products, axis=0)
        d_raw[here, (heads + 1) * LANES :] = pair_of(dv_token).astype(LOW)
        if last:
            wide = heads * LANES
            total = dot(d_raw[here, :wide], w_q[...], 1, 1)
            total = total + dot(d_raw[here, wide:], w_kv[...], 1, 1)
            total = total + dot(d_raw_first[here, :wide], w_q_first[...], 1, 1)
            total = total + dot(d_raw_first[here, wide:], w_kv_first[...], 1, 1)
            target = sum_own if k < 2 else sum_near
            target[(k % 2) * quarter_rows : (k % 2 + 1) * quarter_rows, :] = total.astype(LOW)
    gains[:8, :] = gain_sums[0]
    gains[8:, :] = gain_sums[1]


def feed_body(n_own, n_near, c_own, c_near, w_gate, w_up, w_down, *refs):
    (inner, d_gate, d_up, n_all, c_all, d_own, d_near, y_own, y_near) = refs[-9:]
    mine = pl.program_id(0) < pl.num_programs(0) // 2
    n_rows = jnp.where(mine, n_own[...], n_near[...])
    c_rows = jnp.where(mine, c_own[...], c_near[...])
    n_all[...] = n_rows
    c_all[...] = c_rows
    gate = dot(n_rows, w_gate[...])
    up_part = dot(n_rows, w_up[...])
    d_inner = dot(c_rows, w_down[...], 1, 1)
    sigma = 1.0 / (1.0 + jnp.exp(-gate))
    held = gate * sigma
    inner[...] = (held * up_part).astype(LOW)
    d_gate[...] = (d_inner * up_part * sigma * (1.0 + gate * (1.0 - sigma))).astype(LOW)
    d_up[...] = (d_inner * held).astype(LOW)
    total = dot(d_gate[...], w_gate[...], 1, 1) + dot(d_up[...], w_up[...], 1, 1)
    product = dot(inner[...], w_down[...])

    @pl.when(mine)
    def _():
        d_own[...] = total.astype(LOW)
        y_own[...] = product.astype(LOW)

    @pl.when(jnp.logical_not(mine))
    def _():
        d_near[...] = total.astype(LOW)
        y_near[...] = product.astype(LOW)


def feed(half, kept, n_own, n_near, c_own, c_near, w_gate, w_up, w_down):
    rows, width = n_own.shape
    hidden = w_gate.shape[1]
    block = rows // 2
    steps = 4
    first = pl.BlockSpec((block, width), lambda i: (jnp.minimum(i, 1), 0))
    second = pl.BlockSpec((block, width), lambda i: (jnp.maximum(i - 2, 0), 0))
    whole = lambda values: pl.BlockSpec(values.shape, lambda i: (0, 0))
    part = lambda cols: pl.BlockSpec((block, cols), lambda i: (i + steps * half, 0))
    in_specs = [first, second, first, second] + [whole(v) for v in (w_gate, w_up, w_down)]
    outs = [
        jax.ShapeDtypeStruct((4 * rows, cols), LOW) for cols in (hidden, hidden, hidden, width, width)
    ]
    outs += [jax.ShapeDtypeStruct((rows, width), LOW)] * 4
    out_specs = [part(hidden)] * 3 + [part(width)] * 2
    out_specs += [first, second, first, second]
    aliases = {}
    if half:
        in_specs += [pl.BlockSpec(memory_space=pl.ANY)] * 5
        aliases = {7 + index: index for index in range(5)}
    work = 2 * rows * width * hidden * 2 * 6
    return pl.pallas_call(
        feed_body,
        grid=(steps,),
        in_specs=in_specs,
        out_specs=out_specs,
        out_shape=outs,
        input_output_aliases=aliases,
        compiler_params=pltpu.CompilerParams(
            vmem_limit_bytes=VMEM_BYTES, dimension_semantics=("arbitrary",)
        ),
        cost_estimate=pl.CostEstimate(
            flops=work, bytes_accessed=12 * rows * width * 4, transcendentals=0
        ),
    )(n_own, n_near, c_own, c_near, w_gate, w_up, w_down, *(kept if half else ()))


def each(count, act):
    if count <= 8:
        for index in range(count):
            act(index)
    else:
        lax.fori_loop(0, count, lambda index, carry: (act(index), carry)[1], 0)


def fetch(copies):
    for count, copy_of in copies:
        each(count, lambda index: copy_of(index).start())
    for count, copy_of in copies:
        each(count, lambda index: copy_of(index).wait())


HELD = pl.BlockSpec(memory_space=pl.ANY)


def pick_body(order, source, target, arrived):
    def copy_of(index):
        return pltpu.make_async_copy(
            source.at[order[index]], target.at[index], arrived.at[index]
        )

    fetch([(order.shape[0], copy_of)])


def pick(values, order):
    count = order.shape[0]
    return pl.pallas_call(
        pick_body,
        in_specs=[SMEM, HELD],
        out_specs=VMEM,
        out_shape=jax.ShapeDtypeStruct((count,) + values.shape[1:], values.dtype),
        scratch_shapes=[pltpu.SemaphoreType.DMA((count,))],
        compiler_params=pltpu.CompilerParams(vmem_limit_bytes=VMEM_BYTES),
    )(order, values)


def across_dp(values):
    return lax.all_to_all(values, "dp", split_axis=0, concat_axis=0, tiled=True)


def join_body(first_order, second_order, first, second, target, arrived):
    count = first_order.shape[0]

    def first_copy(index):
        return pltpu.make_async_copy(
            first.at[first_order[index]], target.at[index], arrived.at[index]
        )

    def second_copy(index):
        return pltpu.make_async_copy(
            second.at[second_order[index]], target.at[count + index], arrived.at[count + index]
        )

    fetch([(count, first_copy), (count, second_copy)])


def join(first, first_order, second, second_order):
    count = first_order.shape[0]
    return pl.pallas_call(
        join_body,
        in_specs=[SMEM, SMEM, HELD, HELD],
        out_specs=VMEM,
        out_shape=jax.ShapeDtypeStruct((2 * count,) + first.shape[1:], first.dtype),
        scratch_shapes=[pltpu.SemaphoreType.DMA((2 * count,))],
        compiler_params=pltpu.CompilerParams(vmem_limit_bytes=VMEM_BYTES),
    )(first_order, second_order, first, second)


def place_body(order, member, *refs):
    sources = refs[:4]
    target, arrived = refs[4:]
    copies = []
    for k, source in enumerate(sources):

        def copy_of(index, k=k, source=source):
            return pltpu.make_async_copy(
                source.at[order[index]],
                target.at[index, member[0] ^ RELATIVE[k]],
                arrived.at[k, index],
            )

        copies.append((order.shape[0], copy_of))
    fetch(copies)


def place_pieces(parts, order, member):
    count, part_rows, width = parts[0].shape
    pieces = pl.pallas_call(
        place_body,
        in_specs=[SMEM, SMEM] + [HELD] * 4,
        out_specs=VMEM,
        out_shape=jax.ShapeDtypeStruct((count, 4, part_rows, width), parts[0].dtype),
        scratch_shapes=[pltpu.SemaphoreType.DMA((4, count))],
        compiler_params=pltpu.CompilerParams(vmem_limit_bytes=VMEM_BYTES),
    )(order, member, *parts)
    return pieces.reshape(count * 4 * part_rows, width)


def kernel_params():
    return pltpu.CompilerParams(vmem_limit_bytes=VMEM_BYTES)


def finish_down_body(pull, ahead, gradient, weight):
    value = ahead[0].astype(FULL) - pull[0] * gradient[0].astype(FULL)
    weight[...] = value.astype(LOW)


def finish_down(pull, ahead, gradient):
    count, rows, cols = ahead.shape
    if cols % LANES:
        value = ahead.astype(FULL) - pull * gradient.astype(FULL)
        return value.astype(LOW).transpose(1, 0, 2).reshape(rows, count * cols)
    shard = pl.BlockSpec((1, rows, cols), lambda i: (i, 0, 0))
    return pl.pallas_call(
        finish_down_body,
        grid=(count,),
        in_specs=[SMEM, shard, shard],
        out_specs=pl.BlockSpec((rows, cols), lambda i: (0, i)),
        out_shape=jax.ShapeDtypeStruct((rows, count * cols), LOW),
        compiler_params=kernel_params(),
    )(pull, ahead, gradient)


def finish_small_body(pull, ahead, gradient, query, keyval, output):
    value = ahead[0].astype(FULL) - pull[0] * gradient[0].astype(FULL)
    first = query.shape[1]
    second = first + keyval.shape[1]
    query[...] = value[:, :first].astype(LOW)
    keyval[...] = value[:, first:second].astype(LOW)
    output[...] = value[:, second:].T.astype(LOW)


def finish_small(pull, ahead, gradient, first, second):
    count, rows, cols = ahead.shape
    if rows % LANES:
        value = (ahead.astype(FULL) - pull * gradient.astype(FULL)).astype(LOW)
        value = value.reshape(count * rows, cols)
        return value[:, :first], value[:, first:second], value[:, second:].T
    shard = pl.BlockSpec((1, rows, cols), lambda i: (i, 0, 0))
    shapes = [(count * rows, first), (count * rows, second - first), (cols - second, count * rows)]
    specs = [
        pl.BlockSpec((rows, first), lambda i: (i, 0)),
        pl.BlockSpec((rows, second - first), lambda i: (i, 0)),
        pl.BlockSpec((cols - second, rows), lambda i: (0, i)),
    ]
    return pl.pallas_call(
        finish_small_body,
        grid=(count,),
        in_specs=[SMEM, shard, shard],
        out_specs=specs,
        out_shape=[jax.ShapeDtypeStruct(shape, LOW) for shape in shapes],
        compiler_params=kernel_params(),
    )(pull, ahead, gradient)


def fence(*values):
    return lax.optimization_barrier(values)


def reduce_step(total, step, device):
    bit = (device // step) & 1
    split = total.reshape((total.shape[0] // 2, 2) + total.shape[1:])
    sent = lax.dynamic_index_in_dim(split, 1 - bit, 1, keepdims=False).astype(LOW)
    kept = lax.dynamic_index_in_dim(split, bit, 1, keepdims=False)
    return (kept, swap(sent, "dp", step))


def add(first, second):
    return first.astype(FULL) + second.astype(FULL)


def by_device(product, devices):
    return product.reshape((devices, product.shape[0] // devices) + product.shape[1:])


def row_norm(values, gain_row):
    inverse = lax.rsqrt(jnp.mean(values * values, axis=-1, keepdims=True) + EPSILON)
    return (values * inverse * gain_row, inverse)


def row_norm_back(gradient, values, inverse, gain_row):
    scaled = gradient * gain_row
    d_values = inverse * scaled - values * (inverse * inverse * inverse) * jnp.mean(
        scaled * values, axis=-1, keepdims=True
    )
    d_gain = jnp.sum(gradient * values * inverse, axis=0)
    return (d_values, d_gain)


def local(
    tokens,
    cotangent,
    seq_lengths,
    deal,
    w_query,
    w_keyval,
    w_output,
    w_gateup,
    w_down,
    norm_gains,
    head_gains,
    master_query,
    master_keyval,
    master_output,
    master_gateup,
    master_down,
    start_query,
    start_keyval,
    start_output,
    start_gateup,
    start_down,
    start_norms,
    start_heads,
    step_size,
):
    devices = lax.axis_size("dp")
    ways = lax.axis_size("mp")
    device = lax.axis_index("dp")
    member = lax.axis_index("mp")
    row_count, width = tokens.shape
    total_pieces = deal.shape[0]
    pieces_dev = total_pieces // devices
    piece_rows = row_count // pieces_dev
    part_rows = piece_rows // ways
    slot_count = seq_lengths.shape[0]
    slot_rows = row_count // slot_count
    slot_pieces = pieces_dev // slot_count
    quarter_rows = slot_pieces * part_rows
    half_rows = 2 * quarter_rows
    head_dim = head_gains.shape[1]
    query_cols = w_query.shape[1]
    key_cols = w_keyval.shape[2]
    heads = query_cols // LANES
    hidden = w_down.shape[0]
    step = step_size[0]
    slot = member // 2
    member_ref = member.reshape(1).astype(jnp.int32)

    placed = jnp.arange(pieces_dev, dtype=jnp.int32)
    my_places = lax.dynamic_slice_in_dim(deal, device * pieces_dev, pieces_dev)
    target = my_places // pieces_dev
    piece_to = jnp.sum((target[:, None] == placed[None, :]) * placed[:, None], axis=0)
    whole = jnp.arange(total_pieces, dtype=jnp.int32)
    held_here = deal[:, None] == (device * pieces_dev + placed)[None, :]
    source = jnp.sum(held_here * (whole // pieces_dev)[:, None], axis=0)
    place_from = jnp.sum((source[:, None] == placed[None, :]) * placed[:, None], axis=0)
    slot_source = source.reshape(slot_count, slot_pieces)
    own_source = lax.dynamic_index_in_dim(slot_source, slot, 0, keepdims=False)
    other_source = lax.dynamic_index_in_dim(slot_source, 1 - slot, 0, keepdims=False)
    in_order = jnp.arange(slot_pieces, dtype=jnp.int32)

    def deal_in(values):
        quarters = values.reshape(pieces_dev * ways, part_rows, width)
        return across_dp(pick(quarters, piece_to * ways + member))

    def rows_of(pieces):
        return pieces.reshape(-1, width)

    x_got = deal_in(tokens)

    lengths = lax.dynamic_index_in_dim(seq_lengths, slot, 0, keepdims=False)
    ends = jnp.cumsum(lengths)

    def position_of(token):
        passed = (token[:, None] >= ends[None, :]).astype(jnp.int32)
        return token - jnp.sum(passed * lengths[None, :], axis=1)

    token_row = jnp.arange(slot_rows, dtype=jnp.int32)
    start = token_row - position_of(token_row)
    quarters = jnp.asarray(RELATIVE, jnp.int32) ^ member
    relative_token = (
        (in_order * piece_rows)[None, :, None]
        + (quarters * part_rows)[:, None, None]
        + jnp.arange(part_rows, dtype=jnp.int32)[None, None, :]
    ).reshape(-1)
    lane = jnp.arange(LANES, dtype=jnp.int32)
    half = head_dim // 2
    freqs = ROPE_BASE ** (-(lane % half).astype(FULL) * (2.0 / head_dim))
    angles = position_of(relative_token).astype(FULL)[:, None] * freqs[None, :]
    cosine = jnp.cos(angles)
    sine = jnp.sin(angles) * jnp.where(lane % head_dim < half, -1.0, 1.0)[None, :]
    gain_q = jnp.tile(head_gains[0:1], (1, LANES // head_dim))
    gain_k = jnp.tile(head_gains[1:2], (1, LANES // head_dim))

    w_keyval_flat = w_keyval.reshape(width, 2 * key_cols)
    far_query, far_keyval = far(w_query), far(w_keyval_flat)
    w_gate = w_gateup[:, 0]
    w_up = w_gateup[:, 1]

    def ahead(master, begin):
        return (master - 0.5 * step * begin).astype(LOW)

    small = jnp.concatenate(
        [
            ahead(master_query, start_query),
            ahead(master_keyval, start_keyval).reshape(-1, 2 * key_cols),
            ahead(master_output, start_output).T,
        ],
        axis=1,
    )
    part_gateup = ahead(master_gateup, start_gateup)
    part_down = ahead(master_down, start_down)

    early = fence(
        (x_got, far_query, far_keyval, cosine, sine, w_gate, w_up),
        (small, part_gateup, part_down, cotangent, w_output),
    )
    x_got, far_query, far_keyval, cosine, sine, w_gate, w_up = early[0]
    small, part_gateup, part_down, cotangent, w_output = early[1]
    x_other = far(pick(x_got, other_source))
    c_got = deal_in(cotangent)
    x_other, w_output = fence(x_other, w_output)
    groups = (
        (w_query, w_keyval_flat, w_output),
        (far_query, far_keyval, far(w_output)),
    )
    x_own = rows_of(join(x_got, own_source, x_other, in_order))

    x_full = x_own.astype(FULL)
    norm_one_f, inv_one = row_norm(x_full, norm_gains[0])
    norm_own = norm_one_f.astype(LOW)
    norm_near = near(norm_own)
    stepped = fence(norm_near, c_got, small, part_gateup, part_down)
    norm_near, c_got, small, part_gateup, part_down = stepped

    dims = (slot_rows, slot_pieces, part_rows, slot_rows // 6, head_dim, heads)
    shape = jax.ShapeDtypeStruct

    def attend(last, weights, more):
        token_shape = (heads, slot_rows, LANES)
        outs = [
            shape((slot_rows, query_cols), LOW),
            shape((slot_rows, query_cols + key_cols), LOW),
            shape(token_shape, FULL),
        ] + [shape(token_shape, LOW)] * 5
        if last:
            outs += [shape((half_rows, width), LOW)] * 2
        arguments = (
            member_ref,
            norm_own,
            norm_near,
            weights[0],
            weights[1],
            cosine,
            sine,
            start.reshape(-1, 1),
            gain_q,
            gain_k,
        ) + more
        return pl.pallas_call(
            functools.partial(attend_body, last, dims),
            in_specs=[SMEM] + [VMEM] * (len(arguments) - 1),
            out_specs=[VMEM] * len(outs),
            out_shape=outs,
            scratch_shapes=[
                pltpu.VMEM((heads + 2, slot_rows, LANES), FULL),
                pltpu.VMEM((heads, slot_rows, LANES), FULL),
                pltpu.VMEM((heads, slot_rows, LANES), FULL),
            ],
            compiler_params=pltpu.CompilerParams(vmem_limit_bytes=VMEM_BYTES),
            cost_estimate=pl.CostEstimate(
                flops=12_000_000_000, bytes_accessed=12_000_000, transcendentals=0
            ),
        )(*arguments)

    def attend_back(last, weights, kept, d_own, d_near, more):
        token_shape = (heads, slot_rows, LANES)
        mixed, raw, inverse, *tables = kept
        outs = [shape((slot_rows, query_cols + 2 * key_cols), LOW), shape((16, LANES), FULL)]
        if last:
            outs += [shape((half_rows, width), LOW)] * 2
        arguments = (
            member_ref,
            d_own,
            d_near,
            weights[2],
            mixed,
            inverse,
            raw,
            cosine,
            sine,
            start.reshape(1, -1),
            gain_q,
            gain_k,
            *tables,
        ) + more
        return pl.pallas_call(
            functools.partial(attend_back_body, last, dims),
            in_specs=[SMEM] + [VMEM] * (len(arguments) - 1),
            out_specs=[VMEM] * len(outs),
            out_shape=outs,
            scratch_shapes=[
                pltpu.VMEM((2 * heads, slot_rows, LANES), FULL),
                pltpu.VMEM(token_shape, LOW),
                pltpu.VMEM(token_shape, LOW),
                pltpu.VMEM(token_shape, FULL),
                pltpu.VMEM(token_shape, FULL),
                pltpu.VMEM(token_shape, FULL),
            ],
            compiler_params=pltpu.CompilerParams(vmem_limit_bytes=VMEM_BYTES),
            cost_estimate=pl.CostEstimate(
                flops=20_000_000_000, bytes_accessed=14_000_000, transcendentals=0
            ),
        )(*arguments)

    first_kept = attend(False, groups[0], ())
    c_own_far = far(pick(c_got, other_source))
    c_other_far = far(pick(c_got, own_source))
    ahead_down = lax.all_gather(part_down, "dp", axis=0, tiled=False)
    ahead_gateup = lax.all_gather(part_gateup, "dp", axis=0, tiled=True)
    ahead_small = lax.all_gather(small, "dp", axis=0, tiled=False)
    *second_kept, attn_own, attn_near = attend(
        True, groups[1], (groups[1][2], groups[0][2], first_kept[0])
    )
    attn_got = near(attn_near)
    attn_got, attn_own, c_own_far = fence(attn_got, attn_own, c_own_far)
    c_own = rows_of(join(c_got, own_source, c_own_far, in_order))
    c_near = near(c_own)
    hidden_one = x_full + add(attn_own, attn_got)
    norm_two_f, inv_two = row_norm(hidden_one, norm_gains[1])
    two_own = norm_two_f.astype(LOW)
    two_near = near(two_own)
    two_near, two_own, c_near, c_other_far = fence(two_near, two_own, c_near, c_other_far)
    two_far = far(two_own)

    *kept, d_own, d_near, y_own, y_near = feed(
        0, (), two_own, two_near, c_own, c_near, w_gate, w_up, w_down
    )
    stepped = fence(two_far, d_own, d_near, c_other_far, y_near, ahead_down)
    two_far, d_own, d_near, c_other_far, y_near, ahead_down = stepped
    two_across = near(two_far)
    c_far = rows_of(join(c_other_far, in_order, c_got, other_source))
    c_across = near(c_far)
    d_got = near(d_near)
    y_got = near(y_near)
    *kept, far_own, far_near, far_y_own, far_y_near = feed(
        1, kept, two_far, two_across, c_far, c_across, w_gate, w_up, w_down
    )
    far_got = near(far_near)
    pair_far = add(far_own, far_got).astype(LOW)
    pair_far, kept, far_y_near = fence(pair_far, kept, far_y_near)
    inner, d_gate, d_up, two_all, c_all = kept
    pair_got = far(pair_far)
    far_y_got = near(far_y_near)
    steps = bits_of(devices)
    grad_down = dot(c_all, inner, 0, 0).astype(LOW)
    down_kept, down_got = reduce_step(by_device(grad_down, devices), steps[0], device)
    grad_gate = dot(two_all, d_gate, 0, 0).astype(LOW)
    gate_kept, gate_got = reduce_step(by_device(grad_gate, devices), steps[0], device)
    y_pair = add(y_own, y_got) + hidden_one
    far_y_pair = add(far_y_own, far_y_got)
    y_leaving = jnp.concatenate([y_pair[quarter_rows:], far_y_pair[:quarter_rows]]).astype(LOW)
    grad_up = dot(two_all, d_up, 0, 0).astype(LOW)
    up_kept, up_got = reduce_step(by_device(grad_up, devices), steps[0], device)
    pair_got, gate_kept, up_kept, y_leaving = fence(pair_got, gate_kept, up_kept, y_leaving)
    y_arrived = far(y_leaving)

    d_norm_two = add(d_own, d_got) + pair_got.astype(FULL)
    d_hidden_part, gain_two = row_norm_back(d_norm_two, hidden_one, inv_two, norm_gains[1])
    d_hidden = c_own.astype(FULL) + d_hidden_part
    dh_own = d_hidden.astype(LOW)
    dh_near = near(dh_own)

    def over_rows(own, other, values):
        return dot(own, values[:half_rows], 0, 0) + dot(other, values[half_rows:], 0, 0)

    d_raw_far, gains_far = attend_back(False, groups[1], second_kept, dh_own, dh_near, ())
    d_raw_far, down_got, y_arrived = fence(d_raw_far, down_got, y_arrived)

    out_order = (place_from + (slot_count - slot) * slot_pieces) % pieces_dev

    def deal_out(mine, other):
        rows = jnp.concatenate([mine, other], axis=0)
        return across_dp(pick(rows.reshape(pieces_dev, part_rows, width), out_order))

    def settle(got, got_far):
        return place_pieces((got, got_far, near(got), near(got_far)), target, member_ref)

    out_got = deal_out(
        (y_pair[:quarter_rows] + y_arrived[quarter_rows:].astype(FULL)).astype(LOW),
        (far_y_pair[quarter_rows:] + y_arrived[:quarter_rows].astype(FULL)).astype(LOW),
    )
    down_kept, down_got = reduce_step(add(down_kept, down_got), steps[1], device)
    grad_output_got = far(over_rows(dh_own, dh_near, second_kept[0]).astype(LOW))
    grad_qkv_got = far(over_rows(norm_own, norm_near, d_raw_far).astype(LOW))
    grad_output_mine = over_rows(dh_own, dh_near, first_kept[0])
    d_raw_own, gains_own, d_one_own, d_one_near = attend_back(
        True,
        groups[0],
        first_kept,
        dh_own,
        dh_near,
        (groups[0][0], groups[0][1], groups[1][0], groups[1][1], d_raw_far),
    )
    stepped = fence(d_raw_own, d_one_near, down_got, gate_got, up_got, out_got, ahead_gateup)
    d_raw_own, d_one_near, down_got, gate_got, up_got, out_got, ahead_gateup = stepped

    d_one_got = near(d_one_near)
    down_kept, down_got = reduce_step(add(down_kept, down_got), steps[2], device)
    gate_kept, gate_got = reduce_step(add(gate_kept, gate_got), steps[1], device)
    d_one_got, down_kept, gate_kept = fence(d_one_got, down_kept, gate_kept)
    d_norm_one = add(d_one_own, d_one_got)
    d_input_part, gain_one = row_norm_back(d_norm_one, x_full, inv_one, norm_gains[0])
    dx_own = (d_hidden + d_input_part).astype(LOW)
    dx_other = far(dx_own[quarter_rows:])
    up_kept, up_got = reduce_step(add(up_kept, up_got), steps[1], device)
    grad_qkv_mine = over_rows(norm_own, norm_near, d_raw_own)
    grad_small = jnp.concatenate(
        [add(grad_qkv_mine, grad_qkv_got), add(grad_output_mine, grad_output_got)], axis=1
    )
    small_kept, small_got = reduce_step(by_device(grad_small, devices), steps[0], device)

    down_got, up_kept, gate_got = fence(down_got, up_kept, gate_got)
    own_down = add(down_kept, down_got)[0]
    owned_down = own_down.T
    gate_kept, gate_got = reduce_step(add(gate_kept, gate_got), steps[2], device)
    up_got, gate_kept, owned_down = fence(up_got, gate_kept, owned_down)
    up_kept, up_got = reduce_step(add(up_kept, up_got), steps[2], device)
    all_down = lax.all_gather(owned_down.astype(LOW), "dp", axis=0, tiled=False)
    small_got, up_kept = fence(small_got, up_kept)
    small_kept, small_got = reduce_step(add(small_kept, small_got), steps[1], device)
    gate_got, up_got, dx_other, dx_own, small_kept = fence(
        gate_got, up_got, dx_other, dx_own, small_kept
    )
    own_gate = add(gate_kept, gate_got)[0]
    own_up = add(up_kept, up_got)[0]
    owned_gateup = jnp.stack([own_gate, own_up], axis=1)
    all_gateup = lax.all_gather(owned_gateup.astype(LOW), "dp", axis=0, tiled=True)
    dx_got = deal_out(dx_own[:quarter_rows], dx_other)
    out_far = far(out_got)
    small_got, owned_gateup = fence(small_got, owned_gateup)
    small_kept, small_got = reduce_step(add(small_kept, small_got), steps[2], device)
    small_got, small_kept = fence(small_got, small_kept)
    own_small = add(small_kept, small_got)[0]
    all_small = lax.all_gather(own_small.astype(LOW), "dp", axis=0, tiled=False)

    owned = (own_small, own_gate, own_up, own_down)
    own_square = sum([jnp.sum(part_grad * part_grad) for part_grad in owned])
    gains = jnp.sum((gains_far + gains_own).reshape(2, 8, LANES // head_dim, head_dim), axis=(1, 2))
    packed = jnp.concatenate(
        [gain_one, gain_two, gains.reshape(-1), jnp.broadcast_to(own_square, (LANES,))]
    ).reshape(-1, LANES)
    for axis, size in (("mp", ways), ("dp", devices)):
        for bit in bits_of(size):
            packed = packed + swap(packed, axis, bit)
    flat = packed.reshape(-1)
    norm_sum = flat[: 2 * width].reshape(2, width)
    head_sum = flat[2 * width : 2 * width + 2 * head_dim].reshape(2, head_dim)
    square_sum = flat[2 * width + 2 * head_dim]
    clip_value = jnp.sqrt(square_sum + jnp.sum(norm_sum * norm_sum) + jnp.sum(head_sum * head_sum))
    limit = math.sqrt(2 * D * H * HD + 2 * D * KV * HD + 3 * D * FF + 2 * D + 2 * HD)
    factor = jnp.minimum(1.0, limit / clip_value)

    dx_far = far(dx_got)

    qkv_cols = query_cols + 2 * key_cols
    owned_parts = (
        own_small[:, :query_cols],
        own_small[:, query_cols:qkv_cols].reshape(-1, 2, key_cols),
        own_small[:, qkv_cols:].T,
        owned_gateup,
        owned_down,
    )
    starts = (start_query, start_keyval, start_output, start_gateup, start_down)
    masters = (master_query, master_keyval, master_output, master_gateup, master_down)
    moments = [0.5 * begin + factor * part_grad for begin, part_grad in zip(starts, owned_parts)]
    nexts = [held - step * moved for held, moved in zip(masters, moments)]
    moment_norms = 0.5 * start_norms + factor * norm_sum
    moment_heads = 0.5 * start_heads + factor * head_sum
    next_norms = norm_gains - step * moment_norms
    next_heads = head_gains - step * moment_heads

    pull = (step * factor).reshape(1)
    output = settle(out_got, out_far)
    input_grad = settle(dx_got, dx_far)
    done_query, done_keyval, done_output = finish_small(
        pull, ahead_small, all_small, query_cols, qkv_cols
    )
    done_gateup = ahead_gateup.astype(FULL) - pull[0] * all_gateup.astype(FULL)
    weights = (
        done_query,
        done_keyval.reshape(width, 2, key_cols),
        done_output,
        done_gateup.astype(LOW),
        finish_down(pull, ahead_down, all_down),
    )
    return (
        output,
        input_grad,
        clip_value.reshape(1),
        *moments,
        moment_norms,
        moment_heads,
        *nexts,
        next_norms,
        next_heads,
        *weights,
    )


def solution(mesh):
    in_specs = (
        P("dp", None),
        P("dp", None),
        P("dp", None),
        P(),
        P(None, "mp"),
        P(None, None, "mp"),
        P("mp", None),
        P(None, None, "mp"),
        P("mp", None),
        P(),
        P(),
        P("dp", "mp"),
        P("dp", None, "mp"),
        P("mp", "dp"),
        P("dp", None, "mp"),
        P("mp", "dp"),
        P("dp", "mp"),
        P("dp", None, "mp"),
        P("mp", "dp"),
        P("dp", None, "mp"),
        P("mp", "dp"),
        P(),
        P(),
        P(),
    )
    out_specs = (
        P("dp", None),
        P("dp", None),
        P(),
        P("dp", "mp"),
        P("dp", None, "mp"),
        P("mp", "dp"),
        P("dp", None, "mp"),
        P("mp", "dp"),
        P(),
        P(),
        P("dp", "mp"),
        P("dp", None, "mp"),
        P("mp", "dp"),
        P("dp", None, "mp"),
        P("mp", "dp"),
        P(),
        P(),
        P(None, "mp"),
        P(None, None, "mp"),
        P("mp", None),
        P(None, None, "mp"),
        P("mp", None),
    )
    return jax.shard_map(local, mesh=mesh, in_specs=in_specs, out_specs=out_specs, check_vma=False)
```

```python
import functools
import math

import jax
import jax.numpy as jnp
from jax import lax
from jax.experimental import pallas as pl
from jax.experimental.layout import Layout, with_layout_constraint
from jax.experimental.pallas import tpu as pltpu
from jax.sharding import PartitionSpec as P

D = 1024
H = 16
KV = 8
HD = 64
FF = 4608


EPSILON = 1e-05
ROPE_BASE = 1000000.0
LOW = jnp.bfloat16
FULL = jnp.float32
LANES = 128


def dot(left, right, left_dim=1, right_dim=0):
    return lax.dot_general(
        left, right, (((left_dim,), (right_dim,)), ((), ())), preferred_element_type=FULL
    )


def swap(values, axis, bit):
    size = lax.axis_size(axis)
    return lax.ppermute(values, axis, [(place, place ^ bit) for place in range(size)])


def row_major(values):
    return with_layout_constraint(values, Layout(tuple(range(values.ndim))))


def far(values):
    return swap(values, "mp", 2)


def near(values):
    return swap(values, "mp", 1)


def bits_of(count):
    return [1 << place for place in range(count.bit_length() - 1)]


RELATIVE = (0, 2, 1, 3)
VMEM = pl.BlockSpec(memory_space=pltpu.VMEM)
SMEM = pl.BlockSpec(memory_space=pltpu.SMEM)
VMEM_BYTES = 60 * 1024 * 1024


def group_sums(values, ones):
    high = values.astype(LOW)
    rest = (values - high.astype(FULL)).astype(LOW)
    return dot(high, ones) + dot(rest, ones)


def head_ones(head_dim):
    row = lax.broadcasted_iota(jnp.int32, (LANES, LANES), 0) // head_dim
    col = lax.broadcasted_iota(jnp.int32, (LANES, LANES), 1) // head_dim
    return (row == col).astype(FULL).astype(LOW)


def turn_halves(values, half):
    lane = lax.broadcasted_iota(jnp.int32, values.shape, 1)
    ahead = pltpu.roll(values, LANES - half, 1)
    behind = pltpu.roll(values, half, 1)
    return jnp.where(lane % (2 * half) < half, ahead, behind)


def attend_body(last, dims, *refs):
    rows, pieces, part, block, head_dim, heads = dims
    (member, n_own, n_near, w_q, w_kv, cos, sin, start, gain_q, gain_k) = refs[:10]
    refs = refs[10:]
    if last:
        (w_o, w_o_first, mixed_first) = refs[:3]
        refs = refs[3:]
    (mixed, raw, inverse, q_pair, k_lo, k_hi, v_lo, v_hi) = refs[:8]
    refs = refs[8:]
    if last:
        (sum_own, sum_near) = refs[:2]
        refs = refs[2:]
    (by_token, a_token, r_token) = refs
    quarter_rows = pieces * part
    piece = 4 * part
    ones = head_ones(head_dim)

    def place(k, p):
        quarter = member[0] ^ RELATIVE[k]
        return pl.multiple_of(p * piece + quarter * part, 8)

    for k in range(4):
        here = pl.ds(k * quarter_rows, quarter_rows)
        source = n_own if k < 2 else n_near
        n_rows = source[(k % 2) * quarter_rows : (k % 2 + 1) * quarter_rows, :]
        query = dot(n_rows, w_q[...])
        keyval = dot(n_rows, w_kv[...])
        raw[here, : heads * LANES] = query.astype(LOW)
        raw[here, heads * LANES :] = keyval[:, :LANES].astype(LOW)
        parts = [query[:, h * LANES : (h + 1) * LANES] for h in range(heads)]
        parts.append(keyval[:, :LANES])
        turned = []
        for index, values in enumerate(parts):
            gain = gain_k if index == heads else gain_q
            mean = group_sums(values * values, ones) * (1.0 / head_dim)
            normed = values * lax.rsqrt(mean + EPSILON) * gain[...]
            turned.append(
                normed * cos[here, :] + turn_halves(normed, head_dim // 2) * sin[here, :]
            )
        turned.append(keyval[:, LANES:])
        for p in range(pieces):
            there = pl.ds(place(k, p), part)
            for index, values in enumerate(turned):
                by_token[index, there, :] = values[p * part : (p + 1) * part, :]

    scale = head_dim ** (-0.5)

    def prepare(i, carry):
        there = pl.ds(pl.multiple_of(i * block, block), block)
        low = lax.broadcasted_iota(jnp.int32, (block, LANES), 1) < head_dim
        for h in range(heads):
            q_pair[h, there, :] = (by_token[h, there, :] * scale).astype(LOW)
        key = by_token[heads, there, :]
        value = by_token[heads + 1, there, :]
        key_low = jnp.where(low, key, 0.0)
        key_high = jnp.where(low, 0.0, key)
        value_low = jnp.where(low, value, 1.0)
        value_high = jnp.where(low, 1.0, value)
        k_lo[0, there, :] = key_low.astype(LOW)
        k_hi[0, there, :] = pltpu.roll(key_low, head_dim, 1).astype(LOW)
        k_lo[1, there, :] = pltpu.roll(key_high, head_dim, 1).astype(LOW)
        k_hi[1, there, :] = key_high.astype(LOW)
        v_lo[0, there, :] = value_low.astype(LOW)
        v_hi[0, there, :] = pltpu.roll(value_low, head_dim, 1).astype(LOW)
        v_lo[1, there, :] = pltpu.roll(value_high, head_dim, 1).astype(LOW)
        v_hi[1, there, :] = value_high.astype(LOW)
        return carry

    lax.fori_loop(0, rows // block, prepare, 0)

    def one_head(h, carry):
        for i in range(rows // block):
            here = pl.ds(i * block, block)
            end = (i + 1) * block
            query = q_pair[h, here, :]
            key_row = lax.broadcasted_iota(jnp.int32, (block, end), 1)
            query_row = lax.broadcasted_iota(jnp.int32, (block, end), 0) + i * block
            seen = (key_row <= query_row) & (key_row >= start[here, :])
            mixed_parts = []
            for keys, values in ((k_lo, v_lo), (k_hi, v_hi)):
                scores = dot(query, keys[h, :end, :], 1, 1)
                weight = jnp.where(seen, jnp.exp(scores), 0.0).astype(LOW)
                mixed_parts.append(dot(weight, values[h, :end, :]))
            even, odd = mixed_parts
            low = lax.broadcasted_iota(jnp.int32, (block, LANES), 1) < head_dim
            divided = 1.0 / pltpu.roll(jnp.where(low, odd, even), head_dim, 1)
            a_token[h, here, :] = jnp.where(low, even, odd) * divided
            r_token[h, here, :] = divided
        return carry

    lax.fori_loop(0, heads, one_head, 0)

    for k in range(4):
        here = pl.ds(k * quarter_rows, quarter_rows)
        for h in range(heads):
            pieces_a = [a_token[h, pl.ds(place(k, p), part), :] for p in range(pieces)]
            pieces_r = [r_token[h, pl.ds(place(k, p), part), :] for p in range(pieces)]
            mixed[here, h * LANES : (h + 1) * LANES] = jnp.concatenate(pieces_a, axis=0).astype(LOW)
            inverse[h, here, :] = jnp.concatenate(pieces_r, axis=0)
        if last:
            total = dot(mixed[here, :], w_o[...]) + dot(mixed_first[here, :], w_o_first[...])
            target = sum_own if k < 2 else sum_near
            target[(k % 2) * quarter_rows : (k % 2 + 1) * quarter_rows, :] = total.astype(LOW)


def attend_back_body(last, dims, *refs):
    rows, pieces, part, block, head_dim, heads = dims
    (member, d_own, d_near, w_o, mixed, inverse, raw, cos, sin, start, gain_q, gain_k) = refs[:12]
    (q_pair, k_lo, k_hi, v_lo, v_hi) = refs[12:17]
    refs = refs[17:]
    if last:
        (w_q, w_kv, w_q_first, w_kv_first, d_raw_first) = refs[:5]
        refs = refs[5:]
    (d_raw, gains) = refs[:2]
    refs = refs[2:]
    if last:
        (sum_own, sum_near) = refs[:2]
        refs = refs[2:]
    (grad_token, grad_even, grad_odd, dq_token, dk_token, dv_token) = refs
    quarter_rows = pieces * part
    piece = 4 * part
    ones = head_ones(head_dim)
    scale = head_dim ** (-0.5)

    def place(k, p):
        quarter = member[0] ^ RELATIVE[k]
        return pl.multiple_of(p * piece + quarter * part, 8)

    for k in range(4):
        here = pl.ds(k * quarter_rows, quarter_rows)
        source = d_own if k < 2 else d_near
        d_rows = source[(k % 2) * quarter_rows : (k % 2 + 1) * quarter_rows, :]
        d_mixed = dot(d_rows, w_o[...], 1, 1)
        lane = lax.broadcasted_iota(jnp.int32, (quarter_rows, LANES), 1)
        low = lane < head_dim
        for h in range(heads):
            cols = slice(h * LANES, (h + 1) * LANES)
            grad = d_mixed[:, cols] * inverse[h, here, :]
            delta = group_sums(grad * mixed[here, cols].astype(FULL), ones)
            other = -pltpu.roll(delta, head_dim, 1)
            high = other.astype(LOW).astype(FULL)
            extra = jnp.where(lane % head_dim == 0, high, 0.0)
            extra = jnp.where(lane % head_dim == 1, other - high, extra)
            even = jnp.where(low, grad, extra)
            odd = jnp.where(low, extra, grad)
            for p in range(pieces):
                there = pl.ds(place(k, p), part)
                grad_token[2 * h, there, :] = even[p * part : (p + 1) * part, :]
                grad_token[2 * h + 1, there, :] = odd[p * part : (p + 1) * part, :]

    def prepare(i, carry):
        there = pl.ds(pl.multiple_of(i * block, block), block)
        for h in range(heads):
            grad_even[h, there, :] = grad_token[2 * h, there, :].astype(LOW)
            grad_odd[h, there, :] = grad_token[2 * h + 1, there, :].astype(LOW)
            dq_token[h, there, :] = jnp.zeros((block, LANES), FULL)
        return carry

    lax.fori_loop(0, rows // block, prepare, 0)

    def one_head(h, carry):
        for i in range(rows // block):
            first = i * block
            count = rows - first
            here = pl.ds(first, block)
            after = pl.ds(first, count)
            query = q_pair[h, after, :]
            key_row = lax.broadcasted_iota(jnp.int32, (block, count), 0)
            query_row = lax.broadcasted_iota(jnp.int32, (block, count), 1)
            seen = (key_row <= query_row) & (key_row + first >= start[:, after])
            d_keys = []
            d_values = []
            d_query = None
            for keys, values, grads in ((k_lo, v_lo, grad_even), (k_hi, v_hi, grad_odd)):
                key = keys[h, here, :]
                grad = grads[h, after, :]
                weight = jnp.where(seen, jnp.exp(dot(key, query, 1, 1)), 0.0)
                d_scores = (weight * dot(values[h, here, :], grad, 1, 1)).astype(LOW)
                d_values.append(dot(weight.astype(LOW), grad))
                d_keys.append(dot(d_scores, query))
                moved = dot(d_scores, key, 0, 0)
                d_query = moved if d_query is None else d_query + moved
            dq_token[h, after, :] += d_query
            low = lax.broadcasted_iota(jnp.int32, (block, LANES), 1) < head_dim
            for (even, odd), kept in ((d_keys, dk_token), (d_values, dv_token)):
                kept[h, here, :] = even + pltpu.roll(odd, head_dim, 1)
        return carry

    lax.fori_loop(0, heads, one_head, 0)

    gain_sums = [jnp.zeros((8, LANES), FULL), jnp.zeros((8, LANES), FULL)]
    for k in range(4):
        here = pl.ds(k * quarter_rows, quarter_rows)
        low = lax.broadcasted_iota(jnp.int32, (quarter_rows, LANES), 1) < head_dim

        def rows_of(token, h):
            return jnp.concatenate(
                [token[h, pl.ds(place(k, p), part), :] for p in range(pieces)], axis=0
            )

        def pair_of(token):
            return jnp.where(
                low, rows_of(token, 0), pltpu.roll(rows_of(token, 1), head_dim, 1)
            )

        turned = [rows_of(dq_token, h) * scale for h in range(heads)] + [pair_of(dk_token)]
        for index, values in enumerate(turned):
            is_key = index == heads
            gain = gain_k if is_key else gain_q
            cols = slice(index * LANES, (index + 1) * LANES)
            held = raw[here, cols].astype(FULL)
            root = lax.rsqrt(group_sums(held * held, ones) * (1.0 / head_dim) + EPSILON)
            normed = held * root
            back = values * cos[here, :] - turn_halves(values, head_dim // 2) * sin[here, :]
            scaled = back * gain[...]
            mean = group_sums(scaled * normed, ones) * (1.0 / head_dim)
            d_raw[here, cols] = (root * (scaled - normed * mean)).astype(LOW)
            products = (back * normed).reshape(quarter_rows // 8, 8, LANES)
            gain_sums[int(is_key)] = gain_sums[int(is_key)] + jnp.sum(products, axis=0)
        d_raw[here, (heads + 1) * LANES :] = pair_of(dv_token).astype(LOW)
        if last:
            wide = heads * LANES
            total = dot(d_raw[here, :wide], w_q[...], 1, 1)
            total = total + dot(d_raw[here, wide:], w_kv[...], 1, 1)
            total = total + dot(d_raw_first[here, :wide], w_q_first[...], 1, 1)
            total = total + dot(d_raw_first[here, wide:], w_kv_first[...], 1, 1)
            target = sum_own if k < 2 else sum_near
            target[(k % 2) * quarter_rows : (k % 2 + 1) * quarter_rows, :] = total.astype(LOW)
    gains[:8, :] = gain_sums[0]
    gains[8:, :] = gain_sums[1]


def feed_body(n_own, n_near, c_own, c_near, w_gate, w_up, w_down, *refs):
    (inner, d_both, n_all, c_all, d_own, d_near, y_own, y_near) = refs[-8:]
    hidden = w_gate.shape[1]
    mine = pl.program_id(0) < pl.num_programs(0) // 2
    n_rows = jnp.where(mine, n_own[...], n_near[...])
    c_rows = jnp.where(mine, c_own[...], c_near[...])
    n_all[...] = n_rows
    c_all[...] = c_rows
    gate = dot(n_rows, w_gate[...])
    up_part = dot(n_rows, w_up[...])
    d_inner = dot(c_rows, w_down[...], 1, 1)
    sigma = 1.0 / (1.0 + jnp.exp(-gate))
    held = gate * sigma
    inner[...] = (held * up_part).astype(LOW)
    d_both[:, :hidden] = (d_inner * up_part * sigma * (1.0 + gate * (1.0 - sigma))).astype(LOW)
    d_both[:, hidden:] = (d_inner * held).astype(LOW)
    total = dot(d_both[:, :hidden], w_gate[...], 1, 1)
    total = total + dot(d_both[:, hidden:], w_up[...], 1, 1)
    product = dot(inner[...], w_down[...])

    @pl.when(mine)
    def _():
        d_own[...] = total.astype(LOW)
        y_own[...] = product.astype(LOW)

    @pl.when(jnp.logical_not(mine))
    def _():
        d_near[...] = total.astype(LOW)
        y_near[...] = product.astype(LOW)


def feed(half, kept, n_own, n_near, c_own, c_near, w_gate, w_up, w_down):
    rows, width = n_own.shape
    hidden = w_gate.shape[1]
    block = rows // 2
    steps = 4
    first = pl.BlockSpec((block, width), lambda i: (jnp.minimum(i, 1), 0))
    second = pl.BlockSpec((block, width), lambda i: (jnp.maximum(i - 2, 0), 0))
    whole = lambda values: pl.BlockSpec(values.shape, lambda i: (0, 0))
    part = lambda cols: pl.BlockSpec((block, cols), lambda i: (i + steps * half, 0))
    in_specs = [first, second, first, second] + [whole(v) for v in (w_gate, w_up, w_down)]
    outs = [
        jax.ShapeDtypeStruct((4 * rows, cols), LOW) for cols in (hidden, 2 * hidden, width, width)
    ]
    outs += [jax.ShapeDtypeStruct((rows, width), LOW)] * 4
    out_specs = [part(hidden), part(2 * hidden)] + [part(width)] * 2
    out_specs += [first, second, first, second]
    aliases = {}
    if half:
        in_specs += [pl.BlockSpec(memory_space=pl.ANY)] * 4
        aliases = {7 + index: index for index in range(4)}
    work = 2 * rows * width * hidden * 2 * 6
    return pl.pallas_call(
        feed_body,
        grid=(steps,),
        in_specs=in_specs,
        out_specs=out_specs,
        out_shape=outs,
        input_output_aliases=aliases,
        compiler_params=pltpu.CompilerParams(
            vmem_limit_bytes=VMEM_BYTES, dimension_semantics=("arbitrary",)
        ),
        cost_estimate=pl.CostEstimate(
            flops=work, bytes_accessed=12 * rows * width * 4, transcendentals=0
        ),
    )(n_own, n_near, c_own, c_near, w_gate, w_up, w_down, *(kept if half else ()))


def each(count, act):
    if count <= 8:
        for index in range(count):
            act(index)
    else:
        lax.fori_loop(0, count, lambda index, carry: (act(index), carry)[1], 0)


def fetch(copies):
    for count, copy_of in copies:
        each(count, lambda index: copy_of(index).start())
    for count, copy_of in copies:
        each(count, lambda index: copy_of(index).wait())


HELD = pl.BlockSpec(memory_space=pl.ANY)


def pick_body(order, source, target, arrived):
    def copy_of(index):
        return pltpu.make_async_copy(
            source.at[order[index]], target.at[index], arrived.at[index]
        )

    fetch([(order.shape[0], copy_of)])


def pick(values, order):
    count = order.shape[0]
    return pl.pallas_call(
        pick_body,
        in_specs=[SMEM, HELD],
        out_specs=VMEM,
        out_shape=jax.ShapeDtypeStruct((count,) + values.shape[1:], values.dtype),
        scratch_shapes=[pltpu.SemaphoreType.DMA((count,))],
        compiler_params=pltpu.CompilerParams(vmem_limit_bytes=VMEM_BYTES),
    )(order, values)


def across_dp(values):
    return lax.all_to_all(values, "dp", split_axis=0, concat_axis=0, tiled=True)


def join_body(first_order, second_order, first, second, target, arrived):
    count = first_order.shape[0]

    def first_copy(index):
        return pltpu.make_async_copy(
            first.at[first_order[index]], target.at[index], arrived.at[index]
        )

    def second_copy(index):
        return pltpu.make_async_copy(
            second.at[second_order[index]], target.at[count + index], arrived.at[count + index]
        )

    fetch([(count, first_copy), (count, second_copy)])


def join(first, first_order, second, second_order):
    count = first_order.shape[0]
    return pl.pallas_call(
        join_body,
        in_specs=[SMEM, SMEM, HELD, HELD],
        out_specs=VMEM,
        out_shape=jax.ShapeDtypeStruct((2 * count,) + first.shape[1:], first.dtype),
        scratch_shapes=[pltpu.SemaphoreType.DMA((2 * count,))],
        compiler_params=pltpu.CompilerParams(vmem_limit_bytes=VMEM_BYTES),
    )(first_order, second_order, first, second)


def place_body(order, member, *refs):
    sources = refs[:4]
    target, arrived = refs[4:]
    copies = []
    for k, source in enumerate(sources):

        def copy_of(index, k=k, source=source):
            return pltpu.make_async_copy(
                source.at[order[index]],
                target.at[index, member[0] ^ RELATIVE[k]],
                arrived.at[k, index],
            )

        copies.append((order.shape[0], copy_of))
    fetch(copies)


def place_pieces(parts, order, member):
    count, part_rows, width = parts[0].shape
    pieces = pl.pallas_call(
        place_body,
        in_specs=[SMEM, SMEM] + [HELD] * 4,
        out_specs=VMEM,
        out_shape=jax.ShapeDtypeStruct((count, 4, part_rows, width), parts[0].dtype),
        scratch_shapes=[pltpu.SemaphoreType.DMA((4, count))],
        compiler_params=pltpu.CompilerParams(vmem_limit_bytes=VMEM_BYTES),
    )(order, member, *parts)
    return pieces.reshape(count * 4 * part_rows, width)


def finish_down_body(device, pull, ahead, held, more, weight, gradient, arrived):
    apart = places_apart(ahead.shape[0])
    copies = placing(apart, device, held, more, gradient, arrived)
    fetch(copies)
    cols = ahead.shape[2]
    for index in range(ahead.shape[0]):
        value = ahead[index].astype(FULL) - pull[0] * gradient[index].astype(FULL)
        weight[:, index * cols : (index + 1) * cols] = value.astype(LOW)


def finish_small_body(device, pull, ahead, held, more, query, keyval, output, gradient, arrived):
    apart = places_apart(ahead.shape[0])
    fetch(placing(apart, device, held, more, gradient, arrived))
    rows = ahead.shape[1]
    first = query.shape[1]
    second = first + keyval.shape[1]
    for index in range(ahead.shape[0]):
        value = ahead[index].astype(FULL) - pull[0] * gradient[index].astype(FULL)
        here = slice(index * rows, (index + 1) * rows)
        query[here, :] = value[:, :first].astype(LOW)
        keyval[here, :] = value[:, first:second].astype(LOW)
        output[:, here] = value[:, second:].T.astype(LOW)


def places_apart(count):
    apart = [0]
    for step in reversed(bits_of(count)):
        apart = apart + [other + step for other in apart]
    return apart


def placing(apart, device, held, more, target, arrived):
    half = len(apart) // 2
    copies = []
    for index, distance in enumerate(apart):
        source = held.at[index] if index < half else more.at[index - half]

        def copy_of(_, index=index, distance=distance, source=source):
            return pltpu.make_async_copy(
                source, target.at[device[0] ^ distance], arrived.at[index]
            )

        copies.append((1, copy_of))
    return copies


def place_shards_body(device, *refs):
    *sources, target, arrived = refs
    apart = places_apart(target.shape[0])
    half = len(apart) // 2
    rows = sources[0].shape[1]
    copies = []
    for chunk in range(len(sources) // 2):
        held, more = sources[2 * chunk : 2 * chunk + 2]
        for index, distance in enumerate(apart):
            source = held.at[index] if index < half else more.at[index - half]

            def copy_of(_, index=index, distance=distance, source=source, chunk=chunk):
                there = target.at[device[0] ^ distance, pl.ds(chunk * rows, rows)]
                return pltpu.make_async_copy(source, there, arrived.at[chunk, index])

            copies.append((1, copy_of))
    fetch(copies)


def kernel_params():
    return pltpu.CompilerParams(vmem_limit_bytes=VMEM_BYTES)


def place_shards(device, devices, *chunks):
    shape = (devices, len(chunks) * chunks[0][0].shape[1]) + chunks[0][0].shape[2:]
    sources = [part for chunk in chunks for part in chunk]
    return pl.pallas_call(
        place_shards_body,
        in_specs=[SMEM] + [HELD] * len(sources),
        out_specs=VMEM,
        out_shape=jax.ShapeDtypeStruct(shape, LOW),
        scratch_shapes=[pltpu.SemaphoreType.DMA((len(chunks), devices))],
        compiler_params=kernel_params(),
    )(device, *sources)


def finish_down(device, pull, ahead, held, more):
    count, rows, cols = ahead.shape
    if cols % LANES:
        gradient = place_shards(device, count, (held, more))
        value = ahead.astype(FULL) - pull * gradient.astype(FULL)
        return value.astype(LOW).transpose(1, 0, 2).reshape(rows, count * cols)
    return pl.pallas_call(
        finish_down_body,
        in_specs=[SMEM, SMEM, VMEM, HELD, HELD],
        out_specs=VMEM,
        out_shape=jax.ShapeDtypeStruct((rows, count * cols), LOW),
        scratch_shapes=[pltpu.VMEM(ahead.shape, LOW), pltpu.SemaphoreType.DMA((count,))],
        compiler_params=kernel_params(),
    )(device, pull, ahead, held, more)


def finish_small(device, pull, ahead, held, more, first, second):
    count, rows, cols = ahead.shape
    if rows % LANES:
        gradient = place_shards(device, count, (held, more))
        value = (ahead.astype(FULL) - pull * gradient.astype(FULL)).astype(LOW)
        value = value.reshape(count * rows, cols)
        return value[:, :first], value[:, first:second], value[:, second:].T
    shapes = [
        (count * rows, first),
        (count * rows, second - first),
        (cols - second, count * rows),
    ]
    return pl.pallas_call(
        finish_small_body,
        in_specs=[SMEM, SMEM, VMEM, HELD, HELD],
        out_specs=[VMEM] * 3,
        out_shape=[jax.ShapeDtypeStruct(shape, LOW) for shape in shapes],
        scratch_shapes=[pltpu.VMEM(ahead.shape, LOW), pltpu.SemaphoreType.DMA((count,))],
        compiler_params=kernel_params(),
    )(device, pull, ahead, held, more)


def fence(*values):
    return lax.optimization_barrier(values)


def add(first, second):
    return first.astype(FULL) + second.astype(FULL)


def halve_body(pairs, bit, kept, got, leaving, staying):
    for index, (base, stride) in enumerate(pairs):
        there = base + bit[0] * stride
        total = kept[there].astype(FULL) + got[there].astype(FULL)
        staying[index] = total
        there = base + (1 - bit[0]) * stride
        total = kept[there].astype(FULL) + got[there].astype(FULL)
        leaving[index] = total.astype(LOW)


def pairs_of(count, stride):
    return [(index, stride) for index in range(count) if not (index // stride) % 2]


class Halving:
    def __init__(self, product, device, devices, order):
        rows = product.shape[0] // devices
        self.device = device
        self.left = list(reversed(range(len(bits_of(devices)))))
        self.order = list(order)
        place, bit, stride = self.next()
        split = product.reshape((-1, 2, stride, rows) + product.shape[1:])
        shape = (devices // 2, rows) + product.shape[1:]
        leaving = lax.dynamic_index_in_dim(split, 1 - bit, 1, keepdims=False).reshape(shape)
        self.kept = lax.dynamic_index_in_dim(split, bit, 1, keepdims=False).reshape(shape)
        self.got = swap(leaving.astype(LOW), "dp", 1 << place)

    def next(self):
        place = self.order.pop(0)
        stride = 1 << (len(self.left) - 1 - self.left.index(place))
        self.left.remove(place)
        return place, (self.device >> place) & 1, stride

    def go(self):
        place, bit, stride = self.next()
        count = self.kept.shape[0]
        shape = (count // 2,) + self.kept.shape[1:]
        leaving, self.kept = pl.pallas_call(
            functools.partial(halve_body, pairs_of(count, stride)),
            in_specs=[SMEM, VMEM, VMEM],
            out_specs=[VMEM, VMEM],
            out_shape=[jax.ShapeDtypeStruct(shape, LOW), jax.ShapeDtypeStruct(shape, FULL)],
            compiler_params=kernel_params(),
        )(bit.reshape(1).astype(jnp.int32), self.kept, self.got)
        self.got = swap(leaving, "dp", 1 << place)

    def own(self):
        while self.order:
            self.go()
        return add(self.kept, self.got)[0]


def small_body(pairs, size, bit, *refs):
    (first, first_got, second, second_got, leaving, staying) = refs
    wide = first.shape[1]
    for index, (base, stride) in enumerate(pairs):
        for target, side in ((leaving, 1 - bit[0]), (staying, bit[0])):
            rows = pl.ds(pl.multiple_of((base + side * stride) * size, size), size)
            total = first[rows, :].astype(FULL) + first_got[rows, :].astype(FULL)
            target[index, :, :wide] = total.astype(target.dtype)
            total = second[rows, :].astype(FULL) + second_got[rows, :].astype(FULL)
            target[index, :, wide:] = total.astype(target.dtype)


def small_halving(parts, device, devices, order):
    self = Halving.__new__(Halving)
    self.device = device
    self.left = list(reversed(range(len(bits_of(devices)))))
    self.order = list(order)
    place, bit, stride = self.next()
    size = parts[0].shape[0] // devices
    shape = (devices // 2, size, parts[0].shape[1] + parts[2].shape[1])
    leaving, self.kept = pl.pallas_call(
        functools.partial(small_body, pairs_of(devices, stride), size),
        in_specs=[SMEM] + [VMEM] * 4,
        out_specs=[VMEM, VMEM],
        out_shape=[jax.ShapeDtypeStruct(shape, LOW), jax.ShapeDtypeStruct(shape, FULL)],
        compiler_params=kernel_params(),
    )(bit.reshape(1).astype(jnp.int32), *parts)
    self.got = swap(leaving, "dp", 1 << place)
    return self


def row_norm(values, gain_row):
    inverse = lax.rsqrt(jnp.mean(values * values, axis=-1, keepdims=True) + EPSILON)
    return (values * inverse * gain_row, inverse)


def row_norm_back(gradient, values, inverse, gain_row):
    scaled = gradient * gain_row
    d_values = inverse * scaled - values * (inverse * inverse * inverse) * jnp.mean(
        scaled * values, axis=-1, keepdims=True
    )
    d_gain = jnp.sum(gradient * values * inverse, axis=0)
    return (d_values, d_gain)


def local(
    tokens,
    cotangent,
    seq_lengths,
    deal,
    w_query,
    w_keyval,
    w_output,
    w_gateup,
    w_down,
    norm_gains,
    head_gains,
    master_query,
    master_keyval,
    master_output,
    master_gateup,
    master_down,
    start_query,
    start_keyval,
    start_output,
    start_gateup,
    start_down,
    start_norms,
    start_heads,
    step_size,
):
    devices = lax.axis_size("dp")
    ways = lax.axis_size("mp")
    device = lax.axis_index("dp")
    member = lax.axis_index("mp")
    row_count, width = tokens.shape
    total_pieces = deal.shape[0]
    pieces_dev = total_pieces // devices
    piece_rows = row_count // pieces_dev
    part_rows = piece_rows // ways
    slot_count = seq_lengths.shape[0]
    slot_rows = row_count // slot_count
    slot_pieces = pieces_dev // slot_count
    quarter_rows = slot_pieces * part_rows
    half_rows = 2 * quarter_rows
    head_dim = head_gains.shape[1]
    query_cols = w_query.shape[1]
    key_cols = w_keyval.shape[2]
    heads = query_cols // LANES
    hidden = w_down.shape[0]
    step = step_size[0]
    slot = member // 2
    member_ref = member.reshape(1).astype(jnp.int32)

    placed = jnp.arange(pieces_dev, dtype=jnp.int32)
    my_places = lax.dynamic_slice_in_dim(deal, device * pieces_dev, pieces_dev)
    target = my_places // pieces_dev
    piece_to = jnp.sum((target[:, None] == placed[None, :]) * placed[:, None], axis=0)
    whole = jnp.arange(total_pieces, dtype=jnp.int32)
    held_here = deal[:, None] == (device * pieces_dev + placed)[None, :]
    source = jnp.sum(held_here * (whole // pieces_dev)[:, None], axis=0)
    place_from = jnp.sum((source[:, None] == placed[None, :]) * placed[:, None], axis=0)
    slot_source = source.reshape(slot_count, slot_pieces)
    own_source = lax.dynamic_index_in_dim(slot_source, slot, 0, keepdims=False)
    other_source = lax.dynamic_index_in_dim(slot_source, 1 - slot, 0, keepdims=False)
    in_order = jnp.arange(slot_pieces, dtype=jnp.int32)

    def deal_in(values):
        quarters = values.reshape(pieces_dev * ways, part_rows, width)
        return across_dp(pick(quarters, piece_to * ways + member))

    def rows_of(pieces):
        return pieces.reshape(-1, width)

    x_got = deal_in(tokens)

    lengths = lax.dynamic_index_in_dim(seq_lengths, slot, 0, keepdims=False)
    ends = jnp.cumsum(lengths)

    def position_of(token):
        passed = (token[:, None] >= ends[None, :]).astype(jnp.int32)
        return token - jnp.sum(passed * lengths[None, :], axis=1)

    token_row = jnp.arange(slot_rows, dtype=jnp.int32)
    start = token_row - position_of(token_row)
    quarters = jnp.asarray(RELATIVE, jnp.int32) ^ member
    relative_token = (
        (in_order * piece_rows)[None, :, None]
        + (quarters * part_rows)[:, None, None]
        + jnp.arange(part_rows, dtype=jnp.int32)[None, None, :]
    ).reshape(-1)
    lane = jnp.arange(LANES, dtype=jnp.int32)
    half = head_dim // 2
    freqs = ROPE_BASE ** (-(lane % half).astype(FULL) * (2.0 / head_dim))
    angles = position_of(relative_token).astype(FULL)[:, None] * freqs[None, :]
    cosine = jnp.cos(angles)
    sine = jnp.sin(angles) * jnp.where(lane % head_dim < half, -1.0, 1.0)[None, :]
    gain_q = jnp.tile(head_gains[0:1], (1, LANES // head_dim))
    gain_k = jnp.tile(head_gains[1:2], (1, LANES // head_dim))

    w_keyval_flat = w_keyval.reshape(width, 2 * key_cols)
    far_query, far_keyval = far(w_query), far(w_keyval_flat)
    w_gate = w_gateup[:, 0]
    w_up = w_gateup[:, 1]

    masters = (master_query, master_keyval, master_output, master_gateup, master_down)
    starts = (start_query, start_keyval, start_output, start_gateup, start_down)
    early = fence(
        (x_got, far_query, far_keyval, cosine, sine, w_gate, w_up), cotangent, w_output, masters
    )
    (x_got, far_query, far_keyval, cosine, sine, w_gate, w_up), cotangent, w_output, held = early

    def ahead(index):
        return (held[index] - 0.5 * step * starts[index]).astype(LOW)

    small = jnp.concatenate(
        [ahead(0), ahead(1).reshape(-1, 2 * key_cols), ahead(2).T], axis=1
    )
    part_gateup = row_major(ahead(3))
    part_down = ahead(4)
    x_other = far(pick(x_got, other_source))
    c_got = deal_in(cotangent)
    x_other, w_output = fence(x_other, w_output)
    groups = (
        (w_query, w_keyval_flat, w_output),
        (far_query, far_keyval),
    )
    far_output = far(w_output)
    x_own = rows_of(join(x_got, own_source, x_other, in_order))

    x_full = x_own.astype(FULL)
    norm_one_f, inv_one = row_norm(x_full, norm_gains[0])
    norm_own = norm_one_f.astype(LOW)
    norm_near = near(norm_own)
    dims = (slot_rows, slot_pieces, part_rows, slot_rows // 6, head_dim, heads)
    shape = jax.ShapeDtypeStruct

    def attend(last, weights, more):
        token_shape = (heads, slot_rows, LANES)
        outs = [
            shape((slot_rows, query_cols), LOW),
            shape((slot_rows, query_cols + key_cols), LOW),
            shape(token_shape, FULL),
        ] + [shape(token_shape, LOW)] * 5
        if last:
            outs += [shape((half_rows, width), LOW)] * 2
        arguments = (
            member_ref,
            norm_own,
            norm_near,
            weights[0],
            weights[1],
            cosine,
            sine,
            start.reshape(-1, 1),
            gain_q,
            gain_k,
        ) + more
        return pl.pallas_call(
            functools.partial(attend_body, last, dims),
            in_specs=[SMEM] + [VMEM] * (len(arguments) - 1),
            out_specs=[VMEM] * len(outs),
            out_shape=outs,
            scratch_shapes=[
                pltpu.VMEM((heads + 2, slot_rows, LANES), FULL),
                pltpu.VMEM((heads, slot_rows, LANES), FULL),
                pltpu.VMEM((heads, slot_rows, LANES), FULL),
            ],
            compiler_params=pltpu.CompilerParams(vmem_limit_bytes=VMEM_BYTES),
            cost_estimate=pl.CostEstimate(
                flops=12_000_000_000 if last else 1_000_000_000,
                bytes_accessed=12_000_000 if last else 1_000_000,
                transcendentals=0,
            ),
        )(*arguments)

    def attend_back(last, weights, kept, d_own, d_near, more):
        token_shape = (heads, slot_rows, LANES)
        mixed, raw, inverse, *tables = kept
        outs = [shape((slot_rows, query_cols + 2 * key_cols), LOW), shape((16, LANES), FULL)]
        if last:
            outs += [shape((half_rows, width), LOW)] * 2
        arguments = (
            member_ref,
            d_own,
            d_near,
            weights[2],
            mixed,
            inverse,
            raw,
            cosine,
            sine,
            start.reshape(1, -1),
            gain_q,
            gain_k,
            *tables,
        ) + more
        return pl.pallas_call(
            functools.partial(attend_back_body, last, dims),
            in_specs=[SMEM] + [VMEM] * (len(arguments) - 1),
            out_specs=[VMEM] * len(outs),
            out_shape=outs,
            scratch_shapes=[
                pltpu.VMEM((2 * heads, slot_rows, LANES), FULL),
                pltpu.VMEM(token_shape, LOW),
                pltpu.VMEM(token_shape, LOW),
                pltpu.VMEM(token_shape, FULL),
                pltpu.VMEM(token_shape, FULL),
                pltpu.VMEM(token_shape, FULL),
            ],
            compiler_params=pltpu.CompilerParams(vmem_limit_bytes=VMEM_BYTES),
            cost_estimate=pl.CostEstimate(
                flops=20_000_000_000, bytes_accessed=14_000_000, transcendentals=0
            ),
        )(*arguments)

    first_kept = attend(False, groups[0], ())
    stepped = fence(first_kept, c_got, small, part_gateup, part_down, far_output)
    first_kept, c_got, small, part_gateup, part_down, far_output = stepped
    groups = (groups[0], groups[1] + (far_output,))
    c_first, c_second = pick(c_got, other_source), pick(c_got, own_source)
    first_kept, c_first, c_second = fence(first_kept, c_first, c_second)
    c_own_far, c_other_far = far(c_first), far(c_second)
    ahead_gateup = lax.all_gather(part_gateup, "dp", axis=0, tiled=True)
    ahead_down = lax.all_gather(part_down, "dp", axis=0, tiled=False)
    ahead_small = lax.all_gather(small, "dp", axis=0, tiled=False)
    *second_kept, attn_own, attn_near = attend(
        True, groups[1], (groups[1][2], groups[0][2], first_kept[0])
    )
    attn_own, attn_near, c_own_far = fence(attn_own, attn_near, c_own_far)
    attn_got = near(attn_near)
    c_own = rows_of(join(c_got, own_source, c_own_far, in_order))
    attn_got, c_own = fence(attn_got, c_own)
    c_near = near(c_own)
    hidden_one = x_full + add(attn_own, attn_got)
    norm_two_f, inv_two = row_norm(hidden_one, norm_gains[1])
    two_own = norm_two_f.astype(LOW)
    two_own, c_other_far = fence(two_own, c_other_far)
    two_near = near(two_own)
    two_near, c_near = fence(two_near, c_near)
    two_far = far(two_own)
    c_far = rows_of(join(c_other_far, in_order, c_got, other_source))

    *kept, d_own, d_near, y_own, y_near = feed(
        0, (), two_own, two_near, c_own, c_near, w_gate, w_up, w_down
    )
    stepped = fence(two_far, d_own, d_near, y_near, ahead_gateup)
    two_far, d_own, d_near, y_near, ahead_gateup = stepped
    two_across = near(two_far)
    c_across = near(c_far)
    d_got = near(d_near)
    y_got = near(y_near)
    *kept, far_own, far_near, far_y_own, far_y_near = feed(
        1, kept, two_far, two_across, c_far, c_across, w_gate, w_up, w_down
    )
    far_got = near(far_near)
    pair_far = add(far_own, far_got).astype(LOW)
    pair_far, kept, far_y_near = fence(pair_far, kept, far_y_near)
    inner, d_both, two_all, c_all = kept
    pair_got = far(pair_far)
    far_y_got = near(far_y_near)
    places = list(range(len(bits_of(devices))))
    grad_both = dot(two_all, d_both, 0, 0).astype(LOW)
    gate = Halving(grad_both[:, :hidden], device, devices, places[1:] + places[:1])
    up = Halving(grad_both[:, hidden:], device, devices, places)
    grad_down = dot(c_all, inner, 0, 0).astype(LOW)
    down = Halving(grad_down, device, devices, places)
    y_pair = add(y_own, y_got) + hidden_one
    far_y_pair = add(far_y_own, far_y_got)
    y_leaving = jnp.concatenate([y_pair[quarter_rows:], far_y_pair[:quarter_rows]]).astype(LOW)
    stepped = fence(pair_got, y_leaving, down.kept, gate.kept, up.kept)
    pair_got, y_leaving, down.kept, gate.kept, up.kept = stepped
    y_arrived = far(y_leaving)

    d_norm_two = add(d_own, d_got) + pair_got.astype(FULL)
    d_hidden_part, gain_two = row_norm_back(d_norm_two, hidden_one, inv_two, norm_gains[1])
    d_hidden = c_own.astype(FULL) + d_hidden_part
    dh_own = d_hidden.astype(LOW)
    dh_near = near(dh_own)

    def over_rows(own, other, values):
        return dot(own, values[:half_rows], 0, 0) + dot(other, values[half_rows:], 0, 0)

    d_raw_far, gains_far = attend_back(False, groups[1], second_kept, dh_own, dh_near, ())
    stepped = fence(d_raw_far, down.got, gate.got, ahead_down, y_arrived)
    d_raw_far, down.got, gate.got, ahead_down, y_arrived = stepped
    gate.go()
    down.go()

    out_order = (place_from + (slot_count - slot) * slot_pieces) % pieces_dev

    def to_send(rows):
        return pick(rows.reshape(pieces_dev, part_rows, width), out_order)

    y_mine = y_pair[:quarter_rows] + y_arrived[quarter_rows:].astype(FULL)
    y_other = far_y_pair[quarter_rows:] + y_arrived[:quarter_rows].astype(FULL)
    out_rows = jnp.concatenate([y_mine, y_other], axis=0).astype(LOW)
    grad_output_got = far(over_rows(dh_own, dh_near, second_kept[0]).astype(LOW))
    grad_qkv_got = far(over_rows(norm_own, norm_near, d_raw_far).astype(LOW))
    grad_output_mine = over_rows(dh_own, dh_near, first_kept[0])
    d_raw_own, gains_own, d_one_own, d_one_near = attend_back(
        True,
        groups[0],
        first_kept,
        dh_own,
        dh_near,
        (groups[0][0], groups[0][1], groups[1][0], groups[1][1], d_raw_far),
    )
    stepped = fence(
        (d_raw_own, d_one_near, down.got, gate.got, up.got), out_rows, grad_output_got, ahead_small
    )
    (d_raw_own, d_one_near, down.got, gate.got, up.got), *stepped = stepped
    out_rows, grad_output_got, ahead_small = stepped

    d_one_got = near(d_one_near)
    down.go()
    gate.go()
    up.go()
    stepped = fence(d_one_got, down.kept, gate.kept, up.kept, d_raw_own, out_rows)
    d_one_got, down.kept, gate.kept, up.kept, d_raw_own, out_rows = stepped
    d_norm_one = add(d_one_own, d_one_got)
    d_input_part, gain_one = row_norm_back(d_norm_one, x_full, inv_one, norm_gains[0])
    dx_own = (d_hidden + d_input_part).astype(LOW)
    stepped = fence(dx_own, up.got, down.got, gate.got, out_rows)
    dx_own, up.got, down.got, gate.got, out_rows = stepped

    def grown(held, got):
        return jnp.concatenate([held, got], axis=0)

    def first_steps(own):
        held = own.astype(LOW)[None]
        for bit in reversed(bits_of(devices)[3:]):
            held = grown(held, swap(held, "dp", bit))
        return held

    dx_other = far(dx_own[quarter_rows:])
    up.go()
    own_down = down.own()
    owned_down = own_down.T
    held_down = first_steps(owned_down)
    down_more = swap(held_down, "dp", 4)
    own_gate = gate.own()
    grad_qkv_mine = over_rows(norm_own, norm_near, d_raw_own).astype(LOW)
    small_parts = (grad_qkv_mine, grad_qkv_got, grad_output_mine, grad_output_got)
    rest = small_halving(small_parts, device, devices, places)
    stepped = fence(up.got, rest.got, dx_own, dx_other, down_more, own_gate, out_rows)
    up.got, rest.got, dx_own, dx_other, down_more, own_gate, out_rows = stepped

    own_up = up.own()
    owned_gateup = jnp.stack([own_gate, own_up], axis=1)
    held_gateup = first_steps(row_major(owned_gateup.astype(LOW)))
    gateup_more = swap(held_gateup, "dp", 4)
    rest.go()
    held_down = grown(held_down, down_more)
    down_more = swap(held_down, "dp", 2)
    dx_sent = to_send(jnp.concatenate([dx_own[:quarter_rows], dx_other], axis=0))
    out_sent = to_send(out_rows)
    stepped = fence(rest.got, down_more, gateup_more, dx_sent, out_sent)
    rest.got, down_more, gateup_more, dx_sent, out_sent = stepped

    held_gateup = grown(held_gateup, gateup_more)
    gateup_more = swap(held_gateup, "dp", 2)
    held_down = grown(held_down, down_more)
    down_more = swap(held_down, "dp", 1)
    rest.go()
    rest.got, down_more, gateup_more, out_sent = fence(rest.got, down_more, gateup_more, out_sent)

    held_gateup = grown(held_gateup, gateup_more)
    half_shard = held_gateup.shape[1] // 2
    held_lower, held_upper = held_gateup[:, :half_shard], held_gateup[:, half_shard:]
    lower_more = swap(held_lower, "dp", 1)
    out_got = across_dp(out_sent)
    own_small = rest.own()
    held_small = first_steps(own_small)
    small_more = swap(held_small, "dp", 4)
    owned = (own_small, own_gate, own_up, own_down)
    own_square = sum([jnp.sum(part_grad * part_grad) for part_grad in owned])
    gains = jnp.sum((gains_far + gains_own).reshape(2, 8, LANES // head_dim, head_dim), axis=(1, 2))
    packed = jnp.concatenate(
        [gain_one, gain_two, gains.reshape(-1), jnp.broadcast_to(own_square, (LANES,))]
    ).reshape(-1, LANES)
    for bit in bits_of(ways):
        packed = packed + swap(packed, "mp", bit)
    stepped = fence(lower_more, out_got, small_more, own_small, held_upper, dx_sent, packed)
    lower_more, out_got, small_more, own_small, held_upper, dx_sent, packed = stepped

    for bit in bits_of(devices):
        packed = packed + swap(packed, "dp", bit)
    stepped = fence(held_upper, dx_sent, out_got, small_more, packed)
    held_upper, dx_sent, out_got, small_more, packed = stepped
    upper_more = swap(held_upper, "dp", 1)
    dx_got = across_dp(dx_sent)
    out_far = far(out_got)
    held_small = grown(held_small, small_more)
    small_more = swap(held_small, "dp", 2)
    upper_more, dx_got, out_far, small_more = fence(upper_more, dx_got, out_far, small_more)
    dx_far = far(dx_got)

    flat = packed.reshape(-1)
    norm_sum = flat[: 2 * width].reshape(2, width)
    head_sum = flat[2 * width : 2 * width + 2 * head_dim].reshape(2, head_dim)
    square_sum = flat[2 * width + 2 * head_dim]
    clip_value = jnp.sqrt(square_sum + jnp.sum(norm_sum * norm_sum) + jnp.sum(head_sum * head_sum))
    limit = math.sqrt(2 * D * H * HD + 2 * D * KV * HD + 3 * D * FF + 2 * D + 2 * HD)
    factor = jnp.minimum(1.0, limit / clip_value)

    held_small = grown(held_small, small_more)
    small_more = swap(held_small, "dp", 1)

    qkv_cols = query_cols + 2 * key_cols
    owned_parts = (
        own_small[:, :query_cols],
        own_small[:, query_cols:qkv_cols].reshape(-1, 2, key_cols),
        own_small[:, qkv_cols:].T,
        owned_gateup,
        owned_down,
    )
    moments = [0.5 * begin + factor * part_grad for begin, part_grad in zip(starts, owned_parts)]
    nexts = [held - step * moved for held, moved in zip(masters, moments)]
    moment_norms = 0.5 * start_norms + factor * norm_sum
    moment_heads = 0.5 * start_heads + factor * head_sum
    next_norms = norm_gains - step * moment_norms
    next_heads = head_gains - step * moment_heads

    pull = (step * factor).reshape(1)
    output = place_pieces((out_got, out_far, near(out_got), near(out_far)), target, member_ref)
    device_ref = device.reshape(1).astype(jnp.int32)
    all_gateup = place_shards(
        device_ref, devices, (held_lower, lower_more), (held_upper, upper_more)
    ).reshape(ahead_gateup.shape)
    done_gateup = (ahead_gateup.astype(FULL) - pull[0] * all_gateup.astype(FULL)).astype(LOW)
    done_down = finish_down(device_ref, pull, ahead_down, held_down, down_more)
    near_got = near(dx_got)
    stepped = fence(dx_far, small_more, near_got, output, done_gateup, done_down, moments, nexts)
    dx_far, small_more, near_got, output, done_gateup, done_down, moments, nexts = stepped
    input_grad = place_pieces((dx_got, dx_far, near_got, near(dx_far)), target, member_ref)
    done_query, done_keyval, done_output = finish_small(
        device_ref, pull, ahead_small, held_small, small_more, query_cols, qkv_cols
    )
    weights = (
        done_query,
        done_keyval.reshape(width, 2, key_cols),
        done_output,
        done_gateup,
        done_down,
    )
    return (
        output,
        input_grad,
        clip_value.reshape(1),
        *moments,
        moment_norms,
        moment_heads,
        *nexts,
        next_norms,
        next_heads,
        *weights,
    )


def solution(mesh):
    in_specs = (
        P("dp", None),
        P("dp", None),
        P("dp", None),
        P(),
        P(None, "mp"),
        P(None, None, "mp"),
        P("mp", None),
        P(None, None, "mp"),
        P("mp", None),
        P(),
        P(),
        P("dp", "mp"),
        P("dp", None, "mp"),
        P("mp", "dp"),
        P("dp", None, "mp"),
        P("mp", "dp"),
        P("dp", "mp"),
        P("dp", None, "mp"),
        P("mp", "dp"),
        P("dp", None, "mp"),
        P("mp", "dp"),
        P(),
        P(),
        P(),
    )
    out_specs = (
        P("dp", None),
        P("dp", None),
        P(),
        P("dp", "mp"),
        P("dp", None, "mp"),
        P("mp", "dp"),
        P("dp", None, "mp"),
        P("mp", "dp"),
        P(),
        P(),
        P("dp", "mp"),
        P("dp", None, "mp"),
        P("mp", "dp"),
        P("dp", None, "mp"),
        P("mp", "dp"),
        P(),
        P(),
        P(None, "mp"),
        P(None, None, "mp"),
        P("mp", None),
        P(None, None, "mp"),
        P("mp", None),
    )
    return jax.shard_map(local, mesh=mesh, in_specs=in_specs, out_specs=out_specs, check_vma=False)
```

```python
import functools
import math

import jax
import jax.numpy as jnp
from jax import lax
from jax.experimental import pallas as pl
from jax.experimental.layout import Layout, with_layout_constraint
from jax.experimental.pallas import tpu as pltpu
from jax.sharding import PartitionSpec as P

D = 1024
H = 16
KV = 8
HD = 64
FF = 4608


EPSILON = 1e-05
ROPE_BASE = 1000000.0
LOW = jnp.bfloat16
FULL = jnp.float32
LANES = 128


def dot(left, right, left_dim=1, right_dim=0):
    return lax.dot_general(
        left, right, (((left_dim,), (right_dim,)), ((), ())), preferred_element_type=FULL
    )


def swap(values, axis, bit):
    size = lax.axis_size(axis)
    return lax.ppermute(values, axis, [(place, place ^ bit) for place in range(size)])


def row_major(values):
    return with_layout_constraint(values, Layout(tuple(range(values.ndim))))


def far(values):
    return swap(values, "mp", 2)


def near(values):
    return swap(values, "mp", 1)


def bits_of(count):
    return [1 << place for place in range(count.bit_length() - 1)]


def coordinates(index, devices):
    return [(index >> place) & 1 for place in range(len(bits_of(devices)))]


def gather_masks(devices):
    places = list(reversed(range(len(bits_of(devices)))))
    return [1 << place for place in places]


RELATIVE = (0, 2, 1, 3)
VMEM = pl.BlockSpec(memory_space=pltpu.VMEM)
SMEM = pl.BlockSpec(memory_space=pltpu.SMEM)
VMEM_BYTES = 60 * 1024 * 1024


def group_sums(values, ones):
    high = values.astype(LOW)
    rest = (values - high.astype(FULL)).astype(LOW)
    return dot(high, ones) + dot(rest, ones)


def head_ones(head_dim):
    row = lax.broadcasted_iota(jnp.int32, (LANES, LANES), 0) // head_dim
    col = lax.broadcasted_iota(jnp.int32, (LANES, LANES), 1) // head_dim
    return (row == col).astype(FULL).astype(LOW)


def turn_halves(values, half):
    lane = lax.broadcasted_iota(jnp.int32, values.shape, 1)
    ahead = pltpu.roll(values, LANES - half, 1)
    behind = pltpu.roll(values, half, 1)
    return jnp.where(lane % (2 * half) < half, ahead, behind)


def attend_body(last, dims, *refs):
    rows, pieces, part, block, head_dim, heads = dims
    (member, n_own, n_near, w_q, w_kv, cos, sin, start, gain_q, gain_k) = refs[:10]
    refs = refs[10:]
    if last:
        (w_o, w_o_first, mixed_first) = refs[:3]
        refs = refs[3:]
    (mixed, raw, inverse, q_pair, k_lo, k_hi, v_lo, v_hi) = refs[:8]
    refs = refs[8:]
    if last:
        (sum_own, sum_near) = refs[:2]
        refs = refs[2:]
    (by_token, a_token, r_token) = refs
    quarter_rows = pieces * part
    piece = 4 * part
    ones = head_ones(head_dim)

    def place(k, p):
        quarter = member[0] ^ RELATIVE[k]
        return pl.multiple_of(p * piece + quarter * part, 8)

    for k in range(4):
        here = pl.ds(k * quarter_rows, quarter_rows)
        source = n_own if k < 2 else n_near
        n_rows = source[(k % 2) * quarter_rows : (k % 2 + 1) * quarter_rows, :]
        query = dot(n_rows, w_q[...])
        keyval = dot(n_rows, w_kv[...])
        raw[here, : heads * LANES] = query.astype(LOW)
        raw[here, heads * LANES :] = keyval[:, :LANES].astype(LOW)
        parts = [query[:, h * LANES : (h + 1) * LANES] for h in range(heads)]
        parts.append(keyval[:, :LANES])
        turned = []
        for index, values in enumerate(parts):
            gain = gain_k if index == heads else gain_q
            mean = group_sums(values * values, ones) * (1.0 / head_dim)
            normed = values * lax.rsqrt(mean + EPSILON) * gain[...]
            turned.append(
                normed * cos[here, :] + turn_halves(normed, head_dim // 2) * sin[here, :]
            )
        turned.append(keyval[:, LANES:])
        for p in range(pieces):
            there = pl.ds(place(k, p), part)
            for index, values in enumerate(turned):
                by_token[index, there, :] = values[p * part : (p + 1) * part, :]

    scale = head_dim ** (-0.5)

    def prepare(i, carry):
        there = pl.ds(pl.multiple_of(i * block, block), block)
        low = lax.broadcasted_iota(jnp.int32, (block, LANES), 1) < head_dim
        for h in range(heads):
            q_pair[h, there, :] = (by_token[h, there, :] * scale).astype(LOW)
        key = by_token[heads, there, :]
        value = by_token[heads + 1, there, :]
        key_low = jnp.where(low, key, 0.0)
        key_high = jnp.where(low, 0.0, key)
        value_low = jnp.where(low, value, 1.0)
        value_high = jnp.where(low, 1.0, value)
        k_lo[0, there, :] = key_low.astype(LOW)
        k_hi[0, there, :] = pltpu.roll(key_low, head_dim, 1).astype(LOW)
        k_lo[1, there, :] = pltpu.roll(key_high, head_dim, 1).astype(LOW)
        k_hi[1, there, :] = key_high.astype(LOW)
        v_lo[0, there, :] = value_low.astype(LOW)
        v_hi[0, there, :] = pltpu.roll(value_low, head_dim, 1).astype(LOW)
        v_lo[1, there, :] = pltpu.roll(value_high, head_dim, 1).astype(LOW)
        v_hi[1, there, :] = value_high.astype(LOW)
        return carry

    lax.fori_loop(0, rows // block, prepare, 0)

    def one_head(h, carry):
        for i in range(rows // block):
            here = pl.ds(i * block, block)
            end = (i + 1) * block
            query = q_pair[h, here, :]
            key_row = lax.broadcasted_iota(jnp.int32, (block, end), 1)
            query_row = lax.broadcasted_iota(jnp.int32, (block, end), 0) + i * block
            seen = (key_row <= query_row) & (key_row >= start[here, :])
            mixed_parts = []
            for keys, values in ((k_lo, v_lo), (k_hi, v_hi)):
                scores = dot(query, keys[h, :end, :], 1, 1)
                weight = jnp.where(seen, jnp.exp(scores), 0.0).astype(LOW)
                mixed_parts.append(dot(weight, values[h, :end, :]))
            even, odd = mixed_parts
            low = lax.broadcasted_iota(jnp.int32, (block, LANES), 1) < head_dim
            divided = 1.0 / pltpu.roll(jnp.where(low, odd, even), head_dim, 1)
            a_token[h, here, :] = jnp.where(low, even, odd) * divided
            r_token[h, here, :] = divided
        return carry

    lax.fori_loop(0, heads, one_head, 0)

    for k in range(4):
        here = pl.ds(k * quarter_rows, quarter_rows)
        for h in range(heads):
            pieces_a = [a_token[h, pl.ds(place(k, p), part), :] for p in range(pieces)]
            pieces_r = [r_token[h, pl.ds(place(k, p), part), :] for p in range(pieces)]
            mixed[here, h * LANES : (h + 1) * LANES] = jnp.concatenate(pieces_a, axis=0).astype(LOW)
            inverse[h, here, :] = jnp.concatenate(pieces_r, axis=0)
        if last:
            total = dot(mixed[here, :], w_o[...]) + dot(mixed_first[here, :], w_o_first[...])
            target = sum_own if k < 2 else sum_near
            target[(k % 2) * quarter_rows : (k % 2 + 1) * quarter_rows, :] = total.astype(LOW)


def attend_back_body(last, dims, *refs):
    rows, pieces, part, block, head_dim, heads = dims
    (member, d_own, d_near, w_o, mixed, inverse, raw, cos, sin, start, gain_q, gain_k) = refs[:12]
    (q_pair, k_lo, k_hi, v_lo, v_hi) = refs[12:17]
    refs = refs[17:]
    if last:
        (w_q, w_kv, w_q_first, w_kv_first, d_raw_first) = refs[:5]
        refs = refs[5:]
    (d_raw, gains) = refs[:2]
    refs = refs[2:]
    if last:
        (sum_own, sum_near) = refs[:2]
        refs = refs[2:]
    (grad_token, grad_even, grad_odd, dq_token, dk_token, dv_token) = refs
    quarter_rows = pieces * part
    piece = 4 * part
    ones = head_ones(head_dim)
    scale = head_dim ** (-0.5)

    def place(k, p):
        quarter = member[0] ^ RELATIVE[k]
        return pl.multiple_of(p * piece + quarter * part, 8)

    for k in range(4):
        here = pl.ds(k * quarter_rows, quarter_rows)
        source = d_own if k < 2 else d_near
        d_rows = source[(k % 2) * quarter_rows : (k % 2 + 1) * quarter_rows, :]
        d_mixed = dot(d_rows, w_o[...], 1, 1)
        lane = lax.broadcasted_iota(jnp.int32, (quarter_rows, LANES), 1)
        low = lane < head_dim
        for h in range(heads):
            cols = slice(h * LANES, (h + 1) * LANES)
            grad = d_mixed[:, cols] * inverse[h, here, :]
            delta = group_sums(grad * mixed[here, cols].astype(FULL), ones)
            other = -pltpu.roll(delta, head_dim, 1)
            high = other.astype(LOW).astype(FULL)
            extra = jnp.where(lane % head_dim == 0, high, 0.0)
            extra = jnp.where(lane % head_dim == 1, other - high, extra)
            even = jnp.where(low, grad, extra)
            odd = jnp.where(low, extra, grad)
            for p in range(pieces):
                there = pl.ds(place(k, p), part)
                grad_token[2 * h, there, :] = even[p * part : (p + 1) * part, :]
                grad_token[2 * h + 1, there, :] = odd[p * part : (p + 1) * part, :]

    def prepare(i, carry):
        there = pl.ds(pl.multiple_of(i * block, block), block)
        for h in range(heads):
            grad_even[h, there, :] = grad_token[2 * h, there, :].astype(LOW)
            grad_odd[h, there, :] = grad_token[2 * h + 1, there, :].astype(LOW)
            dq_token[h, there, :] = jnp.zeros((block, LANES), FULL)
        return carry

    lax.fori_loop(0, rows // block, prepare, 0)

    def one_head(h, carry):
        for i in range(rows // block):
            first = i * block
            count = rows - first
            here = pl.ds(first, block)
            after = pl.ds(first, count)
            query = q_pair[h, after, :]
            key_row = lax.broadcasted_iota(jnp.int32, (block, count), 0)
            query_row = lax.broadcasted_iota(jnp.int32, (block, count), 1)
            seen = (key_row <= query_row) & (key_row + first >= start[:, after])
            d_keys = []
            d_values = []
            d_query = None
            for keys, values, grads in ((k_lo, v_lo, grad_even), (k_hi, v_hi, grad_odd)):
                key = keys[h, here, :]
                grad = grads[h, after, :]
                weight = jnp.where(seen, jnp.exp(dot(key, query, 1, 1)), 0.0)
                d_scores = (weight * dot(values[h, here, :], grad, 1, 1)).astype(LOW)
                d_values.append(dot(weight.astype(LOW), grad))
                d_keys.append(dot(d_scores, query))
                moved = dot(d_scores, key, 0, 0)
                d_query = moved if d_query is None else d_query + moved
            dq_token[h, after, :] += d_query
            low = lax.broadcasted_iota(jnp.int32, (block, LANES), 1) < head_dim
            for (even, odd), kept in ((d_keys, dk_token), (d_values, dv_token)):
                kept[h, here, :] = even + pltpu.roll(odd, head_dim, 1)
        return carry

    lax.fori_loop(0, heads, one_head, 0)

    gain_sums = [jnp.zeros((8, LANES), FULL), jnp.zeros((8, LANES), FULL)]
    for k in range(4):
        here = pl.ds(k * quarter_rows, quarter_rows)
        low = lax.broadcasted_iota(jnp.int32, (quarter_rows, LANES), 1) < head_dim

        def rows_of(token, h):
            return jnp.concatenate(
                [token[h, pl.ds(place(k, p), part), :] for p in range(pieces)], axis=0
            )

        def pair_of(token):
            return jnp.where(
                low, rows_of(token, 0), pltpu.roll(rows_of(token, 1), head_dim, 1)
            )

        turned = [rows_of(dq_token, h) * scale for h in range(heads)] + [pair_of(dk_token)]
        for index, values in enumerate(turned):
            is_key = index == heads
            gain = gain_k if is_key else gain_q
            cols = slice(index * LANES, (index + 1) * LANES)
            held = raw[here, cols].astype(FULL)
            root = lax.rsqrt(group_sums(held * held, ones) * (1.0 / head_dim) + EPSILON)
            normed = held * root
            back = values * cos[here, :] - turn_halves(values, head_dim // 2) * sin[here, :]
            scaled = back * gain[...]
            mean = group_sums(scaled * normed, ones) * (1.0 / head_dim)
            d_raw[here, cols] = (root * (scaled - normed * mean)).astype(LOW)
            products = (back * normed).reshape(quarter_rows // 8, 8, LANES)
            gain_sums[int(is_key)] = gain_sums[int(is_key)] + jnp.sum(products, axis=0)
        d_raw[here, (heads + 1) * LANES :] = pair_of(dv_token).astype(LOW)
        if last:
            wide = heads * LANES
            total = dot(d_raw[here, :wide], w_q[...], 1, 1)
            total = total + dot(d_raw[here, wide:], w_kv[...], 1, 1)
            total = total + dot(d_raw_first[here, :wide], w_q_first[...], 1, 1)
            total = total + dot(d_raw_first[here, wide:], w_kv_first[...], 1, 1)
            target = sum_own if k < 2 else sum_near
            target[(k % 2) * quarter_rows : (k % 2 + 1) * quarter_rows, :] = total.astype(LOW)
    gains[:8, :] = gain_sums[0]
    gains[8:, :] = gain_sums[1]


def feed_body(n_own, n_near, c_own, c_near, w_gate, w_up, w_down, *refs):
    (inner, d_both, n_all, c_all, d_own, d_near, y_own, y_near) = refs[-8:]
    hidden = w_gate.shape[1]
    mine = pl.program_id(0) < pl.num_programs(0) // 2
    n_rows = jnp.where(mine, n_own[...], n_near[...])
    c_rows = jnp.where(mine, c_own[...], c_near[...])
    n_all[...] = n_rows
    c_all[...] = c_rows
    gate = dot(n_rows, w_gate[...])
    up_part = dot(n_rows, w_up[...])
    d_inner = dot(c_rows, w_down[...], 1, 1)
    sigma = 1.0 / (1.0 + jnp.exp(-gate))
    held = gate * sigma
    inner[...] = (held * up_part).astype(LOW)
    d_both[:, :hidden] = (d_inner * up_part * sigma * (1.0 + gate * (1.0 - sigma))).astype(LOW)
    d_both[:, hidden:] = (d_inner * held).astype(LOW)
    total = dot(d_both[:, :hidden], w_gate[...], 1, 1)
    total = total + dot(d_both[:, hidden:], w_up[...], 1, 1)
    product = dot(inner[...], w_down[...])

    @pl.when(mine)
    def _():
        d_own[...] = total.astype(LOW)
        y_own[...] = product.astype(LOW)

    @pl.when(jnp.logical_not(mine))
    def _():
        d_near[...] = total.astype(LOW)
        y_near[...] = product.astype(LOW)


def feed(half, kept, n_own, n_near, c_own, c_near, w_gate, w_up, w_down):
    rows, width = n_own.shape
    hidden = w_gate.shape[1]
    block = rows // 2
    steps = 4
    first = pl.BlockSpec((block, width), lambda i: (jnp.minimum(i, 1), 0))
    second = pl.BlockSpec((block, width), lambda i: (jnp.maximum(i - 2, 0), 0))
    whole = lambda values: pl.BlockSpec(values.shape, lambda i: (0, 0))
    part = lambda cols: pl.BlockSpec((block, cols), lambda i: (i + steps * half, 0))
    in_specs = [first, second, first, second] + [whole(v) for v in (w_gate, w_up, w_down)]
    outs = [
        jax.ShapeDtypeStruct((4 * rows, cols), LOW) for cols in (hidden, 2 * hidden, width, width)
    ]
    outs += [jax.ShapeDtypeStruct((rows, width), LOW)] * 4
    out_specs = [part(hidden), part(2 * hidden)] + [part(width)] * 2
    out_specs += [first, second, first, second]
    aliases = {}
    if half:
        in_specs += [pl.BlockSpec(memory_space=pl.ANY)] * 4
        aliases = {7 + index: index for index in range(4)}
    return pl.pallas_call(
        feed_body,
        grid=(steps,),
        in_specs=in_specs,
        out_specs=out_specs,
        out_shape=outs,
        input_output_aliases=aliases,
        compiler_params=pltpu.CompilerParams(
            vmem_limit_bytes=VMEM_BYTES, dimension_semantics=("arbitrary",)
        ),
        cost_estimate=pl.CostEstimate(
            flops=1_000_000_000, bytes_accessed=1_000_000, transcendentals=0
        ),
    )(n_own, n_near, c_own, c_near, w_gate, w_up, w_down, *(kept if half else ()))


def each(count, act):
    if count <= 8:
        for index in range(count):
            act(index)
    else:
        lax.fori_loop(0, count, lambda index, carry: (act(index), carry)[1], 0)


def fetch(copies):
    for count, copy_of in copies:
        each(count, lambda index: copy_of(index).start())
    for count, copy_of in copies:
        each(count, lambda index: copy_of(index).wait())


HELD = pl.BlockSpec(memory_space=pl.ANY)


def pick_body(order, source, target, arrived):
    def copy_of(index):
        return pltpu.make_async_copy(
            source.at[order[index]], target.at[index], arrived.at[index]
        )

    fetch([(order.shape[0], copy_of)])


def pick(values, order):
    count = order.shape[0]
    return pl.pallas_call(
        pick_body,
        in_specs=[SMEM, HELD],
        out_specs=VMEM,
        out_shape=jax.ShapeDtypeStruct((count,) + values.shape[1:], values.dtype),
        scratch_shapes=[pltpu.SemaphoreType.DMA((count,))],
        compiler_params=pltpu.CompilerParams(vmem_limit_bytes=VMEM_BYTES),
    )(order, values)


def across_dp(values):
    return lax.all_to_all(values, "dp", split_axis=0, concat_axis=0, tiled=True)


def join_body(first_order, second_order, first, second, target, arrived):
    count = first_order.shape[0]

    def first_copy(index):
        return pltpu.make_async_copy(
            first.at[first_order[index]], target.at[index], arrived.at[index]
        )

    def second_copy(index):
        return pltpu.make_async_copy(
            second.at[second_order[index]], target.at[count + index], arrived.at[count + index]
        )

    fetch([(count, first_copy), (count, second_copy)])


def join(first, first_order, second, second_order):
    count = first_order.shape[0]
    return pl.pallas_call(
        join_body,
        in_specs=[SMEM, SMEM, HELD, HELD],
        out_specs=VMEM,
        out_shape=jax.ShapeDtypeStruct((2 * count,) + first.shape[1:], first.dtype),
        scratch_shapes=[pltpu.SemaphoreType.DMA((2 * count,))],
        compiler_params=pltpu.CompilerParams(vmem_limit_bytes=VMEM_BYTES),
    )(first_order, second_order, first, second)


def place_body(order, member, *refs):
    sources = refs[:4]
    target, arrived = refs[4:]
    copies = []
    for k, source in enumerate(sources):

        def copy_of(index, k=k, source=source):
            return pltpu.make_async_copy(
                source.at[order[index]],
                target.at[index, member[0] ^ RELATIVE[k]],
                arrived.at[k, index],
            )

        copies.append((order.shape[0], copy_of))
    fetch(copies)


def place_pieces(parts, order, member):
    count, part_rows, width = parts[0].shape
    pieces = pl.pallas_call(
        place_body,
        in_specs=[SMEM, SMEM] + [HELD] * 4,
        out_specs=VMEM,
        out_shape=jax.ShapeDtypeStruct((count, 4, part_rows, width), parts[0].dtype),
        scratch_shapes=[pltpu.SemaphoreType.DMA((4, count))],
        compiler_params=pltpu.CompilerParams(vmem_limit_bytes=VMEM_BYTES),
    )(order, member, *parts)
    return pieces.reshape(count * 4 * part_rows, width)


def finish_down_body(device, pull, ahead, held, more, weight, gradient, arrived):
    apart = places_apart(ahead.shape[0])
    copies = placing(apart, device, held, more, gradient, arrived)
    fetch(copies)
    cols = ahead.shape[2]
    for index in range(ahead.shape[0]):
        value = ahead[index].astype(FULL) - pull[0] * gradient[index].astype(FULL)
        weight[:, index * cols : (index + 1) * cols] = value.astype(LOW)


def finish_small_body(device, pull, ahead, held, more, query, keyval, output, gradient, arrived):
    apart = places_apart(ahead.shape[0])
    fetch(placing(apart, device, held, more, gradient, arrived))
    rows = ahead.shape[1]
    first = query.shape[1]
    second = first + keyval.shape[1]
    for index in range(ahead.shape[0]):
        value = ahead[index].astype(FULL) - pull[0] * gradient[index].astype(FULL)
        here = slice(index * rows, (index + 1) * rows)
        query[here, :] = value[:, :first].astype(LOW)
        keyval[here, :] = value[:, first:second].astype(LOW)
        output[:, here] = value[:, second:].T.astype(LOW)


def places_apart(count):
    apart = [0]
    for mask in gather_masks(count):
        apart = apart + [other ^ mask for other in apart]
    return apart


def placing(apart, device, held, more, target, arrived):
    half = len(apart) // 2
    copies = []
    for index, distance in enumerate(apart):
        source = held.at[index] if index < half else more.at[index - half]

        def copy_of(_, index=index, distance=distance, source=source):
            return pltpu.make_async_copy(
                source, target.at[device[0] ^ distance], arrived.at[index]
            )

        copies.append((1, copy_of))
    return copies


def place_shards_body(device, *refs):
    *sources, target, arrived = refs
    apart = places_apart(target.shape[0])
    half = len(apart) // 2
    rows = sources[0].shape[1]
    copies = []
    for chunk in range(len(sources) // 2):
        held, more = sources[2 * chunk : 2 * chunk + 2]
        for index, distance in enumerate(apart):
            source = held.at[index] if index < half else more.at[index - half]

            def copy_of(_, index=index, distance=distance, source=source, chunk=chunk):
                there = target.at[device[0] ^ distance, pl.ds(chunk * rows, rows)]
                return pltpu.make_async_copy(source, there, arrived.at[chunk, index])

            copies.append((1, copy_of))
    fetch(copies)


def kernel_params():
    return pltpu.CompilerParams(vmem_limit_bytes=VMEM_BYTES)


def place_shards(device, devices, *chunks):
    shape = (devices, len(chunks) * chunks[0][0].shape[1]) + chunks[0][0].shape[2:]
    sources = [part for chunk in chunks for part in chunk]
    return pl.pallas_call(
        place_shards_body,
        in_specs=[SMEM] + [HELD] * len(sources),
        out_specs=VMEM,
        out_shape=jax.ShapeDtypeStruct(shape, LOW),
        scratch_shapes=[pltpu.SemaphoreType.DMA((len(chunks), devices))],
        compiler_params=kernel_params(),
    )(device, *sources)


def finish_down(device, pull, ahead, held, more):
    count, rows, cols = ahead.shape
    if cols % LANES:
        gradient = place_shards(device, count, (held, more))
        value = ahead.astype(FULL) - pull * gradient.astype(FULL)
        return value.astype(LOW).transpose(1, 0, 2).reshape(rows, count * cols)
    return pl.pallas_call(
        finish_down_body,
        in_specs=[SMEM, SMEM, VMEM, HELD, HELD],
        out_specs=VMEM,
        out_shape=jax.ShapeDtypeStruct((rows, count * cols), LOW),
        scratch_shapes=[pltpu.VMEM(ahead.shape, LOW), pltpu.SemaphoreType.DMA((count,))],
        compiler_params=kernel_params(),
    )(device, pull, ahead, held, more)


def finish_small(device, pull, ahead, held, more, first, second):
    count, rows, cols = ahead.shape
    if rows % LANES:
        gradient = place_shards(device, count, (held, more))
        value = (ahead.astype(FULL) - pull * gradient.astype(FULL)).astype(LOW)
        value = value.reshape(count * rows, cols)
        return value[:, :first], value[:, first:second], value[:, second:].T
    shapes = [
        (count * rows, first),
        (count * rows, second - first),
        (cols - second, count * rows),
    ]
    return pl.pallas_call(
        finish_small_body,
        in_specs=[SMEM, SMEM, VMEM, HELD, HELD],
        out_specs=[VMEM] * 3,
        out_shape=[jax.ShapeDtypeStruct(shape, LOW) for shape in shapes],
        scratch_shapes=[pltpu.VMEM(ahead.shape, LOW), pltpu.SemaphoreType.DMA((count,))],
        compiler_params=kernel_params(),
    )(device, pull, ahead, held, more)


def fence(*values):
    return lax.optimization_barrier(values)


def add(first, second):
    return first.astype(FULL) + second.astype(FULL)


def halve_body(pairs, bit, kept, got, leaving, staying):
    for index, (base, stride) in enumerate(pairs):
        there = base + bit[0] * stride
        total = kept[there].astype(FULL) + got[there].astype(FULL)
        staying[index] = total
        there = base + (1 - bit[0]) * stride
        total = kept[there].astype(FULL) + got[there].astype(FULL)
        leaving[index] = total.astype(LOW)


class Halving:
    def __init__(self, device, devices, order):
        self.device = device
        self.devices = devices
        self.order = list(order)
        self.left = list(range(len(self.order)))
        self.stands = {tuple(coordinates(index, devices)): index for index in range(devices)}

    def start(self, product):
        rows = product.shape[0] // self.devices
        place, bit, pairs = self.next()
        shape = (self.devices // 2, rows) + product.shape[1:]
        if all(pair == (2 * index, 1) for index, pair in enumerate(pairs)):
            split = product.reshape((-1, 2, rows) + product.shape[1:])
            leaving, self.kept = [
                lax.dynamic_index_in_dim(split, side, 1, keepdims=False) for side in (1 - bit, bit)
            ]
        else:
            runs = []
            for base, stride in pairs:
                if runs and runs[-1][0] + runs[-1][2] == base and runs[-1][1] == stride:
                    runs[-1][2] += 1
                else:
                    runs.append([base, stride, 1])
            leaving, self.kept = [
                jnp.concatenate(
                    [
                        lax.dynamic_slice_in_dim(product, (base + side * stride) * rows, length * rows)
                        for base, stride, length in runs
                    ]
                ).reshape(shape)
                for side in (1 - bit, bit)
            ]
        self.got = swap(leaving.astype(LOW), "dp", 1 << place)
        return self

    def next(self):
        place = self.order.pop(0)
        at = self.left.index(place)
        self.left.remove(place)
        pairs, stands = [], {}
        for bits in sorted(self.stands):
            if not bits[at]:
                first = self.stands[bits]
                second = self.stands[bits[:at] + (1,) + bits[at + 1 :]]
                stands[bits[:at] + bits[at + 1 :]] = len(pairs)
                pairs.append((first, second - first))
        order = sorted(range(len(pairs)), key=lambda index: pairs[index][0])
        pairs = [pairs[index] for index in order]
        self.stands = {bits: order.index(index) for bits, index in stands.items()}
        return place, coordinates(self.device, self.devices)[place], pairs

    def go(self):
        place, bit, pairs = self.next()
        shape = (len(pairs),) + self.kept.shape[1:]
        leaving, self.kept = pl.pallas_call(
            functools.partial(halve_body, pairs),
            in_specs=[SMEM, VMEM, VMEM],
            out_specs=[VMEM, VMEM],
            out_shape=[jax.ShapeDtypeStruct(shape, LOW), jax.ShapeDtypeStruct(shape, FULL)],
            compiler_params=kernel_params(),
        )(bit.reshape(1).astype(jnp.int32), self.kept, self.got)
        self.got = swap(leaving, "dp", 1 << place)

    def own(self):
        while self.order:
            self.go()
        return add(self.kept, self.got)[0]


def small_body(pairs, size, bit, *refs):
    (first, first_got, second, second_got, leaving, staying) = refs
    wide = first.shape[1]
    for index, (base, stride) in enumerate(pairs):
        for target, side in ((leaving, 1 - bit[0]), (staying, bit[0])):
            rows = pl.ds(pl.multiple_of((base + side * stride) * size, size), size)
            total = first[rows, :].astype(FULL) + first_got[rows, :].astype(FULL)
            target[index, :, :wide] = total.astype(target.dtype)
            total = second[rows, :].astype(FULL) + second_got[rows, :].astype(FULL)
            target[index, :, wide:] = total.astype(target.dtype)


def small_halving(parts, device, devices, order):
    self = Halving(device, devices, order)
    place, bit, pairs = self.next()
    size = parts[0].shape[0] // devices
    shape = (devices // 2, size, parts[0].shape[1] + parts[2].shape[1])
    leaving, self.kept = pl.pallas_call(
        functools.partial(small_body, pairs, size),
        in_specs=[SMEM] + [VMEM] * 4,
        out_specs=[VMEM, VMEM],
        out_shape=[jax.ShapeDtypeStruct(shape, LOW), jax.ShapeDtypeStruct(shape, FULL)],
        compiler_params=kernel_params(),
    )(bit.reshape(1).astype(jnp.int32), *parts)
    self.got = swap(leaving, "dp", 1 << place)
    return self


def row_norm(values, gain_row):
    inverse = lax.rsqrt(jnp.mean(values * values, axis=-1, keepdims=True) + EPSILON)
    return (values * inverse * gain_row, inverse)


def row_norm_back(gradient, values, inverse, gain_row):
    scaled = gradient * gain_row
    d_values = inverse * scaled - values * (inverse * inverse * inverse) * jnp.mean(
        scaled * values, axis=-1, keepdims=True
    )
    d_gain = jnp.sum(gradient * values * inverse, axis=0)
    return (d_values, d_gain)


def local(
    tokens,
    cotangent,
    seq_lengths,
    deal,
    w_query,
    w_keyval,
    w_output,
    w_gateup,
    w_down,
    norm_gains,
    head_gains,
    master_query,
    master_keyval,
    master_output,
    master_gateup,
    master_down,
    start_query,
    start_keyval,
    start_output,
    start_gateup,
    start_down,
    start_norms,
    start_heads,
    step_size,
):
    devices = lax.axis_size("dp")
    ways = lax.axis_size("mp")
    device = lax.axis_index("dp")
    member = lax.axis_index("mp")
    row_count, width = tokens.shape
    total_pieces = deal.shape[0]
    pieces_dev = total_pieces // devices
    piece_rows = row_count // pieces_dev
    part_rows = piece_rows // ways
    slot_count = seq_lengths.shape[0]
    slot_rows = row_count // slot_count
    slot_pieces = pieces_dev // slot_count
    quarter_rows = slot_pieces * part_rows
    half_rows = 2 * quarter_rows
    head_dim = head_gains.shape[1]
    query_cols = w_query.shape[1]
    key_cols = w_keyval.shape[2]
    heads = query_cols // LANES
    hidden = w_down.shape[0]
    step = step_size[0]
    slot = member // 2
    member_ref = member.reshape(1).astype(jnp.int32)

    placed = jnp.arange(pieces_dev, dtype=jnp.int32)
    my_places = lax.dynamic_slice_in_dim(deal, device * pieces_dev, pieces_dev)
    target = my_places // pieces_dev
    piece_to = jnp.sum((target[:, None] == placed[None, :]) * placed[:, None], axis=0)
    whole = jnp.arange(total_pieces, dtype=jnp.int32)
    held_here = deal[:, None] == (device * pieces_dev + placed)[None, :]
    source = jnp.sum(held_here * (whole // pieces_dev)[:, None], axis=0)
    place_from = jnp.sum((source[:, None] == placed[None, :]) * placed[:, None], axis=0)
    slot_source = source.reshape(slot_count, slot_pieces)
    own_source = lax.dynamic_index_in_dim(slot_source, slot, 0, keepdims=False)
    other_source = lax.dynamic_index_in_dim(slot_source, 1 - slot, 0, keepdims=False)
    in_order = jnp.arange(slot_pieces, dtype=jnp.int32)

    def deal_in(values):
        quarters = values.reshape(pieces_dev * ways, part_rows, width)
        return across_dp(pick(quarters, piece_to * ways + member))

    def rows_of(pieces):
        return pieces.reshape(-1, width)

    x_got = deal_in(tokens)

    lengths = lax.dynamic_index_in_dim(seq_lengths, slot, 0, keepdims=False)
    ends = jnp.cumsum(lengths)

    def position_of(token):
        passed = (token[:, None] >= ends[None, :]).astype(jnp.int32)
        return token - jnp.sum(passed * lengths[None, :], axis=1)

    token_row = jnp.arange(slot_rows, dtype=jnp.int32)
    start = token_row - position_of(token_row)
    quarters = jnp.asarray(RELATIVE, jnp.int32) ^ member
    relative_token = (
        (in_order * piece_rows)[None, :, None]
        + (quarters * part_rows)[:, None, None]
        + jnp.arange(part_rows, dtype=jnp.int32)[None, None, :]
    ).reshape(-1)
    lane = jnp.arange(LANES, dtype=jnp.int32)
    half = head_dim // 2
    freqs = ROPE_BASE ** (-(lane % half).astype(FULL) * (2.0 / head_dim))
    angles = position_of(relative_token).astype(FULL)[:, None] * freqs[None, :]
    cosine = jnp.cos(angles)
    sine = jnp.sin(angles) * jnp.where(lane % head_dim < half, -1.0, 1.0)[None, :]
    gain_q = jnp.tile(head_gains[0:1], (1, LANES // head_dim))
    gain_k = jnp.tile(head_gains[1:2], (1, LANES // head_dim))

    w_keyval_flat = w_keyval.reshape(width, 2 * key_cols)
    far_query, far_keyval = far(w_query), far(w_keyval_flat)
    w_gate = w_gateup[:, 0]
    w_up = w_gateup[:, 1]

    masters = (master_query, master_keyval, master_output, master_gateup, master_down)
    starts = (start_query, start_keyval, start_output, start_gateup, start_down)
    early = fence(
        (x_got, far_query, far_keyval, cosine, sine, w_gate, w_up), cotangent, w_output, masters
    )
    (x_got, far_query, far_keyval, cosine, sine, w_gate, w_up), cotangent, w_output, held = early

    def ahead(index):
        return (held[index] - 0.5 * step * starts[index]).astype(LOW)

    small = jnp.concatenate(
        [ahead(0), ahead(1).reshape(-1, 2 * key_cols), ahead(2).T], axis=1
    )
    part_gateup = row_major(ahead(3))
    part_down = ahead(4)
    x_other = far(pick(x_got, other_source))
    c_got = deal_in(cotangent)
    x_other, w_output = fence(x_other, w_output)
    groups = (
        (w_query, w_keyval_flat, w_output),
        (far_query, far_keyval),
    )
    far_output = far(w_output)
    x_own = rows_of(join(x_got, own_source, x_other, in_order))

    x_full = x_own.astype(FULL)
    norm_one_f, inv_one = row_norm(x_full, norm_gains[0])
    norm_own = norm_one_f.astype(LOW)
    norm_near = near(norm_own)
    dims = (slot_rows, slot_pieces, part_rows, slot_rows // 4, head_dim, heads)
    back_dims = dims[:3] + (slot_rows // 6,) + dims[4:]
    shape = jax.ShapeDtypeStruct

    def attend(last, weights, more):
        token_shape = (heads, slot_rows, LANES)
        outs = [
            shape((slot_rows, query_cols), LOW),
            shape((slot_rows, query_cols + key_cols), LOW),
            shape(token_shape, FULL),
        ] + [shape(token_shape, LOW)] * 5
        if last:
            outs += [shape((half_rows, width), LOW)] * 2
        arguments = (
            member_ref,
            norm_own,
            norm_near,
            weights[0],
            weights[1],
            cosine,
            sine,
            start.reshape(-1, 1),
            gain_q,
            gain_k,
        ) + more
        return pl.pallas_call(
            functools.partial(attend_body, last, dims),
            in_specs=[SMEM] + [VMEM] * (len(arguments) - 1),
            out_specs=[VMEM] * len(outs),
            out_shape=outs,
            scratch_shapes=[
                pltpu.VMEM((heads + 2, slot_rows, LANES), FULL),
                pltpu.VMEM((heads, slot_rows, LANES), FULL),
                pltpu.VMEM((heads, slot_rows, LANES), FULL),
            ],
            compiler_params=pltpu.CompilerParams(vmem_limit_bytes=VMEM_BYTES),
            cost_estimate=pl.CostEstimate(
                flops=1_000_000_000,
                bytes_accessed=1_000_000,
                transcendentals=0,
            ),
        )(*arguments)

    def attend_back(last, weights, kept, d_own, d_near, more):
        token_shape = (heads, slot_rows, LANES)
        mixed, raw, inverse, *tables = kept
        outs = [shape((slot_rows, query_cols + 2 * key_cols), LOW), shape((16, LANES), FULL)]
        if last:
            outs += [shape((half_rows, width), LOW)] * 2
        arguments = (
            member_ref,
            d_own,
            d_near,
            weights[2],
            mixed,
            inverse,
            raw,
            cosine,
            sine,
            start.reshape(1, -1),
            gain_q,
            gain_k,
            *tables,
        ) + more
        return pl.pallas_call(
            functools.partial(attend_back_body, last, back_dims),
            in_specs=[SMEM] + [VMEM] * (len(arguments) - 1),
            out_specs=[VMEM] * len(outs),
            out_shape=outs,
            scratch_shapes=[
                pltpu.VMEM((2 * heads, slot_rows, LANES), FULL),
                pltpu.VMEM(token_shape, LOW),
                pltpu.VMEM(token_shape, LOW),
                pltpu.VMEM(token_shape, FULL),
                pltpu.VMEM(token_shape, FULL),
                pltpu.VMEM(token_shape, FULL),
            ],
            compiler_params=pltpu.CompilerParams(vmem_limit_bytes=VMEM_BYTES),
            cost_estimate=pl.CostEstimate(
                flops=1_000_000_000, bytes_accessed=1_000_000, transcendentals=0
            ),
        )(*arguments)

    first_kept = attend(False, groups[0], ())
    stepped = fence(first_kept, c_got, small, part_gateup, part_down, far_output)
    first_kept, c_got, small, part_gateup, part_down, far_output = stepped
    groups = (groups[0], groups[1] + (far_output,))
    c_first, c_second = pick(c_got, other_source), pick(c_got, own_source)
    first_kept, c_first, c_second = fence(first_kept, c_first, c_second)
    c_own_far, c_other_far = far(c_first), far(c_second)
    ahead_gateup = lax.all_gather(part_gateup, "dp", axis=0, tiled=True)
    ahead_down = lax.all_gather(part_down, "dp", axis=0, tiled=False)
    ahead_small = lax.all_gather(small, "dp", axis=0, tiled=False)
    *second_kept, attn_own, attn_near = attend(
        True, groups[1], (groups[1][2], groups[0][2], first_kept[0])
    )
    attn_own, attn_near, c_own_far = fence(attn_own, attn_near, c_own_far)
    attn_got = near(attn_near)
    c_own = rows_of(join(c_got, own_source, c_own_far, in_order))
    attn_got, c_own = fence(attn_got, c_own)
    c_near = near(c_own)
    hidden_one = x_full + add(attn_own, attn_got)
    norm_two_f, inv_two = row_norm(hidden_one, norm_gains[1])
    two_own = norm_two_f.astype(LOW)
    two_own, c_other_far = fence(two_own, c_other_far)
    two_near = near(two_own)
    two_near, c_near = fence(two_near, c_near)
    two_far = far(two_own)
    c_far = rows_of(join(c_other_far, in_order, c_got, other_source))

    *kept, d_own, d_near, y_own, y_near = feed(
        0, (), two_own, two_near, c_own, c_near, w_gate, w_up, w_down
    )
    two_far, d_own, d_near, y_near = fence(two_far, d_own, d_near, y_near)
    two_across = near(two_far)
    c_across = near(c_far)
    d_got = near(d_near)
    y_got = near(y_near)
    *kept, far_own, far_near, far_y_own, far_y_near = feed(
        1, kept, two_far, two_across, c_far, c_across, w_gate, w_up, w_down
    )
    far_own, far_near, ahead_gateup = fence(far_own, far_near, ahead_gateup)
    far_got = near(far_near)
    pair_far = add(far_own, far_got).astype(LOW)
    pair_far, kept, far_y_near = fence(pair_far, kept, far_y_near)
    inner, d_both, two_all, c_all = kept
    pair_got = far(pair_far)
    far_y_got = near(far_y_near)
    x_first = list(range(len(bits_of(devices))))
    z_first = x_first[1:] + x_first[:1]
    *masks, mask_one, mask_two, mask_three = gather_masks(devices)
    grad_both = dot(two_all, d_both, 0, 0).astype(LOW)
    grad_down = dot(c_all, inner, 0, 0).astype(LOW)
    y_pair = add(y_own, y_got) + hidden_one
    far_y_pair = add(far_y_own, far_y_got)
    y_leaving = jnp.concatenate([y_pair[quarter_rows:], far_y_pair[:quarter_rows]]).astype(LOW)
    stepped = fence(pair_got, y_leaving, grad_both, grad_down)
    pair_got, y_leaving, grad_both, grad_down = stepped
    gate = Halving(device, devices, z_first).start(grad_both[:, :hidden])
    down = Halving(device, devices, x_first).start(grad_down)
    up = Halving(device, devices, x_first).start(grad_both[:, hidden:])
    y_arrived = far(y_leaving)

    d_norm_two = add(d_own, d_got) + pair_got.astype(FULL)
    d_hidden_part, gain_two = row_norm_back(d_norm_two, hidden_one, inv_two, norm_gains[1])
    d_hidden = c_own.astype(FULL) + d_hidden_part
    dh_own = d_hidden.astype(LOW)
    dh_near = near(dh_own)

    def over_rows(own, other, values):
        return dot(own, values[:half_rows], 0, 0) + dot(other, values[half_rows:], 0, 0)

    d_raw_far, gains_far = attend_back(False, groups[1], second_kept, dh_own, dh_near, ())
    d_raw_far, y_arrived = fence(d_raw_far, y_arrived)

    out_order = (place_from + (slot_count - slot) * slot_pieces) % pieces_dev

    def to_send(rows):
        return pick(rows.reshape(pieces_dev, part_rows, width), out_order)

    y_mine = y_pair[:quarter_rows] + y_arrived[quarter_rows:].astype(FULL)
    y_other = far_y_pair[quarter_rows:] + y_arrived[:quarter_rows].astype(FULL)
    out_sent = to_send(jnp.concatenate([y_mine, y_other], axis=0).astype(LOW))
    out_sent, down.got, gate.got = fence(out_sent, down.got, gate.got)
    out_got = across_dp(out_sent)
    gate.go()
    down.go()
    stepped = fence(gate.kept, down.kept, d_raw_far, dh_own)
    gate.kept, down.kept, d_raw_far, dh_own = stepped
    grad_output_got = far(over_rows(dh_own, dh_near, second_kept[0]).astype(LOW))
    grad_qkv_got = far(over_rows(norm_own, norm_near, d_raw_far).astype(LOW))
    grad_output_mine = over_rows(dh_own, dh_near, first_kept[0]).astype(LOW)
    d_raw_own, gains_own, d_one_own, d_one_near = attend_back(
        True,
        groups[0],
        first_kept,
        dh_own,
        dh_near,
        (groups[0][0], groups[0][1], groups[1][0], groups[1][1], d_raw_far),
    )
    stepped = fence(
        (d_raw_own, d_one_near, down.got, gate.got, up.got, out_got),
        (grad_output_got, grad_qkv_got, grad_output_mine, ahead_small, ahead_down),
    )
    d_raw_own, d_one_near, down.got, gate.got, up.got, out_got = stepped[0]
    grad_output_got, grad_qkv_got, grad_output_mine, ahead_small, ahead_down = stepped[1]

    d_one_got = near(d_one_near)
    down.go()
    gate.go()
    up.go()
    stepped = fence(d_one_got, down.kept, gate.kept, up.kept, d_raw_own)
    d_one_got, down.kept, gate.kept, up.kept, d_raw_own = stepped
    d_norm_one = add(d_one_own, d_one_got)
    d_input_part, gain_one = row_norm_back(d_norm_one, x_full, inv_one, norm_gains[0])
    dx_own = (d_hidden + d_input_part).astype(LOW)
    dx_own, up.got, down.got, gate.got = fence(dx_own, up.got, down.got, gate.got)

    def grown(held, got):
        return jnp.concatenate([held, got], axis=0)

    def first_steps(own):
        held = own.astype(LOW)[None]
        for mask in masks:
            held = grown(held, swap(held, "dp", mask))
        return held

    dx_other = far(dx_own[quarter_rows:])
    up.go()
    up.kept, down.kept, gate.kept, d_raw_own = fence(up.kept, down.kept, gate.kept, d_raw_own)
    own_down = down.own()
    owned_down = own_down.T
    held_down = first_steps(owned_down)
    down_more = swap(held_down, "dp", mask_one)
    own_gate = gate.own()
    grad_qkv_mine = over_rows(norm_own, norm_near, d_raw_own).astype(LOW)
    small_parts = (grad_qkv_mine, grad_qkv_got, grad_output_mine, grad_output_got)
    rest = small_halving(small_parts, device, devices, x_first)
    stepped = fence(up.got, rest.got, dx_own, dx_other, down_more, own_gate, out_got)
    up.got, rest.got, dx_own, dx_other, down_more, own_gate, out_got = stepped

    own_up = up.own()
    owned_gateup = jnp.stack([own_gate, own_up], axis=1)
    low_gateup = row_major(owned_gateup.astype(LOW))
    half_shard = low_gateup.shape[0] // 2
    held_lower = first_steps(low_gateup[:half_shard])
    held_upper = first_steps(low_gateup[half_shard:])
    lower_more = swap(held_lower, "dp", mask_one)
    rest.go()
    held_down = grown(held_down, down_more)
    down_more = swap(held_down, "dp", mask_two)
    dx_sent = to_send(jnp.concatenate([dx_own[:quarter_rows], dx_other], axis=0))
    stepped = fence(rest.got, down_more, lower_more, held_upper, dx_sent)
    rest.got, down_more, lower_more, held_upper, dx_sent = stepped

    upper_more = swap(held_upper, "dp", mask_one)
    held_lower = grown(held_lower, lower_more)
    lower_more = swap(held_lower, "dp", mask_two)
    held_down = grown(held_down, down_more)
    down_more = swap(held_down, "dp", mask_three)
    rest.go()
    out_far = far(out_got)
    rest.got, lower_more, upper_more = fence(rest.got, lower_more, upper_more)

    held_lower = grown(held_lower, lower_more)
    lower_more = swap(held_lower, "dp", mask_three)
    held_upper = grown(held_upper, upper_more)
    upper_more = swap(held_upper, "dp", mask_two)
    dx_got = across_dp(dx_sent)
    own_small = rest.own()
    held_small = first_steps(own_small)
    small_more = swap(held_small, "dp", mask_one)
    owned = (own_small, own_gate, own_up, own_down)
    own_square = sum([jnp.sum(part_grad * part_grad) for part_grad in owned])
    gains = jnp.sum((gains_far + gains_own).reshape(2, 8, LANES // head_dim, head_dim), axis=(1, 2))
    packed = jnp.concatenate(
        [gain_one, gain_two, gains.reshape(-1), jnp.broadcast_to(own_square, (LANES,))]
    ).reshape(-1, LANES)
    for bit in bits_of(ways):
        packed = packed + swap(packed, "mp", bit)
    output = place_pieces((out_got, out_far, near(out_got), near(out_far)), target, member_ref)
    stepped = fence(
        (lower_more, upper_more, down_more, small_more), dx_got, packed, own_small, output
    )
    (lower_more, upper_more, down_more, small_more), dx_got, packed, own_small, output = stepped
    packed = packed + swap(packed, "dp", 1)
    stepped = fence(held_upper, held_small, dx_got, packed, upper_more, small_more)
    held_upper, held_small, dx_got, packed, upper_more, small_more = stepped
    held_upper = grown(held_upper, upper_more)
    upper_more = swap(held_upper, "dp", mask_three)
    dx_far = far(dx_got)
    for bit in bits_of(devices)[1:]:
        packed = packed + swap(packed, "dp", bit)
    packed, held_small, small_more = fence(packed, held_small, small_more)
    held_small = grown(held_small, small_more)
    small_more = swap(held_small, "dp", mask_two)

    flat = packed.reshape(-1)
    norm_sum = flat[: 2 * width].reshape(2, width)
    head_sum = flat[2 * width : 2 * width + 2 * head_dim].reshape(2, head_dim)
    square_sum = flat[2 * width + 2 * head_dim]
    clip_value = jnp.sqrt(square_sum + jnp.sum(norm_sum * norm_sum) + jnp.sum(head_sum * head_sum))
    limit = math.sqrt(2 * D * H * HD + 2 * D * KV * HD + 3 * D * FF + 2 * D + 2 * HD)
    factor = jnp.minimum(1.0, limit / clip_value)

    qkv_cols = query_cols + 2 * key_cols
    owned_parts = (
        own_small[:, :query_cols],
        own_small[:, query_cols:qkv_cols].reshape(-1, 2, key_cols),
        own_small[:, qkv_cols:].T,
        owned_gateup,
        owned_down,
    )
    moments = [0.5 * begin + factor * part_grad for begin, part_grad in zip(starts, owned_parts)]
    nexts = [held - step * moved for held, moved in zip(masters, moments)]
    moment_norms = 0.5 * start_norms + factor * norm_sum
    moment_heads = 0.5 * start_heads + factor * head_sum
    next_norms = norm_gains - step * moment_norms
    next_heads = head_gains - step * moment_heads

    pull = (step * factor).reshape(1)
    device_ref = device.reshape(1).astype(jnp.int32)
    done_down = finish_down(device_ref, pull, ahead_down, held_down, down_more)
    dx_far, done_down, small_more = fence(dx_far, done_down, small_more)
    held_small = grown(held_small, small_more)
    small_more = swap(held_small, "dp", mask_three)
    input_grad = place_pieces((dx_got, dx_far, near(dx_got), near(dx_far)), target, member_ref)
    upper_more, input_grad = fence(upper_more, input_grad)
    all_gateup = place_shards(
        device_ref, devices, (held_lower, lower_more), (held_upper, upper_more)
    ).reshape(ahead_gateup.shape)
    done_gateup = (ahead_gateup.astype(FULL) - pull[0] * all_gateup.astype(FULL)).astype(LOW)
    small_more, done_gateup = fence(small_more, done_gateup)
    done_query, done_keyval, done_output = finish_small(
        device_ref, pull, ahead_small, held_small, small_more, query_cols, qkv_cols
    )
    weights = (
        done_query,
        done_keyval.reshape(width, 2, key_cols),
        done_output,
        done_gateup,
        done_down,
    )
    return (
        output,
        input_grad,
        clip_value.reshape(1),
        *moments,
        moment_norms,
        moment_heads,
        *nexts,
        next_norms,
        next_heads,
        *weights,
    )


def solution(mesh):
    in_specs = (
        P("dp", None),
        P("dp", None),
        P("dp", None),
        P(),
        P(None, "mp"),
        P(None, None, "mp"),
        P("mp", None),
        P(None, None, "mp"),
        P("mp", None),
        P(),
        P(),
        P("dp", "mp"),
        P("dp", None, "mp"),
        P("mp", "dp"),
        P("dp", None, "mp"),
        P("mp", "dp"),
        P("dp", "mp"),
        P("dp", None, "mp"),
        P("mp", "dp"),
        P("dp", None, "mp"),
        P("mp", "dp"),
        P(),
        P(),
        P(),
    )
    out_specs = (
        P("dp", None),
        P("dp", None),
        P(),
        P("dp", "mp"),
        P("dp", None, "mp"),
        P("mp", "dp"),
        P("dp", None, "mp"),
        P("mp", "dp"),
        P(),
        P(),
        P("dp", "mp"),
        P("dp", None, "mp"),
        P("mp", "dp"),
        P("dp", None, "mp"),
        P("mp", "dp"),
        P(),
        P(),
        P(None, "mp"),
        P(None, None, "mp"),
        P("mp", None),
        P(None, None, "mp"),
        P("mp", None),
    )
    return jax.shard_map(local, mesh=mesh, in_specs=in_specs, out_specs=out_specs, check_vma=False)
```
